256 devices in a mesh: group: 4 (over y), dev: 64 (over z, x, core).
Axes of the slice: x: 4, y: 4, z: 8, core: 2. Of those that a mesh axis runs over, the one named last changes fastest.
Arguments:
- level_set: float32 [512, 65536], P(None, ('group', 'dev')), may hold values from -8 to 8
- speed: float32 [512, 65536], P(None, ('group', 'dev')), may hold values from 0.25 to 1
- peer_slabs: int32 [16384, 8], P(('group', 'dev')), may hold values from -1 to 1535, as said below
- region_slabs: int32 [512, 16], P(('group', 'dev')), may hold values from 0 to 511, as said below
- halo_source: int32 [6, 65536], P(None, ('group', 'dev')), may hold values from 0 to 2079, as said below
Outputs:
- offset: float32 [512, 65536], P(None, ('group', 'dev'))
The draws below stay inside these ranges and needn't reach their ends.
Inputs may be any that keep to these rules, and one draw needn't show every extreme that they name: `peer_slabs`: row (device, e) lists the local slab ids that the device sends to device e of its region, -1 in empty slots. Every device fills all 8 slots of at least one row, and receives 8 slabs from at least one device. `region_slabs`: local slab ids of the leaf faces that border the previous region (row 0) and the next region (row 1). `halo_source`: an entry of the halo table of the column's device; only slots that the sender fills are named.
All inputs are finite; a program needn't handle non-finite values.
Results may differ from the reference program's by a relative error of at most 0.0003.
Values sent between devices are 32-bit elements; how exact they have to be, the bound alone decides.
A program may use at most 64 MiB of HBM per device.

```python
import math
import jax
import jax.numpy as jnp
from jax import lax

LEAF_VOXELS = 512
BRICK_X = 16
BRICK_Y = 4
BRICK_Z = 4
OFFSET_STEPS = 2
REDIST_PASSES = 2
REGIONS = 4
GROUP_DEVS = 64
LEAVES_DEV = 256
LEAVES = 65536
FACES_PEER = 128
FACES_REGION = 16
HALF_SLOTS = 4
PEER_SLOTS = 8


def brick_layout(key):
    regions = REGIONS
    peer_count = GROUP_DEVS
    count = LEAVES_DEV
    keys = jax.random.split(jax.random.fold_in(key, 7001), 4)
    slot_of = jax.vmap(lambda subkey: jax.random.permutation(subkey, count))(jax.random.split(keys[0], regions * peer_count))
    slot_of = slot_of.astype(jnp.int32).reshape(regions, peer_count, count)
    leaf_at = jnp.argsort(slot_of, axis=2).astype(jnp.int32)
    ranking = jax.vmap(lambda subkey: jax.random.permutation(subkey, peer_count))(jax.random.split(keys[1], regions)).astype(jnp.int32)
    inverse = jnp.argsort(ranking, axis=1).astype(jnp.int32)
    classes = peer_count - 1
    grid_size = classes * HALF_SLOTS
    score = jax.random.permutation(keys[2], grid_size).astype(jnp.int32)
    cells = jnp.arange(grid_size, dtype=jnp.int32)
    forced = cells // HALF_SLOTS == peer_count // 2 - 1
    score = jnp.where(forced, score - grid_size, score)
    chosen = jnp.argsort(score).astype(jnp.int32)[:FACES_PEER]
    chosen = chosen[jax.random.permutation(keys[3], FACES_PEER)]
    shift_of = (chosen // HALF_SLOTS + 1).astype(jnp.int32)
    slot_in = (chosen % HALF_SLOTS).astype(jnp.int32)
    return (slot_of, leaf_at, ranking, inverse, shift_of, slot_in)


def peer_faces():
    places = jnp.arange(FACES_PEER, dtype=jnp.int32)
    y_count = BRICK_X * BRICK_Z
    on_y = places < y_count
    first = jnp.minimum(places, y_count - 1)
    second = jnp.maximum(places - y_count, 0)
    x_of_y = first // BRICK_Z
    z_of_y = first % BRICK_Z
    x_of_z = second // BRICK_Y
    y_of_z = second % BRICK_Y
    high_leaf = jnp.where(on_y, (x_of_y * BRICK_Y + BRICK_Y - 1) * BRICK_Z + z_of_y, (x_of_z * BRICK_Y + y_of_z) * BRICK_Z + BRICK_Z - 1)
    low_leaf = jnp.where(on_y, x_of_y * BRICK_Y * BRICK_Z + z_of_y, (x_of_z * BRICK_Y + y_of_z) * BRICK_Z)
    high_side = jnp.where(on_y, 3, 5).astype(jnp.int32)
    return (high_leaf.astype(jnp.int32), low_leaf.astype(jnp.int32), high_side)


def draw_peer_slabs(key, part):
    slot_of, leaf_at, ranking, inverse, shift_of, slot_in = brick_layout(key)
    high_leaf, low_leaf, high_side = peer_faces()
    regions = REGIONS
    peer_count = GROUP_DEVS
    count = LEAVES_DEV
    region_idx = jnp.arange(regions, dtype=jnp.int32)[:, None, None]
    device_idx = jnp.arange(peer_count, dtype=jnp.int32)[None, :, None]
    rank = ranking[:, :, None]
    up_target = inverse[region_idx, (rank + shift_of) % peer_count]
    down_target = inverse[region_idx, (rank - shift_of + peer_count) % peer_count]
    high_ids = high_side * count + slot_of[:, :, high_leaf]
    low_ids = (high_side - 1) * count + slot_of[:, :, low_leaf]
    listing = jnp.full((regions, peer_count, peer_count, PEER_SLOTS), -1, jnp.int32)
    listing = listing.at[region_idx, device_idx, up_target, slot_in].set(high_ids)
    listing = listing.at[region_idx, device_idx, down_target, HALF_SLOTS + slot_in].set(low_ids)
    return listing.reshape(regions * peer_count * peer_count, PEER_SLOTS)


def draw_region_slabs(key, part):
    slot_of, leaf_at, ranking, inverse, shift_of, slot_in = brick_layout(key)
    count = LEAVES_DEV
    places = jnp.arange(FACES_REGION, dtype=jnp.int32)
    y_place = places // BRICK_Z
    z_place = places % BRICK_Z
    low_leaf = y_place * BRICK_Z + z_place
    high_leaf = ((BRICK_X - 1) * BRICK_Y + y_place) * BRICK_Z + z_place
    stacked = jnp.stack([slot_of[:, :, low_leaf], count + slot_of[:, :, high_leaf]], axis=2)
    return stacked.reshape(REGIONS * GROUP_DEVS * 2, FACES_REGION).astype(jnp.int32)


def draw_halo_source(key, part):
    slot_of, leaf_at, ranking, inverse, shift_of, slot_in = brick_layout(key)
    regions = REGIONS
    peer_count = GROUP_DEVS
    count = LEAVES_DEV
    plane = BRICK_Y * BRICK_Z
    lattice = leaf_at
    x_pos = lattice // plane
    y_pos = lattice // BRICK_Z % BRICK_Y
    z_pos = lattice % BRICK_Z

    def slot_at(place):
        return jnp.take_along_axis(slot_of, jnp.clip(place, 0, count - 1), axis=2)
    local_total = 6 * count
    region_base = local_total + peer_count * PEER_SLOTS
    rank = ranking[:, :, None]
    region_idx = jnp.arange(regions, dtype=jnp.int32)[:, None, None]
    y_face = x_pos * BRICK_Z + z_pos
    z_face = BRICK_X * BRICK_Z + x_pos * BRICK_Y + y_pos

    def from_below(face):
        source = inverse[region_idx, (rank - shift_of[face] + peer_count) % peer_count]
        return local_total + source * PEER_SLOTS + slot_in[face]

    def from_above(face):
        source = inverse[region_idx, (rank + shift_of[face]) % peer_count]
        return local_total + source * PEER_SLOTS + HALF_SLOTS + slot_in[face]
    cross_place = y_pos * BRICK_Z + z_pos
    side_zero = jnp.where(x_pos > 0, count + slot_at(lattice - plane), region_base + cross_place)
    side_one = jnp.where(x_pos < BRICK_X - 1, slot_at(lattice + plane), region_base + FACES_REGION + cross_place)
    side_two = jnp.where(y_pos > 0, 3 * count + slot_at(lattice - BRICK_Z), from_below(y_face))
    side_three = jnp.where(y_pos < BRICK_Y - 1, 2 * count + slot_at(lattice + BRICK_Z), from_above(y_face))
    side_four = jnp.where(z_pos > 0, 5 * count + slot_at(lattice - 1), from_below(z_face))
    side_five = jnp.where(z_pos < BRICK_Z - 1, 4 * count + slot_at(lattice + 1), from_above(z_face))
    stacked = jnp.stack([side_zero, side_one, side_two, side_three, side_four, side_five], axis=0)
    return stacked.reshape(6, regions * peer_count * count).astype(jnp.int32)


def steps_of(own_key, shape, cuts, smallest, top_value):
    def one(dim, blocks):
        steps = jax.random.uniform(jax.random.fold_in(jax.random.fold_in(own_key, 6), dim), (blocks,), jnp.float32, smallest / len(cuts), top_value / len(cuts))
        return jnp.repeat(jnp.exp(steps), shape[dim] // blocks).reshape((-1,) + (1,) * (len(shape) - dim - 1))

    gain = one(*cuts[0])
    for cut in cuts[1:]:
        gain = gain * one(*cut)
    return gain


def noise(key, shape, deviation, bound, cuts=(), kind=jnp.bfloat16):
    values = jax.random.normal(key, shape, jnp.float32) * deviation
    if len(cuts) > 0:
        values = steps_of(key, shape, cuts, -0.22, 0.18) * values
    return jnp.clip(values, min=-bound, max=bound).astype(kind)


def setup_inputs(seed: int = 0) -> dict:
    seeds = jax.random.split(jax.random.key(seed), 6)
    return {
        "level_set": noise(seeds[0], (LEAF_VOXELS, LEAVES), 2.0, 8.0, ((1, 256),), jnp.float32),
        "speed": jnp.clip(jnp.exp(math.log(1.0) - 1.3862944 * jax.random.uniform(seeds[1], (LEAF_VOXELS, LEAVES), jnp.float32) ** steps_of(seeds[1], (LEAF_VOXELS, LEAVES), ((1, 256),), -0.2, 0.2)), 0.25, 1.0),
        "peer_slabs": draw_peer_slabs(jax.random.fold_in(seeds[5], 71), 0),
        "region_slabs": draw_region_slabs(jax.random.fold_in(seeds[5], 71), 0),
        "halo_source": draw_halo_source(jax.random.fold_in(seeds[5], 71), 0),
    }


advect_scale = 0.3
relax_scale = 0.3
weno_floor = 1e-06

def face_slabs(voxels, layers):
    count = voxels.shape[3]
    pieces = [voxels[:layers], voxels[8 - layers:], voxels[:, :layers], voxels[:, 8 - layers:], voxels[:, :, :layers], voxels[:, :, 8 - layers:]]
    return jnp.concatenate([piece.reshape(64 * layers, count) for piece in pieces], axis=1)

def weno_side(first, second, third, fourth, fifth):
    guess_a = first / 3.0 - 7.0 * second / 6.0 + 11.0 * third / 6.0
    guess_b = -second / 6.0 + 5.0 * third / 6.0 + fourth / 3.0
    guess_c = third / 3.0 + 5.0 * fourth / 6.0 - fifth / 6.0
    bend_a = first - 2.0 * second + third
    tilt_a = first - 4.0 * second + 3.0 * third
    bend_b = second - 2.0 * third + fourth
    tilt_b = second - fourth
    bend_c = third - 2.0 * fourth + fifth
    tilt_c = 3.0 * third - 4.0 * fourth + fifth
    smooth_a = weno_floor + 13.0 / 12.0 * bend_a * bend_a + 0.25 * tilt_a * tilt_a
    smooth_b = weno_floor + 13.0 / 12.0 * bend_b * bend_b + 0.25 * tilt_b * tilt_b
    smooth_c = weno_floor + 13.0 / 12.0 * bend_c * bend_c + 0.25 * tilt_c * tilt_c
    weight_a = 0.1 / (smooth_a * smooth_a)
    weight_b = 0.6 / (smooth_b * smooth_b)
    weight_c = 0.3 / (smooth_c * smooth_c)
    return (weight_a * guess_a + weight_b * guess_b + weight_c * guess_c) / (weight_a + weight_b + weight_c)

def one_sided(padded, along):
    differences = jnp.diff(padded, axis=along)

    def window(lowest):
        return lax.slice_in_dim(differences, lowest, lowest + 8, axis=along)
    backward = weno_side(window(0), window(1), window(2), window(3), window(4))
    forward = weno_side(window(5), window(4), window(3), window(2), window(1))
    return (backward, forward)

def widen(voxels, picked, layers):
    count = voxels.shape[3]

    def face_part(side, extent):
        return picked[:, side, :].reshape(extent + (count,))
    along_x = jnp.concatenate([face_part(0, (layers, 8, 8)), voxels, face_part(1, (layers, 8, 8))], axis=0)
    along_y = jnp.concatenate([face_part(2, (8, layers, 8)), voxels, face_part(3, (8, layers, 8))], axis=1)
    along_z = jnp.concatenate([face_part(4, (8, 8, layers)), voxels, face_part(5, (8, 8, layers))], axis=2)
    return (along_x, along_y, along_z)

def advect_leaves(voxels, speeds, picked):
    squared = jnp.zeros_like(voxels)
    for along, padded in enumerate(widen(voxels, picked, 3)):
        backward, forward = one_sided(padded, along)
        squared = squared + jnp.maximum(jnp.square(jnp.maximum(backward, 0.0)), jnp.square(jnp.minimum(forward, 0.0)))
    return voxels - advect_scale * speeds * jnp.sqrt(squared)

def relax_leaves(voxels, sign_field, picked):
    squared = jnp.zeros_like(voxels)
    for along, padded in enumerate(widen(voxels, picked, 1)):
        centre = lax.slice_in_dim(padded, 1, 9, axis=along)
        backward = centre - lax.slice_in_dim(padded, 0, 8, axis=along)
        forward = lax.slice_in_dim(padded, 2, 10, axis=along) - centre
        rising = jnp.maximum(jnp.square(jnp.maximum(backward, 0.0)), jnp.square(jnp.minimum(forward, 0.0)))
        falling = jnp.maximum(jnp.square(jnp.minimum(backward, 0.0)), jnp.square(jnp.maximum(forward, 0.0)))
        squared = squared + jnp.where(sign_field > 0.0, rising, falling)
    return voxels - relax_scale * sign_field * (jnp.sqrt(squared) - 1.0)

def pick_columns(entries, indices):
    return jnp.take(entries, indices, axis=1)

def halo_pass(voxels, layers, peer_slabs, region_slabs, sources):
    regions = voxels.shape[0]
    peer_count = voxels.shape[1]
    slab_rows = 64 * layers
    tables = jax.vmap(jax.vmap(lambda block: face_slabs(block, layers)))(voxels)
    pick = jax.vmap(jax.vmap(pick_columns))
    sends = jnp.maximum(peer_slabs.reshape(regions, peer_count, peer_count * PEER_SLOTS), 0)
    outgoing = pick(tables, sends).reshape(regions, peer_count, slab_rows, peer_count, PEER_SLOTS)
    arrived = jnp.transpose(outgoing, (0, 3, 2, 1, 4)).reshape(regions, peer_count, slab_rows, peer_count * PEER_SLOTS)
    border = pick(tables, region_slabs.reshape(regions, peer_count, 2 * FACES_REGION))
    border = border.reshape(regions, peer_count, slab_rows, 2, FACES_REGION)
    preceding = jnp.roll(border[:, :, :, 1], 1, axis=0)
    following = jnp.roll(border[:, :, :, 0], -1, axis=0)
    combined = jnp.concatenate([tables, arrived, preceding, following], axis=3)
    return pick(combined, sources)

def map_devices(update, first, second, third):
    leading = first.shape[:2]
    flattened = tuple((array.reshape((-1,) + array.shape[2:]) for array in (first, second, third)))
    updated = lax.map(lambda items: update(items[0], items[1], items[2]), flattened)
    return updated.reshape(leading + updated.shape[1:])

def reference(level_set, speed, peer_slabs, region_slabs, halo_source):
    regions = REGIONS
    peer_count = GROUP_DEVS
    count = LEAVES_DEV

    def per_device(values):
        return values.reshape(512, regions, peer_count, count).transpose(1, 2, 0, 3).reshape(regions, peer_count, 8, 8, 8, count)
    voxels = per_device(level_set)
    speeds = per_device(speed)
    sources = halo_source.reshape(6, regions, peer_count, count).transpose(1, 2, 0, 3)
    for offset_step in range(OFFSET_STEPS):
        picked = halo_pass(voxels, 3, peer_slabs, region_slabs, sources)
        voxels = map_devices(advect_leaves, voxels, speeds, picked)
        sign_field = voxels / jnp.sqrt(voxels * voxels + 1.0)
        for redist_pass in range(REDIST_PASSES):
            picked = halo_pass(voxels, 1, peer_slabs, region_slabs, sources)
            voxels = map_devices(relax_leaves, voxels, sign_field, picked)
    return voxels.reshape(regions, peer_count, 512, count).transpose(2, 0, 1, 3).reshape(512, regions * peer_count * count)
```

```python
import jax
import jax.numpy as jnp
from jax import lax
from jax.experimental import pallas as pl
from jax.experimental.pallas import tpu as pltpu
from jax.sharding import PartitionSpec as P

OFFSET_STEPS = 2
REDIST_PASSES = 2


advect_scale = 0.3
relax_scale = 0.3
weno_floor = 1e-06


def with_halo(block, sides, width):
    for axis, dim in sides:
        count = lax.axis_size(axis)
        forward = [(i, i + 1) for i in range(count - 1)]
        forward.append((count - 1, 0))
        backward = [(target, source) for source, target in forward]
        low = lax.ppermute(
            lax.slice_in_dim(block, block.shape[dim] - width, None, axis=dim), axis, forward
        )
        high = lax.ppermute(lax.slice_in_dim(block, 0, width, axis=dim), axis, backward)
        block = jnp.concatenate([low, block, high], axis=dim)
    return block


def face_slabs(voxels, layers):
    count = voxels.shape[3]
    pieces = [
        voxels[:layers],
        voxels[8 - layers :],
        voxels[:, :layers],
        voxels[:, 8 - layers :],
        voxels[:, :, :layers],
        voxels[:, :, 8 - layers :],
    ]
    return jnp.concatenate([piece.reshape(64 * layers, count) for piece in pieces], axis=1)


def weno_side(first, second, third, fourth, fifth):
    guess_a = first / 3.0 - 7.0 * second / 6.0 + 11.0 * third / 6.0
    guess_b = -second / 6.0 + 5.0 * third / 6.0 + fourth / 3.0
    guess_c = third / 3.0 + 5.0 * fourth / 6.0 - fifth / 6.0
    bend_a = first - 2.0 * second + third
    tilt_a = first - 4.0 * second + 3.0 * third
    bend_b = second - 2.0 * third + fourth
    tilt_b = second - fourth
    bend_c = third - 2.0 * fourth + fifth
    tilt_c = 3.0 * third - 4.0 * fourth + fifth
    smooth_a = weno_floor + 13.0 / 12.0 * bend_a * bend_a + 0.25 * tilt_a * tilt_a
    smooth_b = weno_floor + 13.0 / 12.0 * bend_b * bend_b + 0.25 * tilt_b * tilt_b
    smooth_c = weno_floor + 13.0 / 12.0 * bend_c * bend_c + 0.25 * tilt_c * tilt_c
    weight_a = 0.1 / (smooth_a * smooth_a)
    weight_b = 0.6 / (smooth_b * smooth_b)
    weight_c = 0.3 / (smooth_c * smooth_c)
    return (weight_a * guess_a + weight_b * guess_b + weight_c * guess_c) / (
        weight_a + weight_b + weight_c
    )


def one_sided(padded, along):
    differences = jnp.diff(padded, axis=along)

    def window(lowest):
        return lax.slice_in_dim(differences, lowest, lowest + 8, axis=along)

    backward = weno_side(window(0), window(1), window(2), window(3), window(4))
    forward = weno_side(window(5), window(4), window(3), window(2), window(1))
    return (backward, forward)


def widen(voxels, picked, layers):
    count = voxels.shape[3]

    def face_part(side, extent):
        return picked[:, side, :].reshape(extent + (count,))

    along_x = jnp.concatenate(
        [face_part(0, (layers, 8, 8)), voxels, face_part(1, (layers, 8, 8))], axis=0
    )
    along_y = jnp.concatenate(
        [face_part(2, (8, layers, 8)), voxels, face_part(3, (8, layers, 8))], axis=1
    )
    along_z = jnp.concatenate(
        [face_part(4, (8, 8, layers)), voxels, face_part(5, (8, 8, layers))], axis=2
    )
    return (along_x, along_y, along_z)


def advect_leaves(voxels, speeds, picked):
    squared = jnp.zeros_like(voxels)
    for along, padded in enumerate(widen(voxels, picked, 3)):
        backward, forward = one_sided(padded, along)
        squared = squared + jnp.maximum(
            jnp.square(jnp.maximum(backward, 0.0)), jnp.square(jnp.minimum(forward, 0.0))
        )
    return voxels - advect_scale * speeds * jnp.sqrt(squared)


def relax_leaves(voxels, sign_field, picked):
    squared = jnp.zeros_like(voxels)
    for along, padded in enumerate(widen(voxels, picked, 1)):
        centre = lax.slice_in_dim(padded, 1, 9, axis=along)
        backward = centre - lax.slice_in_dim(padded, 0, 8, axis=along)
        forward = lax.slice_in_dim(padded, 2, 10, axis=along) - centre
        rising = jnp.maximum(
            jnp.square(jnp.maximum(backward, 0.0)), jnp.square(jnp.minimum(forward, 0.0))
        )
        falling = jnp.maximum(
            jnp.square(jnp.minimum(backward, 0.0)), jnp.square(jnp.maximum(forward, 0.0))
        )
        squared = squared + jnp.where(sign_field > 0.0, rising, falling)
    return voxels - relax_scale * sign_field * (jnp.sqrt(squared) - 1.0)


def exchange_kernel(out_ref, bord_ref, arr_ref, reg_ref, send_sem, recv_sem, rsend_sem, rrecv_sem):
    peers = lax.axis_size("dev")
    regions = lax.axis_size("group")
    me = lax.axis_index("dev")
    region = lax.axis_index("group")
    up = lax.rem(region + 1, regions)
    down = lax.rem(region + regions - 1, regions)
    mesh_ids = pl.DeviceIdType.MESH

    barrier = pltpu.get_barrier_semaphore()

    def greet(k, carry):
        e = lax.rem(me + k, peers)
        pl.semaphore_signal(barrier, inc=1, device_id=(region, e), device_id_type=mesh_ids)
        return carry

    lax.fori_loop(1, peers, greet, 0)
    pl.semaphore_signal(barrier, inc=1, device_id=(up, me), device_id_type=mesh_ids)
    pl.semaphore_signal(barrier, inc=1, device_id=(down, me), device_id_type=mesh_ids)
    pl.semaphore_wait(barrier, peers + 1)

    pltpu.make_async_remote_copy(
        src_ref=bord_ref.at[1],
        dst_ref=reg_ref.at[0],
        send_sem=rsend_sem,
        recv_sem=rrecv_sem,
        device_id=(up, me),
        device_id_type=mesh_ids,
    ).start()
    pltpu.make_async_remote_copy(
        src_ref=bord_ref.at[0],
        dst_ref=reg_ref.at[1],
        send_sem=rsend_sem,
        recv_sem=rrecv_sem,
        device_id=(down, me),
        device_id_type=mesh_ids,
    ).start()

    def send(k, carry):
        e = lax.rem(me + k, peers)
        pltpu.make_async_remote_copy(
            src_ref=out_ref.at[e],
            dst_ref=arr_ref.at[me],
            send_sem=send_sem,
            recv_sem=recv_sem,
            device_id=(region, e),
            device_id_type=mesh_ids,
        ).start()
        return carry

    lax.fori_loop(1, peers, send, 0)
    pltpu.make_async_copy(out_ref.at[me], arr_ref.at[me], recv_sem).start()

    pltpu.make_async_copy(out_ref.at[pl.ds(0, peers - 1)], out_ref.at[pl.ds(0, peers - 1)], send_sem).wait()
    pltpu.make_async_copy(bord_ref, bord_ref, rsend_sem).wait()
    pltpu.make_async_copy(arr_ref, arr_ref, recv_sem).wait()
    pltpu.make_async_copy(reg_ref, reg_ref, rrecv_sem).wait()


def exchange(outgoing, border, layers):
    vmem = pl.BlockSpec(memory_space=pltpu.VMEM)
    return pl.pallas_call(
        exchange_kernel,
        out_shape=(
            jax.ShapeDtypeStruct(outgoing.shape, outgoing.dtype),
            jax.ShapeDtypeStruct(border.shape, border.dtype),
        ),
        in_specs=[vmem, vmem],
        out_specs=(vmem, vmem),
        scratch_shapes=[
            pltpu.SemaphoreType.DMA(()),
            pltpu.SemaphoreType.DMA(()),
            pltpu.SemaphoreType.DMA(()),
            pltpu.SemaphoreType.DMA(()),
        ],
        compiler_params=pltpu.CompilerParams(collective_id=layers, has_side_effects=True),
    )(outgoing, border)


def assemble(voxels, layers, peer_slabs, region_slabs, halo_source):
    slab_table = face_slabs(voxels, layers)
    slab_rows = 64 * layers
    region_width = region_slabs.shape[1]
    peers = peer_slabs.shape[0]
    slots = peer_slabs.shape[1]
    outgoing = jnp.take(slab_table, jnp.maximum(peer_slabs.reshape(-1), 0), axis=1)
    outgoing = outgoing.T.reshape(peers, slots, slab_rows)
    border = jnp.take(slab_table, region_slabs.reshape(-1), axis=1)
    border = border.T.reshape(2, region_width, slab_rows)
    arrived, beside = exchange(outgoing, border, layers)
    arrived = arrived.reshape(peers * slots, slab_rows).T
    beside = beside.reshape(2 * region_width, slab_rows).T
    combined = jnp.concatenate([slab_table, arrived, beside], axis=1)
    picked = jnp.take(combined, halo_source, axis=1)
    return picked


def per_device(level_set, speed, peer_slabs, region_slabs, halo_source):
    count = level_set.shape[1]
    voxels = level_set.reshape(8, 8, 8, count)
    speeds = speed.reshape(8, 8, 8, count)
    for offset_step in range(OFFSET_STEPS):
        picked = assemble(voxels, 3, peer_slabs, region_slabs, halo_source)
        voxels = advect_leaves(voxels, speeds, picked)
        sign_field = voxels / jnp.sqrt(voxels * voxels + 1.0)
        for redist_pass in range(REDIST_PASSES):
            picked = assemble(voxels, 1, peer_slabs, region_slabs, halo_source)
            voxels = relax_leaves(voxels, sign_field, picked)
    return voxels.reshape(512, count)


def solution(mesh):
    return jax.shard_map(
        per_device,
        mesh=mesh,
        in_specs=(
            P(None, ("group", "dev")),
            P(None, ("group", "dev")),
            P(("group", "dev"), None),
            P(("group", "dev"), None),
            P(None, ("group", "dev")),
        ),
        out_specs=P(None, ("group", "dev")),
        check_vma=False,
    )
```

```python
import functools

import jax
import jax.numpy as jnp
from jax import lax
from jax.experimental import pallas as pl
from jax.experimental.pallas import tpu as pltpu
from jax.sharding import PartitionSpec as P

OFFSET_STEPS = 2
REDIST_PASSES = 2


advect_scale = 0.3
relax_scale = 0.3
weno_floor = 1e-06


def with_halo(block, sides, width):
    for axis, dim in sides:
        count = lax.axis_size(axis)
        forward = [(i, i + 1) for i in range(count - 1)]
        forward.append((count - 1, 0))
        backward = [(target, source) for source, target in forward]
        low = lax.ppermute(
            lax.slice_in_dim(block, block.shape[dim] - width, None, axis=dim), axis, forward
        )
        high = lax.ppermute(lax.slice_in_dim(block, 0, width, axis=dim), axis, backward)
        block = jnp.concatenate([low, block, high], axis=dim)
    return block


def face_slabs(voxels, layers):
    count = voxels.shape[3]
    pieces = [
        voxels[:layers],
        voxels[8 - layers :],
        voxels[:, :layers],
        voxels[:, 8 - layers :],
        voxels[:, :, :layers],
        voxels[:, :, 8 - layers :],
    ]
    return jnp.concatenate([piece.reshape(64 * layers, count) for piece in pieces], axis=1)


def weno_side(first, second, third, fourth, fifth):
    guess_a = first / 3.0 - 7.0 * second / 6.0 + 11.0 * third / 6.0
    guess_b = -second / 6.0 + 5.0 * third / 6.0 + fourth / 3.0
    guess_c = third / 3.0 + 5.0 * fourth / 6.0 - fifth / 6.0
    bend_a = first - 2.0 * second + third
    tilt_a = first - 4.0 * second + 3.0 * third
    bend_b = second - 2.0 * third + fourth
    tilt_b = second - fourth
    bend_c = third - 2.0 * fourth + fifth
    tilt_c = 3.0 * third - 4.0 * fourth + fifth
    smooth_a = weno_floor + 13.0 / 12.0 * bend_a * bend_a + 0.25 * tilt_a * tilt_a
    smooth_b = weno_floor + 13.0 / 12.0 * bend_b * bend_b + 0.25 * tilt_b * tilt_b
    smooth_c = weno_floor + 13.0 / 12.0 * bend_c * bend_c + 0.25 * tilt_c * tilt_c
    weight_a = 0.1 / (smooth_a * smooth_a)
    weight_b = 0.6 / (smooth_b * smooth_b)
    weight_c = 0.3 / (smooth_c * smooth_c)
    return (weight_a * guess_a + weight_b * guess_b + weight_c * guess_c) / (
        weight_a + weight_b + weight_c
    )


def one_sided(padded, along):
    differences = jnp.diff(padded, axis=along)

    def window(lowest):
        return lax.slice_in_dim(differences, lowest, lowest + 8, axis=along)

    backward = weno_side(window(0), window(1), window(2), window(3), window(4))
    forward = weno_side(window(5), window(4), window(3), window(2), window(1))
    return (backward, forward)


def widen(voxels, picked, layers):
    count = voxels.shape[3]

    def face_part(side, extent):
        return picked[:, side, :].reshape(extent + (count,))

    along_x = jnp.concatenate(
        [face_part(0, (layers, 8, 8)), voxels, face_part(1, (layers, 8, 8))], axis=0
    )
    along_y = jnp.concatenate(
        [face_part(2, (8, layers, 8)), voxels, face_part(3, (8, layers, 8))], axis=1
    )
    along_z = jnp.concatenate(
        [face_part(4, (8, 8, layers)), voxels, face_part(5, (8, 8, layers))], axis=2
    )
    return (along_x, along_y, along_z)


def advect_leaves(voxels, speeds, picked):
    squared = jnp.zeros_like(voxels)
    for along, padded in enumerate(widen(voxels, picked, 3)):
        backward, forward = one_sided(padded, along)
        squared = squared + jnp.maximum(
            jnp.square(jnp.maximum(backward, 0.0)), jnp.square(jnp.minimum(forward, 0.0))
        )
    return voxels - advect_scale * speeds * jnp.sqrt(squared)


def relax_leaves(voxels, sign_field, picked):
    squared = jnp.zeros_like(voxels)
    for along, padded in enumerate(widen(voxels, picked, 1)):
        centre = lax.slice_in_dim(padded, 1, 9, axis=along)
        backward = centre - lax.slice_in_dim(padded, 0, 8, axis=along)
        forward = lax.slice_in_dim(padded, 2, 10, axis=along) - centre
        rising = jnp.maximum(
            jnp.square(jnp.maximum(backward, 0.0)), jnp.square(jnp.minimum(forward, 0.0))
        )
        falling = jnp.maximum(
            jnp.square(jnp.minimum(backward, 0.0)), jnp.square(jnp.maximum(forward, 0.0))
        )
        squared = squared + jnp.where(sign_field > 0.0, rising, falling)
    return voxels - relax_scale * sign_field * (jnp.sqrt(squared) - 1.0)


def exchange_kernel(
    ring, out_ref, bord_ref, arr_ref, reg_ref, mid_ref, turned_ref, sems
):
    peers = lax.axis_size("dev")
    regions = lax.axis_size("group")
    rows = peers // ring
    me = lax.axis_index("dev")
    region = lax.axis_index("group")
    row = me // ring
    col = me % ring
    up = lax.rem(region + 1, regions)
    down = lax.rem(region + regions - 1, regions)
    mesh_ids = pl.DeviceIdType.MESH

    barrier = pltpu.get_barrier_semaphore()
    for k in range(1, rows):
        other = lax.rem(row + k, rows) * ring + col
        pl.semaphore_signal(barrier, inc=1, device_id=(region, other), device_id_type=mesh_ids)
    for k in range(1, ring):
        other = row * ring + lax.rem(col + k, ring)
        pl.semaphore_signal(barrier, inc=1, device_id=(region, other), device_id_type=mesh_ids)
    pl.semaphore_signal(barrier, inc=1, device_id=(up, me), device_id_type=mesh_ids)
    pl.semaphore_signal(barrier, inc=1, device_id=(down, me), device_id_type=mesh_ids)
    pl.semaphore_wait(barrier, rows + ring)

    pltpu.make_async_remote_copy(
        src_ref=bord_ref.at[1],
        dst_ref=reg_ref.at[0],
        send_sem=sems.at[4],
        recv_sem=sems.at[5],
        device_id=(up, me),
        device_id_type=mesh_ids,
    ).start()
    pltpu.make_async_remote_copy(
        src_ref=bord_ref.at[0],
        dst_ref=reg_ref.at[1],
        send_sem=sems.at[4],
        recv_sem=sems.at[5],
        device_id=(down, me),
        device_id_type=mesh_ids,
    ).start()

    for k in range(1, rows):
        target = lax.rem(row + k, rows)
        pltpu.make_async_remote_copy(
            src_ref=out_ref.at[pl.ds(target * ring, ring)],
            dst_ref=mid_ref.at[row],
            send_sem=sems.at[0],
            recv_sem=sems.at[1],
            device_id=(region, target * ring + col),
            device_id_type=mesh_ids,
        ).start()
    pltpu.make_async_copy(out_ref.at[pl.ds(row * ring, ring)], mid_ref.at[row], sems.at[1]).start()
    pltpu.make_async_copy(mid_ref, mid_ref, sems.at[1]).wait()

    for c in range(ring):
        turned_ref[c] = mid_ref[:, c]

    for k in range(1, ring):
        target = lax.rem(col + k, ring)
        pltpu.make_async_remote_copy(
            src_ref=turned_ref.at[target],
            dst_ref=arr_ref.at[col],
            send_sem=sems.at[2],
            recv_sem=sems.at[3],
            device_id=(region, row * ring + target),
            device_id_type=mesh_ids,
        ).start()
    pltpu.make_async_copy(turned_ref.at[col], arr_ref.at[col], sems.at[3]).start()

    pltpu.make_async_copy(mid_ref.at[pl.ds(0, rows - 1)], mid_ref.at[pl.ds(0, rows - 1)], sems.at[0]).wait()
    pltpu.make_async_copy(turned_ref.at[pl.ds(0, ring - 1)], turned_ref.at[pl.ds(0, ring - 1)], sems.at[2]).wait()
    pltpu.make_async_copy(bord_ref, bord_ref, sems.at[4]).wait()
    pltpu.make_async_copy(arr_ref, arr_ref, sems.at[3]).wait()
    pltpu.make_async_copy(reg_ref, reg_ref, sems.at[5]).wait()


def exchange(outgoing, border, layers, ring):
    peers, slots, slab_rows = outgoing.shape
    rows = peers // ring
    vmem = pl.BlockSpec(memory_space=pltpu.VMEM)
    return pl.pallas_call(
        functools.partial(exchange_kernel, ring),
        out_shape=(
            jax.ShapeDtypeStruct((ring, rows, slots, slab_rows), outgoing.dtype),
            jax.ShapeDtypeStruct(border.shape, border.dtype),
        ),
        in_specs=[vmem, vmem],
        out_specs=(vmem, vmem),
        scratch_shapes=[
            pltpu.VMEM((rows, ring, slots, slab_rows), outgoing.dtype),
            pltpu.VMEM((ring, rows, slots, slab_rows), outgoing.dtype),
            pltpu.SemaphoreType.DMA((6,)),
        ],
        compiler_params=pltpu.CompilerParams(collective_id=layers, has_side_effects=True),
    )(outgoing, border)


def assemble(voxels, layers, peer_slabs, region_slabs, halo_source):
    slab_table = face_slabs(voxels, layers)
    slab_rows = 64 * layers
    region_width = region_slabs.shape[1]
    peers = peer_slabs.shape[0]
    slots = peer_slabs.shape[1]
    outgoing = jnp.take(slab_table, jnp.maximum(peer_slabs.reshape(-1), 0), axis=1)
    outgoing = outgoing.T.reshape(peers, slots, slab_rows)
    border = jnp.take(slab_table, region_slabs.reshape(-1), axis=1)
    border = border.T.reshape(2, region_width, slab_rows)
    ring = 8 if peers % 8 == 0 and peers > 8 else 2
    arrived, beside = exchange(outgoing, border, layers, ring)
    arrived = arrived.reshape(peers * slots, slab_rows).T
    beside = beside.reshape(2 * region_width, slab_rows).T
    combined = jnp.concatenate([slab_table, arrived, beside], axis=1)
    local = slab_table.shape[1]
    entry = halo_source - local
    sender = entry // slots
    moved = local + ((sender % ring) * (peers // ring) + sender // ring) * slots + entry % slots
    inside = (entry >= 0) & (entry < peers * slots)
    picked = jnp.take(combined, jnp.where(inside, moved, halo_source), axis=1)
    return picked


def per_device(level_set, speed, peer_slabs, region_slabs, halo_source):
    count = level_set.shape[1]
    voxels = level_set.reshape(8, 8, 8, count)
    speeds = speed.reshape(8, 8, 8, count)
    for offset_step in range(OFFSET_STEPS):
        picked = assemble(voxels, 3, peer_slabs, region_slabs, halo_source)
        voxels = advect_leaves(voxels, speeds, picked)
        sign_field = voxels / jnp.sqrt(voxels * voxels + 1.0)
        for redist_pass in range(REDIST_PASSES):
            picked = assemble(voxels, 1, peer_slabs, region_slabs, halo_source)
            voxels = relax_leaves(voxels, sign_field, picked)
    return voxels.reshape(512, count)


def solution(mesh):
    return jax.shard_map(
        per_device,
        mesh=mesh,
        in_specs=(
            P(None, ("group", "dev")),
            P(None, ("group", "dev")),
            P(("group", "dev"), None),
            P(("group", "dev"), None),
            P(None, ("group", "dev")),
        ),
        out_specs=P(None, ("group", "dev")),
        check_vma=False,
    )
```

```python
import jax
import jax.numpy as jnp
from jax import lax
from jax.experimental import pallas as pl
from jax.experimental.pallas import tpu as pltpu
from jax.sharding import PartitionSpec as P

OFFSET_STEPS = 2
REDIST_PASSES = 2


advect_scale = 0.3
relax_scale = 0.3
weno_floor = 1e-06


def with_halo(block, sides, width):
    for axis, dim in sides:
        count = lax.axis_size(axis)
        forward = [(i, i + 1) for i in range(count - 1)]
        forward.append((count - 1, 0))
        backward = [(target, source) for source, target in forward]
        low = lax.ppermute(
            lax.slice_in_dim(block, block.shape[dim] - width, None, axis=dim), axis, forward
        )
        high = lax.ppermute(lax.slice_in_dim(block, 0, width, axis=dim), axis, backward)
        block = jnp.concatenate([low, block, high], axis=dim)
    return block


def face_slabs(voxels, layers):
    count = voxels.shape[3]
    pieces = [
        voxels[:layers],
        voxels[8 - layers :],
        voxels[:, :layers],
        voxels[:, 8 - layers :],
        voxels[:, :, :layers],
        voxels[:, :, 8 - layers :],
    ]
    return jnp.concatenate([piece.reshape(64 * layers, count) for piece in pieces], axis=1)


def weno_side(first, second, third, fourth, fifth):
    guess_a = first / 3.0 - 7.0 * second / 6.0 + 11.0 * third / 6.0
    guess_b = -second / 6.0 + 5.0 * third / 6.0 + fourth / 3.0
    guess_c = third / 3.0 + 5.0 * fourth / 6.0 - fifth / 6.0
    bend_a = first - 2.0 * second + third
    tilt_a = first - 4.0 * second + 3.0 * third
    bend_b = second - 2.0 * third + fourth
    tilt_b = second - fourth
    bend_c = third - 2.0 * fourth + fifth
    tilt_c = 3.0 * third - 4.0 * fourth + fifth
    smooth_a = weno_floor + 13.0 / 12.0 * bend_a * bend_a + 0.25 * tilt_a * tilt_a
    smooth_b = weno_floor + 13.0 / 12.0 * bend_b * bend_b + 0.25 * tilt_b * tilt_b
    smooth_c = weno_floor + 13.0 / 12.0 * bend_c * bend_c + 0.25 * tilt_c * tilt_c
    weight_a = 0.1 / (smooth_a * smooth_a)
    weight_b = 0.6 / (smooth_b * smooth_b)
    weight_c = 0.3 / (smooth_c * smooth_c)
    return (weight_a * guess_a + weight_b * guess_b + weight_c * guess_c) / (
        weight_a + weight_b + weight_c
    )


def one_sided(padded, along):
    differences = jnp.diff(padded, axis=along)

    def window(lowest):
        return lax.slice_in_dim(differences, lowest, lowest + 8, axis=along)

    backward = weno_side(window(0), window(1), window(2), window(3), window(4))
    forward = weno_side(window(5), window(4), window(3), window(2), window(1))
    return (backward, forward)


def widen(voxels, picked, layers):
    count = voxels.shape[3]

    def face_part(side, extent):
        return picked[:, side, :].reshape(extent + (count,))

    along_x = jnp.concatenate(
        [face_part(0, (layers, 8, 8)), voxels, face_part(1, (layers, 8, 8))], axis=0
    )
    along_y = jnp.concatenate(
        [face_part(2, (8, layers, 8)), voxels, face_part(3, (8, layers, 8))], axis=1
    )
    along_z = jnp.concatenate(
        [face_part(4, (8, 8, layers)), voxels, face_part(5, (8, 8, layers))], axis=2
    )
    return (along_x, along_y, along_z)


def advect_leaves(voxels, speeds, picked):
    squared = jnp.zeros_like(voxels)
    for along, padded in enumerate(widen(voxels, picked, 3)):
        backward, forward = one_sided(padded, along)
        squared = squared + jnp.maximum(
            jnp.square(jnp.maximum(backward, 0.0)), jnp.square(jnp.minimum(forward, 0.0))
        )
    return voxels - advect_scale * speeds * jnp.sqrt(squared)


def relax_leaves(voxels, sign_field, picked):
    squared = jnp.zeros_like(voxels)
    for along, padded in enumerate(widen(voxels, picked, 1)):
        centre = lax.slice_in_dim(padded, 1, 9, axis=along)
        backward = centre - lax.slice_in_dim(padded, 0, 8, axis=along)
        forward = lax.slice_in_dim(padded, 2, 10, axis=along) - centre
        rising = jnp.maximum(
            jnp.square(jnp.maximum(backward, 0.0)), jnp.square(jnp.minimum(forward, 0.0))
        )
        falling = jnp.maximum(
            jnp.square(jnp.minimum(backward, 0.0)), jnp.square(jnp.maximum(forward, 0.0))
        )
        squared = squared + jnp.where(sign_field > 0.0, rising, falling)
    return voxels - relax_scale * sign_field * (jnp.sqrt(squared) - 1.0)


def exchange_kernel(out_ref, bord_ref, arr_ref, reg_ref, send_sem, recv_sem, rsend_sem, rrecv_sem):
    peers = lax.axis_size("dev")
    regions = lax.axis_size("group")
    me = lax.axis_index("dev")
    region = lax.axis_index("group")
    up = lax.rem(region + 1, regions)
    down = lax.rem(region + regions - 1, regions)
    mesh_ids = pl.DeviceIdType.MESH

    barrier = pltpu.get_barrier_semaphore()

    def greet(k, carry):
        e = lax.rem(me + k, peers)
        pl.semaphore_signal(barrier, inc=1, device_id=(region, e), device_id_type=mesh_ids)
        return carry

    lax.fori_loop(1, peers, greet, 0)
    pl.semaphore_signal(barrier, inc=1, device_id=(up, me), device_id_type=mesh_ids)
    pl.semaphore_signal(barrier, inc=1, device_id=(down, me), device_id_type=mesh_ids)
    pl.semaphore_wait(barrier, peers + 1)

    pltpu.make_async_remote_copy(
        src_ref=bord_ref.at[1],
        dst_ref=reg_ref.at[0],
        send_sem=rsend_sem,
        recv_sem=rrecv_sem,
        device_id=(up, me),
        device_id_type=mesh_ids,
    ).start()
    pltpu.make_async_remote_copy(
        src_ref=bord_ref.at[0],
        dst_ref=reg_ref.at[1],
        send_sem=rsend_sem,
        recv_sem=rrecv_sem,
        device_id=(down, me),
        device_id_type=mesh_ids,
    ).start()

    def send(k, carry):
        e = lax.rem(me + k, peers)
        pltpu.make_async_remote_copy(
            src_ref=out_ref.at[e],
            dst_ref=arr_ref.at[me],
            send_sem=send_sem,
            recv_sem=recv_sem,
            device_id=(region, e),
            device_id_type=mesh_ids,
        ).start()
        return carry

    lax.fori_loop(1, peers, send, 0)
    pltpu.make_async_copy(out_ref.at[me], arr_ref.at[me], recv_sem).start()

    pltpu.make_async_copy(out_ref.at[pl.ds(0, peers - 1)], out_ref.at[pl.ds(0, peers - 1)], send_sem).wait()
    pltpu.make_async_copy(bord_ref, bord_ref, rsend_sem).wait()
    pltpu.make_async_copy(arr_ref, arr_ref, recv_sem).wait()
    pltpu.make_async_copy(reg_ref, reg_ref, rrecv_sem).wait()


def exchange(outgoing, border, layers):
    vmem = pl.BlockSpec(memory_space=pltpu.VMEM)
    return pl.pallas_call(
        exchange_kernel,
        out_shape=(
            jax.ShapeDtypeStruct(outgoing.shape, outgoing.dtype),
            jax.ShapeDtypeStruct(border.shape, border.dtype),
        ),
        in_specs=[vmem, vmem],
        out_specs=(vmem, vmem),
        scratch_shapes=[
            pltpu.SemaphoreType.DMA(()),
            pltpu.SemaphoreType.DMA(()),
            pltpu.SemaphoreType.DMA(()),
            pltpu.SemaphoreType.DMA(()),
        ],
        compiler_params=pltpu.CompilerParams(collective_id=layers, has_side_effects=True),
    )(outgoing, border)


def assemble(voxels, layers, peer_slabs, region_slabs, halo_source):
    slab_table = face_slabs(voxels, layers)
    slab_rows = 64 * layers
    region_width = region_slabs.shape[1]
    peers = peer_slabs.shape[0]
    slots = peer_slabs.shape[1]
    outgoing = slab_table.at[:, jnp.clip(peer_slabs.reshape(-1), 0, slab_table.shape[1] - 1)].get(mode="promise_in_bounds")
    outgoing = outgoing.T.reshape(peers, slots, slab_rows)
    border = slab_table.at[:, jnp.clip(region_slabs.reshape(-1), 0, slab_table.shape[1] - 1)].get(mode="promise_in_bounds")
    border = border.T.reshape(2, region_width, slab_rows)
    arrived, beside = exchange(outgoing, border, layers)
    arrived = arrived.reshape(peers * slots, slab_rows).T
    beside = beside.reshape(2 * region_width, slab_rows).T
    combined = jnp.concatenate([slab_table, arrived, beside], axis=1)
    picked = combined.at[:, jnp.clip(halo_source, 0, combined.shape[1] - 1)].get(mode="promise_in_bounds")
    return picked


def per_device(level_set, speed, peer_slabs, region_slabs, halo_source):
    count = level_set.shape[1]
    voxels = level_set.reshape(8, 8, 8, count)
    speeds = speed.reshape(8, 8, 8, count)
    for offset_step in range(OFFSET_STEPS):
        picked = assemble(voxels, 3, peer_slabs, region_slabs, halo_source)
        voxels = advect_leaves(voxels, speeds, picked)
        sign_field = voxels / jnp.sqrt(voxels * voxels + 1.0)
        for redist_pass in range(REDIST_PASSES):
            picked = assemble(voxels, 1, peer_slabs, region_slabs, halo_source)
            voxels = relax_leaves(voxels, sign_field, picked)
    return voxels.reshape(512, count)


def solution(mesh):
    return jax.shard_map(
        per_device,
        mesh=mesh,
        in_specs=(
            P(None, ("group", "dev")),
            P(None, ("group", "dev")),
            P(("group", "dev"), None),
            P(("group", "dev"), None),
            P(None, ("group", "dev")),
        ),
        out_specs=P(None, ("group", "dev")),
        check_vma=False,
    )
```

```python
import jax
import jax.numpy as jnp
from jax import lax
from jax.experimental import pallas as pl
from jax.experimental.pallas import tpu as pltpu
from jax.sharding import PartitionSpec as P

OFFSET_STEPS = 2
REDIST_PASSES = 2


advect_scale = 0.3
relax_scale = 0.3
weno_floor = 1e-06


def with_halo(block, sides, width):
    for axis, dim in sides:
        count = lax.axis_size(axis)
        forward = [(i, i + 1) for i in range(count - 1)]
        forward.append((count - 1, 0))
        backward = [(target, source) for source, target in forward]
        low = lax.ppermute(
            lax.slice_in_dim(block, block.shape[dim] - width, None, axis=dim), axis, forward
        )
        high = lax.ppermute(lax.slice_in_dim(block, 0, width, axis=dim), axis, backward)
        block = jnp.concatenate([low, block, high], axis=dim)
    return block


def face_slabs(voxels, layers):
    count = voxels.shape[3]
    pieces = [
        voxels[:layers],
        voxels[8 - layers :],
        voxels[:, :layers],
        voxels[:, 8 - layers :],
        voxels[:, :, :layers],
        voxels[:, :, 8 - layers :],
    ]
    return jnp.concatenate([piece.reshape(64 * layers, count) for piece in pieces], axis=1)


def weno_side(first, second, third, fourth, fifth):
    guess_a = first / 3.0 - 7.0 * second / 6.0 + 11.0 * third / 6.0
    guess_b = -second / 6.0 + 5.0 * third / 6.0 + fourth / 3.0
    guess_c = third / 3.0 + 5.0 * fourth / 6.0 - fifth / 6.0
    bend_a = first - 2.0 * second + third
    tilt_a = first - 4.0 * second + 3.0 * third
    bend_b = second - 2.0 * third + fourth
    tilt_b = second - fourth
    bend_c = third - 2.0 * fourth + fifth
    tilt_c = 3.0 * third - 4.0 * fourth + fifth
    smooth_a = weno_floor + 13.0 / 12.0 * bend_a * bend_a + 0.25 * tilt_a * tilt_a
    smooth_b = weno_floor + 13.0 / 12.0 * bend_b * bend_b + 0.25 * tilt_b * tilt_b
    smooth_c = weno_floor + 13.0 / 12.0 * bend_c * bend_c + 0.25 * tilt_c * tilt_c
    weight_a = 0.1 / (smooth_a * smooth_a)
    weight_b = 0.6 / (smooth_b * smooth_b)
    weight_c = 0.3 / (smooth_c * smooth_c)
    return (weight_a * guess_a + weight_b * guess_b + weight_c * guess_c) / (
        weight_a + weight_b + weight_c
    )


def one_sided(padded, along):
    differences = jnp.diff(padded, axis=along)

    def window(lowest):
        return lax.slice_in_dim(differences, lowest, lowest + 8, axis=along)

    backward = weno_side(window(0), window(1), window(2), window(3), window(4))
    forward = weno_side(window(5), window(4), window(3), window(2), window(1))
    return (backward, forward)


def widen(voxels, picked, layers):
    count = voxels.shape[3]

    def face_part(side, extent):
        return picked[:, side, :].reshape(extent + (count,))

    along_x = jnp.concatenate(
        [face_part(0, (layers, 8, 8)), voxels, face_part(1, (layers, 8, 8))], axis=0
    )
    along_y = jnp.concatenate(
        [face_part(2, (8, layers, 8)), voxels, face_part(3, (8, layers, 8))], axis=1
    )
    along_z = jnp.concatenate(
        [face_part(4, (8, 8, layers)), voxels, face_part(5, (8, 8, layers))], axis=2
    )
    return (along_x, along_y, along_z)


def advect_leaves(voxels, speeds, picked):
    squared = jnp.zeros_like(voxels)
    for along, padded in enumerate(widen(voxels, picked, 3)):
        backward, forward = one_sided(padded, along)
        squared = squared + jnp.maximum(
            jnp.square(jnp.maximum(backward, 0.0)), jnp.square(jnp.minimum(forward, 0.0))
        )
    return voxels - advect_scale * speeds * jnp.sqrt(squared)


def relax_leaves(voxels, sign_field, picked):
    squared = jnp.zeros_like(voxels)
    for along, padded in enumerate(widen(voxels, picked, 1)):
        centre = lax.slice_in_dim(padded, 1, 9, axis=along)
        backward = centre - lax.slice_in_dim(padded, 0, 8, axis=along)
        forward = lax.slice_in_dim(padded, 2, 10, axis=along) - centre
        rising = jnp.maximum(
            jnp.square(jnp.maximum(backward, 0.0)), jnp.square(jnp.minimum(forward, 0.0))
        )
        falling = jnp.maximum(
            jnp.square(jnp.minimum(backward, 0.0)), jnp.square(jnp.maximum(forward, 0.0))
        )
        squared = squared + jnp.where(sign_field > 0.0, rising, falling)
    return voxels - relax_scale * sign_field * (jnp.sqrt(squared) - 1.0)


def exchange_kernel(
    tab_ref, idx_ref, ridx_ref, arr_ref, reg_ref, og_ref, bd_ref, sems
):
    peers, slots = og_ref.shape[0], og_ref.shape[1]
    regions = lax.axis_size("group")
    width = bd_ref.shape[1]
    me = lax.axis_index("dev")
    region = lax.axis_index("group")
    up = lax.rem(region + 1, regions)
    down = lax.rem(region + regions - 1, regions)
    mesh_ids = pl.DeviceIdType.MESH

    barrier = pltpu.get_barrier_semaphore()

    def greet(k, carry):
        e = lax.rem(me + k, peers)
        pl.semaphore_signal(barrier, inc=1, device_id=(region, e), device_id_type=mesh_ids)
        return carry

    lax.fori_loop(1, peers, greet, 0)
    pl.semaphore_signal(barrier, inc=1, device_id=(up, me), device_id_type=mesh_ids)
    pl.semaphore_signal(barrier, inc=1, device_id=(down, me), device_id_type=mesh_ids)

    for h in range(2):
        for p in range(width):
            source = ridx_ref[h * width + p]
            bd_ref[h, pl.ds(p, 1), :] = tab_ref[pl.ds(source, 1), :]

    def pack(e, carry):
        for c in range(slots):
            source = idx_ref[e * slots + c]
            og_ref[e, pl.ds(c, 1), :] = tab_ref[pl.ds(source, 1), :]
        return carry

    lax.fori_loop(0, peers, pack, 0)

    pl.semaphore_wait(barrier, peers + 1)

    pltpu.make_async_remote_copy(
        src_ref=bd_ref.at[1],
        dst_ref=reg_ref.at[0],
        send_sem=sems.at[2],
        recv_sem=sems.at[3],
        device_id=(up, me),
        device_id_type=mesh_ids,
    ).start()
    pltpu.make_async_remote_copy(
        src_ref=bd_ref.at[0],
        dst_ref=reg_ref.at[1],
        send_sem=sems.at[2],
        recv_sem=sems.at[3],
        device_id=(down, me),
        device_id_type=mesh_ids,
    ).start()

    def send(k, carry):
        e = lax.rem(me + k, peers)
        pltpu.make_async_remote_copy(
            src_ref=og_ref.at[e],
            dst_ref=arr_ref.at[me],
            send_sem=sems.at[0],
            recv_sem=sems.at[1],
            device_id=(region, e),
            device_id_type=mesh_ids,
        ).start()
        return carry

    lax.fori_loop(1, peers, send, 0)
    arr_ref[me] = og_ref[me]

    pltpu.make_async_copy(og_ref.at[pl.ds(0, peers - 1)], og_ref.at[pl.ds(0, peers - 1)], sems.at[0]).wait()
    pltpu.make_async_copy(bd_ref, bd_ref, sems.at[2]).wait()
    pltpu.make_async_copy(arr_ref.at[pl.ds(0, peers - 1)], arr_ref.at[pl.ds(0, peers - 1)], sems.at[1]).wait()
    pltpu.make_async_copy(reg_ref, reg_ref, sems.at[3]).wait()


def exchange(table, peer_ids, region_ids, peers, layers):
    entries, slab_rows = table.shape
    slots = peer_ids.shape[0] // peers
    width = region_ids.shape[0] // 2
    vmem = pl.BlockSpec(memory_space=pltpu.VMEM)
    smem = pl.BlockSpec(memory_space=pltpu.SMEM)
    return pl.pallas_call(
        exchange_kernel,
        out_shape=(
            jax.ShapeDtypeStruct((peers, slots, slab_rows), table.dtype),
            jax.ShapeDtypeStruct((2, width, slab_rows), table.dtype),
        ),
        in_specs=[vmem, smem, smem],
        out_specs=(vmem, vmem),
        scratch_shapes=[
            pltpu.VMEM((peers, slots, slab_rows), table.dtype),
            pltpu.VMEM((2, width, slab_rows), table.dtype),
            pltpu.SemaphoreType.DMA((4,)),
        ],
        compiler_params=pltpu.CompilerParams(collective_id=layers, has_side_effects=True),
    )(table, peer_ids, region_ids)


def assemble(voxels, layers, peer_ids, region_ids, halo_ids):
    slab_table = face_slabs(voxels, layers)
    slab_rows = 64 * layers
    peers = lax.axis_size("dev")
    arrived, beside = exchange(slab_table.T, peer_ids, region_ids, peers, layers)
    arrived = arrived.reshape(-1, slab_rows).T
    beside = beside.reshape(-1, slab_rows).T
    combined = jnp.concatenate([slab_table, arrived, beside], axis=1)
    picked = combined.at[:, halo_ids].get(mode="promise_in_bounds")
    return picked


def per_device(level_set, speed, peer_slabs, region_slabs, halo_source):
    count = level_set.shape[1]
    local = 6 * count
    peer_ids = jnp.clip(peer_slabs.reshape(-1), 0, local - 1)
    region_ids = jnp.clip(region_slabs.reshape(-1), 0, local - 1)
    halo_ids = jnp.clip(halo_source, 0, local + peer_ids.shape[0] + region_ids.shape[0] - 1)
    voxels = level_set.reshape(8, 8, 8, count)
    speeds = speed.reshape(8, 8, 8, count)
    for offset_step in range(OFFSET_STEPS):
        picked = assemble(voxels, 3, peer_ids, region_ids, halo_ids)
        voxels = advect_leaves(voxels, speeds, picked)
        sign_field = voxels / jnp.sqrt(voxels * voxels + 1.0)
        for redist_pass in range(REDIST_PASSES):
            picked = assemble(voxels, 1, peer_ids, region_ids, halo_ids)
            voxels = relax_leaves(voxels, sign_field, picked)
    return voxels.reshape(512, count)


def solution(mesh):
    return jax.shard_map(
        per_device,
        mesh=mesh,
        in_specs=(
            P(None, ("group", "dev")),
            P(None, ("group", "dev")),
            P(("group", "dev"), None),
            P(("group", "dev"), None),
            P(None, ("group", "dev")),
        ),
        out_specs=P(None, ("group", "dev")),
        check_vma=False,
    )
```

```python
import jax
import jax.numpy as jnp
from jax import lax
from jax.experimental import pallas as pl
from jax.experimental.pallas import tpu as pltpu
from jax.sharding import PartitionSpec as P

OFFSET_STEPS = 2
REDIST_PASSES = 2


advect_scale = 0.3
relax_scale = 0.3
weno_floor = 1e-06


def with_halo(block, sides, width):
    for axis, dim in sides:
        count = lax.axis_size(axis)
        forward = [(i, i + 1) for i in range(count - 1)]
        forward.append((count - 1, 0))
        backward = [(target, source) for source, target in forward]
        low = lax.ppermute(
            lax.slice_in_dim(block, block.shape[dim] - width, None, axis=dim), axis, forward
        )
        high = lax.ppermute(lax.slice_in_dim(block, 0, width, axis=dim), axis, backward)
        block = jnp.concatenate([low, block, high], axis=dim)
    return block


def face_slabs(voxels, layers):
    count = voxels.shape[3]
    pieces = [
        voxels[:layers],
        voxels[8 - layers :],
        voxels[:, :layers],
        voxels[:, 8 - layers :],
        voxels[:, :, :layers],
        voxels[:, :, 8 - layers :],
    ]
    return jnp.concatenate([piece.reshape(64 * layers, count) for piece in pieces], axis=1)


def weno_side(first, second, third, fourth, fifth):
    guess_a = first / 3.0 - 7.0 * second / 6.0 + 11.0 * third / 6.0
    guess_b = -second / 6.0 + 5.0 * third / 6.0 + fourth / 3.0
    guess_c = third / 3.0 + 5.0 * fourth / 6.0 - fifth / 6.0
    bend_a = first - 2.0 * second + third
    tilt_a = first - 4.0 * second + 3.0 * third
    bend_b = second - 2.0 * third + fourth
    tilt_b = second - fourth
    bend_c = third - 2.0 * fourth + fifth
    tilt_c = 3.0 * third - 4.0 * fourth + fifth
    smooth_a = weno_floor + 13.0 / 12.0 * bend_a * bend_a + 0.25 * tilt_a * tilt_a
    smooth_b = weno_floor + 13.0 / 12.0 * bend_b * bend_b + 0.25 * tilt_b * tilt_b
    smooth_c = weno_floor + 13.0 / 12.0 * bend_c * bend_c + 0.25 * tilt_c * tilt_c
    weight_a = 0.1 / (smooth_a * smooth_a)
    weight_b = 0.6 / (smooth_b * smooth_b)
    weight_c = 0.3 / (smooth_c * smooth_c)
    return (weight_a * guess_a + weight_b * guess_b + weight_c * guess_c) / (
        weight_a + weight_b + weight_c
    )


def one_sided(padded, along):
    differences = jnp.diff(padded, axis=along)

    def window(lowest):
        return lax.slice_in_dim(differences, lowest, lowest + 8, axis=along)

    backward = weno_side(window(0), window(1), window(2), window(3), window(4))
    forward = weno_side(window(5), window(4), window(3), window(2), window(1))
    return (backward, forward)


def widen(voxels, picked, layers):
    count = voxels.shape[3]

    def face_part(side, extent):
        return picked[:, side, :].reshape(extent + (count,))

    along_x = jnp.concatenate(
        [face_part(0, (layers, 8, 8)), voxels, face_part(1, (layers, 8, 8))], axis=0
    )
    along_y = jnp.concatenate(
        [face_part(2, (8, layers, 8)), voxels, face_part(3, (8, layers, 8))], axis=1
    )
    along_z = jnp.concatenate(
        [face_part(4, (8, 8, layers)), voxels, face_part(5, (8, 8, layers))], axis=2
    )
    return (along_x, along_y, along_z)


def advect_leaves(voxels, speeds, picked):
    squared = jnp.zeros_like(voxels)
    for along, padded in enumerate(widen(voxels, picked, 3)):
        backward, forward = one_sided(padded, along)
        squared = squared + jnp.maximum(
            jnp.square(jnp.maximum(backward, 0.0)), jnp.square(jnp.minimum(forward, 0.0))
        )
    return voxels - advect_scale * speeds * jnp.sqrt(squared)


def relax_leaves(voxels, sign_field, picked):
    squared = jnp.zeros_like(voxels)
    for along, padded in enumerate(widen(voxels, picked, 1)):
        centre = lax.slice_in_dim(padded, 1, 9, axis=along)
        backward = centre - lax.slice_in_dim(padded, 0, 8, axis=along)
        forward = lax.slice_in_dim(padded, 2, 10, axis=along) - centre
        rising = jnp.maximum(
            jnp.square(jnp.maximum(backward, 0.0)), jnp.square(jnp.minimum(forward, 0.0))
        )
        falling = jnp.maximum(
            jnp.square(jnp.minimum(backward, 0.0)), jnp.square(jnp.maximum(forward, 0.0))
        )
        squared = squared + jnp.where(sign_field > 0.0, rising, falling)
    return voxels - relax_scale * sign_field * (jnp.sqrt(squared) - 1.0)


def exchange_kernel(
    tab_hbm, idx_ref, ridx_ref, comb_ref, tab_ref, og_ref, bd_ref, sems
):
    peers, slots = og_ref.shape[0], og_ref.shape[1]
    local = tab_ref.shape[0]
    width = bd_ref.shape[1]
    regions = lax.axis_size("group")
    me = lax.axis_index("dev")
    region = lax.axis_index("group")
    up = lax.rem(region + 1, regions)
    down = lax.rem(region + regions - 1, regions)
    mesh_ids = pl.DeviceIdType.MESH
    arrived = local
    bordering = local + peers * slots

    fetch = pltpu.make_async_copy(tab_hbm, tab_ref, sems.at[4])
    fetch.start()
    keep = pltpu.make_async_copy(tab_hbm, comb_ref.at[pl.ds(0, local)], sems.at[5])
    keep.start()

    barrier = pltpu.get_barrier_semaphore()

    def greet(k, carry):
        e = lax.rem(me + k, peers)
        pl.semaphore_signal(barrier, inc=1, device_id=(region, e), device_id_type=mesh_ids)
        return carry

    lax.fori_loop(1, peers, greet, 0)
    pl.semaphore_signal(barrier, inc=1, device_id=(up, me), device_id_type=mesh_ids)
    pl.semaphore_signal(barrier, inc=1, device_id=(down, me), device_id_type=mesh_ids)

    fetch.wait()
    for h in range(2):
        for p in range(width):
            source = ridx_ref[h * width + p]
            bd_ref[h, pl.ds(p, 1), :] = tab_ref[pl.ds(source, 1), :]

    def pack(e, carry):
        for c in range(slots):
            source = idx_ref[e * slots + c]
            og_ref[e, pl.ds(c, 1), :] = tab_ref[pl.ds(source, 1), :]
        return carry

    lax.fori_loop(0, peers, pack, 0)

    pl.semaphore_wait(barrier, peers + 1)

    pltpu.make_async_remote_copy(
        src_ref=bd_ref.at[1],
        dst_ref=comb_ref.at[pl.ds(bordering, width)],
        send_sem=sems.at[2],
        recv_sem=sems.at[3],
        device_id=(up, me),
        device_id_type=mesh_ids,
    ).start()
    pltpu.make_async_remote_copy(
        src_ref=bd_ref.at[0],
        dst_ref=comb_ref.at[pl.ds(bordering + width, width)],
        send_sem=sems.at[2],
        recv_sem=sems.at[3],
        device_id=(down, me),
        device_id_type=mesh_ids,
    ).start()

    mine = pl.ds(pl.multiple_of(arrived + me * slots, slots), slots)

    def send(k, carry):
        e = lax.rem(me + k, peers)
        pltpu.make_async_remote_copy(
            src_ref=og_ref.at[e],
            dst_ref=comb_ref.at[mine],
            send_sem=sems.at[0],
            recv_sem=sems.at[1],
            device_id=(region, e),
            device_id_type=mesh_ids,
        ).start()
        return carry

    lax.fori_loop(1, peers, send, 0)
    comb_ref[mine, :] = og_ref[me]

    pltpu.make_async_copy(og_ref.at[pl.ds(0, peers - 1)], og_ref.at[pl.ds(0, peers - 1)], sems.at[0]).wait()
    pltpu.make_async_copy(bd_ref, bd_ref, sems.at[2]).wait()
    pltpu.make_async_copy(og_ref.at[pl.ds(0, peers - 1)], og_ref.at[pl.ds(0, peers - 1)], sems.at[1]).wait()
    pltpu.make_async_copy(bd_ref, bd_ref, sems.at[3]).wait()
    keep.wait()


def exchange(table, peer_ids, region_ids, peers, layers):
    local, slab_rows = table.shape
    slots = peer_ids.shape[0] // peers
    width = region_ids.shape[0] // 2
    vmem = pl.BlockSpec(memory_space=pltpu.VMEM)
    smem = pl.BlockSpec(memory_space=pltpu.SMEM)
    return pl.pallas_call(
        exchange_kernel,
        out_shape=jax.ShapeDtypeStruct((local + peers * slots + 2 * width, slab_rows), table.dtype),
        in_specs=[pl.BlockSpec(memory_space=pl.ANY), smem, smem],
        out_specs=vmem,
        scratch_shapes=[
            pltpu.VMEM((local, slab_rows), table.dtype),
            pltpu.VMEM((peers, slots, slab_rows), table.dtype),
            pltpu.VMEM((2, width, slab_rows), table.dtype),
            pltpu.SemaphoreType.DMA((6,)),
        ],
        compiler_params=pltpu.CompilerParams(collective_id=layers, has_side_effects=True),
    )(table, peer_ids, region_ids)


def assemble(voxels, layers, peer_ids, region_ids, halo_ids):
    slab_table = face_slabs(voxels, layers)
    peers = lax.axis_size("dev")
    combined = exchange(slab_table.T, peer_ids, region_ids, peers, layers).T
    picked = combined.at[:, halo_ids].get(mode="promise_in_bounds")
    return picked


def per_device(level_set, speed, peer_slabs, region_slabs, halo_source):
    count = level_set.shape[1]
    local = 6 * count
    peer_ids = jnp.clip(peer_slabs.reshape(-1), 0, local - 1)
    region_ids = jnp.clip(region_slabs.reshape(-1), 0, local - 1)
    halo_ids = jnp.clip(halo_source, 0, local + peer_ids.shape[0] + region_ids.shape[0] - 1)
    voxels = level_set.reshape(8, 8, 8, count)
    speeds = speed.reshape(8, 8, 8, count)
    for offset_step in range(OFFSET_STEPS):
        picked = assemble(voxels, 3, peer_ids, region_ids, halo_ids)
        voxels = advect_leaves(voxels, speeds, picked)
        sign_field = voxels / jnp.sqrt(voxels * voxels + 1.0)
        for redist_pass in range(REDIST_PASSES):
            picked = assemble(voxels, 1, peer_ids, region_ids, halo_ids)
            voxels = relax_leaves(voxels, sign_field, picked)
    return voxels.reshape(512, count)


def solution(mesh):
    return jax.shard_map(
        per_device,
        mesh=mesh,
        in_specs=(
            P(None, ("group", "dev")),
            P(None, ("group", "dev")),
            P(("group", "dev"), None),
            P(("group", "dev"), None),
            P(None, ("group", "dev")),
        ),
        out_specs=P(None, ("group", "dev")),
        check_vma=False,
    )
```

```python
import jax
import jax.numpy as jnp
from jax import lax
from jax.experimental import pallas as pl
from jax.experimental.pallas import tpu as pltpu
from jax.sharding import PartitionSpec as P

OFFSET_STEPS = 2
REDIST_PASSES = 2


advect_scale = 0.3
relax_scale = 0.3
weno_floor = 1e-06


def with_halo(block, sides, width):
    for axis, dim in sides:
        count = lax.axis_size(axis)
        forward = [(i, i + 1) for i in range(count - 1)]
        forward.append((count - 1, 0))
        backward = [(target, source) for source, target in forward]
        low = lax.ppermute(
            lax.slice_in_dim(block, block.shape[dim] - width, None, axis=dim), axis, forward
        )
        high = lax.ppermute(lax.slice_in_dim(block, 0, width, axis=dim), axis, backward)
        block = jnp.concatenate([low, block, high], axis=dim)
    return block


def face_slabs(voxels, layers):
    count = voxels.shape[3]
    pieces = [
        voxels[:layers],
        voxels[8 - layers :],
        voxels[:, :layers],
        voxels[:, 8 - layers :],
        voxels[:, :, :layers],
        voxels[:, :, 8 - layers :],
    ]
    return jnp.concatenate([piece.reshape(64 * layers, count) for piece in pieces], axis=1)


def weno_side(first, second, third, fourth, fifth):
    guess_a = first / 3.0 - 7.0 * second / 6.0 + 11.0 * third / 6.0
    guess_b = -second / 6.0 + 5.0 * third / 6.0 + fourth / 3.0
    guess_c = third / 3.0 + 5.0 * fourth / 6.0 - fifth / 6.0
    bend_a = first - 2.0 * second + third
    tilt_a = first - 4.0 * second + 3.0 * third
    bend_b = second - 2.0 * third + fourth
    tilt_b = second - fourth
    bend_c = third - 2.0 * fourth + fifth
    tilt_c = 3.0 * third - 4.0 * fourth + fifth
    smooth_a = weno_floor + 13.0 / 12.0 * bend_a * bend_a + 0.25 * tilt_a * tilt_a
    smooth_b = weno_floor + 13.0 / 12.0 * bend_b * bend_b + 0.25 * tilt_b * tilt_b
    smooth_c = weno_floor + 13.0 / 12.0 * bend_c * bend_c + 0.25 * tilt_c * tilt_c
    weight_a = 0.1 / (smooth_a * smooth_a)
    weight_b = 0.6 / (smooth_b * smooth_b)
    weight_c = 0.3 / (smooth_c * smooth_c)
    return (weight_a * guess_a + weight_b * guess_b + weight_c * guess_c) / (
        weight_a + weight_b + weight_c
    )


def one_sided(padded, along):
    differences = jnp.diff(padded, axis=along)

    def window(lowest):
        return lax.slice_in_dim(differences, lowest, lowest + 8, axis=along)

    backward = weno_side(window(0), window(1), window(2), window(3), window(4))
    forward = weno_side(window(5), window(4), window(3), window(2), window(1))
    return (backward, forward)


def widen(voxels, picked, layers):
    count = voxels.shape[3]

    def face_part(side, extent):
        return picked[:, side, :].reshape(extent + (count,))

    along_x = jnp.concatenate(
        [face_part(0, (layers, 8, 8)), voxels, face_part(1, (layers, 8, 8))], axis=0
    )
    along_y = jnp.concatenate(
        [face_part(2, (8, layers, 8)), voxels, face_part(3, (8, layers, 8))], axis=1
    )
    along_z = jnp.concatenate(
        [face_part(4, (8, 8, layers)), voxels, face_part(5, (8, 8, layers))], axis=2
    )
    return (along_x, along_y, along_z)


def advect_leaves(voxels, speeds, picked):
    squared = jnp.zeros_like(voxels)
    for along, padded in enumerate(widen(voxels, picked, 3)):
        backward, forward = one_sided(padded, along)
        squared = squared + jnp.maximum(
            jnp.square(jnp.maximum(backward, 0.0)), jnp.square(jnp.minimum(forward, 0.0))
        )
    return voxels - advect_scale * speeds * jnp.sqrt(squared)


def relax_leaves(voxels, sign_field, picked):
    squared = jnp.zeros_like(voxels)
    for along, padded in enumerate(widen(voxels, picked, 1)):
        centre = lax.slice_in_dim(padded, 1, 9, axis=along)
        backward = centre - lax.slice_in_dim(padded, 0, 8, axis=along)
        forward = lax.slice_in_dim(padded, 2, 10, axis=along) - centre
        rising = jnp.maximum(
            jnp.square(jnp.maximum(backward, 0.0)), jnp.square(jnp.minimum(forward, 0.0))
        )
        falling = jnp.maximum(
            jnp.square(jnp.minimum(backward, 0.0)), jnp.square(jnp.maximum(forward, 0.0))
        )
        squared = squared + jnp.where(sign_field > 0.0, rising, falling)
    return voxels - relax_scale * sign_field * (jnp.sqrt(squared) - 1.0)


def exchange_kernel(
    tab_ref, idx_ref, ridx_ref, comb_ref, og_ref, bd_ref, sems
):
    peers, slots = og_ref.shape[0], og_ref.shape[1]
    local = tab_ref.shape[0]
    width = bd_ref.shape[1]
    regions = lax.axis_size("group")
    me = lax.axis_index("dev")
    region = lax.axis_index("group")
    up = lax.rem(region + 1, regions)
    down = lax.rem(region + regions - 1, regions)
    mesh_ids = pl.DeviceIdType.MESH
    arrived = local
    bordering = local + peers * slots

    keep = pltpu.make_async_copy(tab_ref, comb_ref.at[pl.ds(0, local)], sems.at[4])
    keep.start()

    barrier = pltpu.get_barrier_semaphore()

    def greet(k, carry):
        e = lax.rem(me + k, peers)
        pl.semaphore_signal(barrier, inc=1, device_id=(region, e), device_id_type=mesh_ids)
        return carry

    lax.fori_loop(1, peers, greet, 0)
    pl.semaphore_signal(barrier, inc=1, device_id=(up, me), device_id_type=mesh_ids)
    pl.semaphore_signal(barrier, inc=1, device_id=(down, me), device_id_type=mesh_ids)

    for h in range(2):
        for p in range(width):
            source = ridx_ref[h * width + p]
            bd_ref[h, pl.ds(p, 1), :] = tab_ref[pl.ds(source, 1), :]

    def pack(e, carry):
        for c in range(slots):
            source = idx_ref[e * slots + c]
            og_ref[e, pl.ds(c, 1), :] = tab_ref[pl.ds(source, 1), :]
        return carry

    lax.fori_loop(0, peers, pack, 0)

    pl.semaphore_wait(barrier, peers + 1)

    pltpu.make_async_remote_copy(
        src_ref=bd_ref.at[1],
        dst_ref=comb_ref.at[pl.ds(bordering, width)],
        send_sem=sems.at[2],
        recv_sem=sems.at[3],
        device_id=(up, me),
        device_id_type=mesh_ids,
    ).start()
    pltpu.make_async_remote_copy(
        src_ref=bd_ref.at[0],
        dst_ref=comb_ref.at[pl.ds(bordering + width, width)],
        send_sem=sems.at[2],
        recv_sem=sems.at[3],
        device_id=(down, me),
        device_id_type=mesh_ids,
    ).start()

    mine = pl.ds(pl.multiple_of(arrived + me * slots, slots), slots)

    def send(k, carry):
        e = lax.rem(me + k, peers)
        pltpu.make_async_remote_copy(
            src_ref=og_ref.at[e],
            dst_ref=comb_ref.at[mine],
            send_sem=sems.at[0],
            recv_sem=sems.at[1],
            device_id=(region, e),
            device_id_type=mesh_ids,
        ).start()
        return carry

    lax.fori_loop(1, peers, send, 0)
    comb_ref[mine, :] = og_ref[me]

    pltpu.make_async_copy(og_ref.at[pl.ds(0, peers - 1)], og_ref.at[pl.ds(0, peers - 1)], sems.at[0]).wait()
    pltpu.make_async_copy(bd_ref, bd_ref, sems.at[2]).wait()
    pltpu.make_async_copy(og_ref.at[pl.ds(0, peers - 1)], og_ref.at[pl.ds(0, peers - 1)], sems.at[1]).wait()
    pltpu.make_async_copy(bd_ref, bd_ref, sems.at[3]).wait()
    keep.wait()


def exchange(table, peer_ids, region_ids, peers, layers):
    local, slab_rows = table.shape
    slots = peer_ids.shape[0] // peers
    width = region_ids.shape[0] // 2
    vmem = pl.BlockSpec(memory_space=pltpu.VMEM)
    smem = pl.BlockSpec(memory_space=pltpu.SMEM)
    return pl.pallas_call(
        exchange_kernel,
        out_shape=(pltpu.VMEM if layers == 1 else jax.ShapeDtypeStruct)(
            (local + peers * slots + 2 * width, slab_rows), table.dtype
        ),
        in_specs=[vmem, smem, smem],
        out_specs=vmem,
        scratch_shapes=[
            pltpu.VMEM((peers, slots, slab_rows), table.dtype),
            pltpu.VMEM((2, width, slab_rows), table.dtype),
            pltpu.SemaphoreType.DMA((5,)),
        ],
        compiler_params=pltpu.CompilerParams(collective_id=layers, has_side_effects=True),
    )(pltpu.with_memory_space_constraint(table, pltpu.VMEM), peer_ids, region_ids)


def assemble(voxels, layers, peer_ids, region_ids, halo_ids):
    slab_table = face_slabs(voxels, layers)
    peers = lax.axis_size("dev")
    combined = exchange(slab_table.T, peer_ids, region_ids, peers, layers).T
    picked = combined.at[:, halo_ids].get(mode="promise_in_bounds")
    return picked


def per_device(level_set, speed, peer_slabs, region_slabs, halo_source):
    count = level_set.shape[1]
    local = 6 * count
    peer_ids = jnp.clip(peer_slabs.reshape(-1), 0, local - 1)
    region_ids = jnp.clip(region_slabs.reshape(-1), 0, local - 1)
    halo_ids = jnp.clip(halo_source, 0, local + peer_ids.shape[0] + region_ids.shape[0] - 1)
    voxels = level_set.reshape(8, 8, 8, count)
    speeds = speed.reshape(8, 8, 8, count)
    for offset_step in range(OFFSET_STEPS):
        picked = assemble(voxels, 3, peer_ids, region_ids, halo_ids)
        voxels = advect_leaves(voxels, speeds, picked)
        sign_field = voxels / jnp.sqrt(voxels * voxels + 1.0)
        for redist_pass in range(REDIST_PASSES):
            picked = assemble(voxels, 1, peer_ids, region_ids, halo_ids)
            voxels = relax_leaves(voxels, sign_field, picked)
    return voxels.reshape(512, count)


def solution(mesh):
    return jax.shard_map(
        per_device,
        mesh=mesh,
        in_specs=(
            P(None, ("group", "dev")),
            P(None, ("group", "dev")),
            P(("group", "dev"), None),
            P(("group", "dev"), None),
            P(None, ("group", "dev")),
        ),
        out_specs=P(None, ("group", "dev")),
        check_vma=False,
    )
```

```python
import jax
import jax.numpy as jnp
from jax import lax
from jax.experimental import pallas as pl
from jax.experimental.pallas import tpu as pltpu
from jax.sharding import PartitionSpec as P

OFFSET_STEPS = 2
REDIST_PASSES = 2


advect_scale = 0.3
relax_scale = 0.3
weno_floor = 1e-06


def with_halo(block, sides, width):
    for axis, dim in sides:
        count = lax.axis_size(axis)
        forward = [(i, i + 1) for i in range(count - 1)]
        forward.append((count - 1, 0))
        backward = [(target, source) for source, target in forward]
        low = lax.ppermute(
            lax.slice_in_dim(block, block.shape[dim] - width, None, axis=dim), axis, forward
        )
        high = lax.ppermute(lax.slice_in_dim(block, 0, width, axis=dim), axis, backward)
        block = jnp.concatenate([low, block, high], axis=dim)
    return block


def face_slabs(voxels, layers):
    count = voxels.shape[3]
    pieces = [
        voxels[:layers],
        voxels[8 - layers :],
        voxels[:, :layers],
        voxels[:, 8 - layers :],
        voxels[:, :, :layers],
        voxels[:, :, 8 - layers :],
    ]
    return jnp.concatenate([piece.reshape(64 * layers, count) for piece in pieces], axis=1)


def weno_side(first, second, third, fourth, fifth):
    guess_a = first / 3.0 - 7.0 * second / 6.0 + 11.0 * third / 6.0
    guess_b = -second / 6.0 + 5.0 * third / 6.0 + fourth / 3.0
    guess_c = third / 3.0 + 5.0 * fourth / 6.0 - fifth / 6.0
    bend_a = first - 2.0 * second + third
    tilt_a = first - 4.0 * second + 3.0 * third
    bend_b = second - 2.0 * third + fourth
    tilt_b = second - fourth
    bend_c = third - 2.0 * fourth + fifth
    tilt_c = 3.0 * third - 4.0 * fourth + fifth
    smooth_a = weno_floor + 13.0 / 12.0 * bend_a * bend_a + 0.25 * tilt_a * tilt_a
    smooth_b = weno_floor + 13.0 / 12.0 * bend_b * bend_b + 0.25 * tilt_b * tilt_b
    smooth_c = weno_floor + 13.0 / 12.0 * bend_c * bend_c + 0.25 * tilt_c * tilt_c
    weight_a = 0.1 / (smooth_a * smooth_a)
    weight_b = 0.6 / (smooth_b * smooth_b)
    weight_c = 0.3 / (smooth_c * smooth_c)
    return (weight_a * guess_a + weight_b * guess_b + weight_c * guess_c) / (
        weight_a + weight_b + weight_c
    )


def one_sided(padded, along):
    differences = jnp.diff(padded, axis=along)

    def window(lowest):
        return lax.slice_in_dim(differences, lowest, lowest + 8, axis=along)

    backward = weno_side(window(0), window(1), window(2), window(3), window(4))
    forward = weno_side(window(5), window(4), window(3), window(2), window(1))
    return (backward, forward)


def widen(voxels, picked, layers):
    count = voxels.shape[3]

    def face_part(side, extent):
        return picked[:, side, :].reshape(extent + (count,))

    along_x = jnp.concatenate(
        [face_part(0, (layers, 8, 8)), voxels, face_part(1, (layers, 8, 8))], axis=0
    )
    along_y = jnp.concatenate(
        [face_part(2, (8, layers, 8)), voxels, face_part(3, (8, layers, 8))], axis=1
    )
    along_z = jnp.concatenate(
        [face_part(4, (8, 8, layers)), voxels, face_part(5, (8, 8, layers))], axis=2
    )
    return (along_x, along_y, along_z)


def advect_leaves(voxels, speeds, picked):
    squared = jnp.zeros_like(voxels)
    for along, padded in enumerate(widen(voxels, picked, 3)):
        backward, forward = one_sided(padded, along)
        squared = squared + jnp.maximum(
            jnp.square(jnp.maximum(backward, 0.0)), jnp.square(jnp.minimum(forward, 0.0))
        )
    return voxels - advect_scale * speeds * jnp.sqrt(squared)


def relax_leaves(voxels, sign_field, picked):
    squared = jnp.zeros_like(voxels)
    for along, padded in enumerate(widen(voxels, picked, 1)):
        centre = lax.slice_in_dim(padded, 1, 9, axis=along)
        backward = centre - lax.slice_in_dim(padded, 0, 8, axis=along)
        forward = lax.slice_in_dim(padded, 2, 10, axis=along) - centre
        rising = jnp.maximum(
            jnp.square(jnp.maximum(backward, 0.0)), jnp.square(jnp.minimum(forward, 0.0))
        )
        falling = jnp.maximum(
            jnp.square(jnp.minimum(backward, 0.0)), jnp.square(jnp.maximum(forward, 0.0))
        )
        squared = squared + jnp.where(sign_field > 0.0, rising, falling)
    return voxels - relax_scale * sign_field * (jnp.sqrt(squared) - 1.0)


def far_first(me, peers):
    if peers != 64:
        return [lax.rem(me + k, peers) for k in range(1, peers)]
    moves = [
        (dz, dx, dc) for dz in range(8) for dx in range(4) for dc in range(2) if (dz, dx, dc) != (0, 0, 0)
    ]
    moves.sort(key=lambda m: -(min(m[0], 8 - m[0]) + min(m[1], 4 - m[1])))
    z, x, c = me // 8, (me // 2) % 4, me % 2
    return [
        lax.rem(z + dz, 8) * 8 + lax.rem(x + dx, 4) * 2 + lax.rem(c + dc, 2) for dz, dx, dc in moves
    ]


def exchange_kernel(
    tab_ref, idx_ref, ridx_ref, comb_ref, og_ref, bd_ref, sems
):
    peers, slots = og_ref.shape[0], og_ref.shape[1]
    local = tab_ref.shape[0]
    width = bd_ref.shape[1]
    regions = lax.axis_size("group")
    me = lax.axis_index("dev")
    region = lax.axis_index("group")
    up = lax.rem(region + 1, regions)
    down = lax.rem(region + regions - 1, regions)
    mesh_ids = pl.DeviceIdType.MESH
    arrived = local
    bordering = local + peers * slots

    keep = pltpu.make_async_copy(tab_ref, comb_ref.at[pl.ds(0, local)], sems.at[4])
    keep.start()

    barrier = pltpu.get_barrier_semaphore()

    targets = far_first(me, peers)
    for e in targets:
        pl.semaphore_signal(barrier, inc=1, device_id=(region, e), device_id_type=mesh_ids)
    pl.semaphore_signal(barrier, inc=1, device_id=(up, me), device_id_type=mesh_ids)
    pl.semaphore_signal(barrier, inc=1, device_id=(down, me), device_id_type=mesh_ids)

    for h in range(2):
        for p in range(width):
            source = ridx_ref[h * width + p]
            bd_ref[h, pl.ds(p, 1), :] = tab_ref[pl.ds(source, 1), :]

    def pack(e, carry):
        for c in range(slots):
            source = idx_ref[e * slots + c]
            og_ref[e, pl.ds(c, 1), :] = tab_ref[pl.ds(source, 1), :]
        return carry

    lax.fori_loop(0, peers, pack, 0)

    pl.semaphore_wait(barrier, peers + 1)

    pltpu.make_async_remote_copy(
        src_ref=bd_ref.at[1],
        dst_ref=comb_ref.at[pl.ds(bordering, width)],
        send_sem=sems.at[2],
        recv_sem=sems.at[3],
        device_id=(up, me),
        device_id_type=mesh_ids,
    ).start()
    pltpu.make_async_remote_copy(
        src_ref=bd_ref.at[0],
        dst_ref=comb_ref.at[pl.ds(bordering + width, width)],
        send_sem=sems.at[2],
        recv_sem=sems.at[3],
        device_id=(down, me),
        device_id_type=mesh_ids,
    ).start()

    mine = pl.ds(pl.multiple_of(arrived + me * slots, slots), slots)

    for e in targets:
        pltpu.make_async_remote_copy(
            src_ref=og_ref.at[e],
            dst_ref=comb_ref.at[mine],
            send_sem=sems.at[0],
            recv_sem=sems.at[1],
            device_id=(region, e),
            device_id_type=mesh_ids,
        ).start()
    comb_ref[mine, :] = og_ref[me]

    pltpu.make_async_copy(og_ref.at[pl.ds(0, peers - 1)], og_ref.at[pl.ds(0, peers - 1)], sems.at[0]).wait()
    pltpu.make_async_copy(bd_ref, bd_ref, sems.at[2]).wait()
    pltpu.make_async_copy(og_ref.at[pl.ds(0, peers - 1)], og_ref.at[pl.ds(0, peers - 1)], sems.at[1]).wait()
    pltpu.make_async_copy(bd_ref, bd_ref, sems.at[3]).wait()
    keep.wait()


def exchange(table, peer_ids, region_ids, peers, layers):
    local, slab_rows = table.shape
    slots = peer_ids.shape[0] // peers
    width = region_ids.shape[0] // 2
    vmem = pl.BlockSpec(memory_space=pltpu.VMEM)
    smem = pl.BlockSpec(memory_space=pltpu.SMEM)
    return pl.pallas_call(
        exchange_kernel,
        out_shape=(pltpu.VMEM if layers == 1 else jax.ShapeDtypeStruct)(
            (local + peers * slots + 2 * width, slab_rows), table.dtype
        ),
        in_specs=[vmem, smem, smem],
        out_specs=vmem,
        scratch_shapes=[
            pltpu.VMEM((peers, slots, slab_rows), table.dtype),
            pltpu.VMEM((2, width, slab_rows), table.dtype),
            pltpu.SemaphoreType.DMA((5,)),
        ],
        compiler_params=pltpu.CompilerParams(collective_id=layers, has_side_effects=True),
    )(pltpu.with_memory_space_constraint(table, pltpu.VMEM), peer_ids, region_ids)


def assemble(voxels, layers, peer_ids, region_ids, halo_ids):
    slab_table = face_slabs(voxels, layers)
    peers = lax.axis_size("dev")
    combined = exchange(slab_table.T, peer_ids, region_ids, peers, layers).T
    picked = combined.at[:, halo_ids].get(mode="promise_in_bounds")
    return picked


def per_device(level_set, speed, peer_slabs, region_slabs, halo_source):
    count = level_set.shape[1]
    local = 6 * count
    peer_ids = jnp.clip(peer_slabs.reshape(-1), 0, local - 1)
    region_ids = jnp.clip(region_slabs.reshape(-1), 0, local - 1)
    halo_ids = jnp.clip(halo_source, 0, local + peer_ids.shape[0] + region_ids.shape[0] - 1)
    voxels = level_set.reshape(8, 8, 8, count)
    speeds = speed.reshape(8, 8, 8, count)
    for offset_step in range(OFFSET_STEPS):
        picked = assemble(voxels, 3, peer_ids, region_ids, halo_ids)
        voxels = advect_leaves(voxels, speeds, picked)
        sign_field = voxels / jnp.sqrt(voxels * voxels + 1.0)
        for redist_pass in range(REDIST_PASSES):
            picked = assemble(voxels, 1, peer_ids, region_ids, halo_ids)
            voxels = relax_leaves(voxels, sign_field, picked)
    return voxels.reshape(512, count)


def solution(mesh):
    return jax.shard_map(
        per_device,
        mesh=mesh,
        in_specs=(
            P(None, ("group", "dev")),
            P(None, ("group", "dev")),
            P(("group", "dev"), None),
            P(("group", "dev"), None),
            P(None, ("group", "dev")),
        ),
        out_specs=P(None, ("group", "dev")),
        check_vma=False,
    )
```

```python
import jax
import jax.numpy as jnp
from jax import lax
from jax.experimental import pallas as pl
from jax.experimental.pallas import tpu as pltpu
from jax.sharding import PartitionSpec as P

OFFSET_STEPS = 2
REDIST_PASSES = 2


advect_scale = 0.3
relax_scale = 0.3
weno_floor = 1e-06


def with_halo(block, sides, width):
    for axis, dim in sides:
        count = lax.axis_size(axis)
        forward = [(i, i + 1) for i in range(count - 1)]
        forward.append((count - 1, 0))
        backward = [(target, source) for source, target in forward]
        low = lax.ppermute(
            lax.slice_in_dim(block, block.shape[dim] - width, None, axis=dim), axis, forward
        )
        high = lax.ppermute(lax.slice_in_dim(block, 0, width, axis=dim), axis, backward)
        block = jnp.concatenate([low, block, high], axis=dim)
    return block


def face_slabs(voxels, layers):
    count = voxels.shape[3]
    pieces = [
        voxels[:layers],
        voxels[8 - layers :],
        voxels[:, :layers],
        voxels[:, 8 - layers :],
        voxels[:, :, :layers],
        voxels[:, :, 8 - layers :],
    ]
    return jnp.concatenate([piece.reshape(64 * layers, count) for piece in pieces], axis=1)


def weno_side(first, second, third, fourth, fifth):
    guess_a = first / 3.0 - 7.0 * second / 6.0 + 11.0 * third / 6.0
    guess_b = -second / 6.0 + 5.0 * third / 6.0 + fourth / 3.0
    guess_c = third / 3.0 + 5.0 * fourth / 6.0 - fifth / 6.0
    bend_a = first - 2.0 * second + third
    tilt_a = first - 4.0 * second + 3.0 * third
    bend_b = second - 2.0 * third + fourth
    tilt_b = second - fourth
    bend_c = third - 2.0 * fourth + fifth
    tilt_c = 3.0 * third - 4.0 * fourth + fifth
    smooth_a = weno_floor + 13.0 / 12.0 * bend_a * bend_a + 0.25 * tilt_a * tilt_a
    smooth_b = weno_floor + 13.0 / 12.0 * bend_b * bend_b + 0.25 * tilt_b * tilt_b
    smooth_c = weno_floor + 13.0 / 12.0 * bend_c * bend_c + 0.25 * tilt_c * tilt_c
    square_a = smooth_a * smooth_a
    square_b = smooth_b * smooth_b
    square_c = smooth_c * smooth_c
    weight_a = 0.1 * (square_b * square_c)
    weight_b = 0.6 * (square_a * square_c)
    weight_c = 0.3 * (square_a * square_b)
    return (weight_a * guess_a + weight_b * guess_b + weight_c * guess_c) / (
        weight_a + weight_b + weight_c
    )


def one_sided(padded, along):
    differences = jnp.diff(padded, axis=along)

    def window(lowest):
        return lax.slice_in_dim(differences, lowest, lowest + 8, axis=along)

    backward = weno_side(window(0), window(1), window(2), window(3), window(4))
    forward = weno_side(window(5), window(4), window(3), window(2), window(1))
    return (backward, forward)


def widen(voxels, picked, layers):
    count = voxels.shape[3]

    def face_part(side, extent):
        return picked[:, side, :].reshape(extent + (count,))

    along_x = jnp.concatenate(
        [face_part(0, (layers, 8, 8)), voxels, face_part(1, (layers, 8, 8))], axis=0
    )
    along_y = jnp.concatenate(
        [face_part(2, (8, layers, 8)), voxels, face_part(3, (8, layers, 8))], axis=1
    )
    along_z = jnp.concatenate(
        [face_part(4, (8, 8, layers)), voxels, face_part(5, (8, 8, layers))], axis=2
    )
    return (along_x, along_y, along_z)


def advect_leaves(voxels, speeds, picked):
    squared = jnp.zeros_like(voxels)
    for along, padded in enumerate(widen(voxels, picked, 3)):
        backward, forward = one_sided(padded, along)
        squared = squared + jnp.maximum(
            jnp.square(jnp.maximum(backward, 0.0)), jnp.square(jnp.minimum(forward, 0.0))
        )
    return voxels - advect_scale * speeds * jnp.sqrt(squared)


def relax_leaves(voxels, sign_field, picked):
    squared = jnp.zeros_like(voxels)
    for along, padded in enumerate(widen(voxels, picked, 1)):
        centre = lax.slice_in_dim(padded, 1, 9, axis=along)
        backward = centre - lax.slice_in_dim(padded, 0, 8, axis=along)
        forward = lax.slice_in_dim(padded, 2, 10, axis=along) - centre
        rising = jnp.maximum(
            jnp.square(jnp.maximum(backward, 0.0)), jnp.square(jnp.minimum(forward, 0.0))
        )
        falling = jnp.maximum(
            jnp.square(jnp.minimum(backward, 0.0)), jnp.square(jnp.maximum(forward, 0.0))
        )
        squared = squared + jnp.where(sign_field > 0.0, rising, falling)
    return voxels - relax_scale * sign_field * (jnp.sqrt(squared) - 1.0)


def far_first(me, peers):
    if peers != 64:
        return [lax.rem(me + k, peers) for k in range(1, peers)]
    moves = [
        (dz, dx, dc) for dz in range(8) for dx in range(4) for dc in range(2) if (dz, dx, dc) != (0, 0, 0)
    ]
    moves.sort(key=lambda m: -(min(m[0], 8 - m[0]) + min(m[1], 4 - m[1])))
    z, x, c = me // 8, (me // 2) % 4, me % 2
    return [
        lax.rem(z + dz, 8) * 8 + lax.rem(x + dx, 4) * 2 + lax.rem(c + dc, 2) for dz, dx, dc in moves
    ]


def exchange_kernel(
    tab_ref, idx_ref, ridx_ref, comb_ref, og_ref, bd_ref, sems
):
    peers, slots = og_ref.shape[0], og_ref.shape[1]
    local = tab_ref.shape[0]
    width = bd_ref.shape[1]
    regions = lax.axis_size("group")
    me = lax.axis_index("dev")
    region = lax.axis_index("group")
    up = lax.rem(region + 1, regions)
    down = lax.rem(region + regions - 1, regions)
    mesh_ids = pl.DeviceIdType.MESH
    arrived = local
    bordering = local + peers * slots

    keep = pltpu.make_async_copy(tab_ref, comb_ref.at[pl.ds(0, local)], sems.at[4])
    keep.start()

    barrier = pltpu.get_barrier_semaphore()

    targets = far_first(me, peers)
    for e in targets:
        pl.semaphore_signal(barrier, inc=1, device_id=(region, e), device_id_type=mesh_ids)
    pl.semaphore_signal(barrier, inc=1, device_id=(up, me), device_id_type=mesh_ids)
    pl.semaphore_signal(barrier, inc=1, device_id=(down, me), device_id_type=mesh_ids)

    for h in range(2):
        for p in range(width):
            source = ridx_ref[h * width + p]
            bd_ref[h, pl.ds(p, 1), :] = tab_ref[pl.ds(source, 1), :]

    def pack(e, carry):
        for c in range(slots):
            source = idx_ref[e * slots + c]
            og_ref[e, pl.ds(c, 1), :] = tab_ref[pl.ds(source, 1), :]
        return carry

    lax.fori_loop(0, peers, pack, 0)

    pl.semaphore_wait(barrier, peers + 1)

    pltpu.make_async_remote_copy(
        src_ref=bd_ref.at[1],
        dst_ref=comb_ref.at[pl.ds(bordering, width)],
        send_sem=sems.at[2],
        recv_sem=sems.at[3],
        device_id=(up, me),
        device_id_type=mesh_ids,
    ).start()
    pltpu.make_async_remote_copy(
        src_ref=bd_ref.at[0],
        dst_ref=comb_ref.at[pl.ds(bordering + width, width)],
        send_sem=sems.at[2],
        recv_sem=sems.at[3],
        device_id=(down, me),
        device_id_type=mesh_ids,
    ).start()

    mine = pl.ds(pl.multiple_of(arrived + me * slots, slots), slots)

    for e in targets:
        pltpu.make_async_remote_copy(
            src_ref=og_ref.at[e],
            dst_ref=comb_ref.at[mine],
            send_sem=sems.at[0],
            recv_sem=sems.at[1],
            device_id=(region, e),
            device_id_type=mesh_ids,
        ).start()
    comb_ref[mine, :] = og_ref[me]

    pltpu.make_async_copy(og_ref.at[pl.ds(0, peers - 1)], og_ref.at[pl.ds(0, peers - 1)], sems.at[0]).wait()
    pltpu.make_async_copy(bd_ref, bd_ref, sems.at[2]).wait()
    pltpu.make_async_copy(og_ref.at[pl.ds(0, peers - 1)], og_ref.at[pl.ds(0, peers - 1)], sems.at[1]).wait()
    pltpu.make_async_copy(bd_ref, bd_ref, sems.at[3]).wait()
    keep.wait()


def exchange(table, peer_ids, region_ids, peers, layers):
    local, slab_rows = table.shape
    slots = peer_ids.shape[0] // peers
    width = region_ids.shape[0] // 2
    vmem = pl.BlockSpec(memory_space=pltpu.VMEM)
    smem = pl.BlockSpec(memory_space=pltpu.SMEM)
    return pl.pallas_call(
        exchange_kernel,
        out_shape=(pltpu.VMEM if layers == 1 else jax.ShapeDtypeStruct)(
            (local + peers * slots + 2 * width, slab_rows), table.dtype
        ),
        in_specs=[vmem, smem, smem],
        out_specs=vmem,
        scratch_shapes=[
            pltpu.VMEM((peers, slots, slab_rows), table.dtype),
            pltpu.VMEM((2, width, slab_rows), table.dtype),
            pltpu.SemaphoreType.DMA((5,)),
        ],
        compiler_params=pltpu.CompilerParams(collective_id=layers, has_side_effects=True),
    )(pltpu.with_memory_space_constraint(table, pltpu.VMEM), peer_ids, region_ids)


def assemble(voxels, layers, peer_ids, region_ids, halo_ids):
    slab_table = face_slabs(voxels, layers)
    peers = lax.axis_size("dev")
    combined = exchange(slab_table.T, peer_ids, region_ids, peers, layers).T
    picked = combined.at[:, halo_ids].get(mode="promise_in_bounds")
    return picked


def per_device(level_set, speed, peer_slabs, region_slabs, halo_source):
    count = level_set.shape[1]
    local = 6 * count
    peer_ids = jnp.clip(peer_slabs.reshape(-1), 0, local - 1)
    region_ids = jnp.clip(region_slabs.reshape(-1), 0, local - 1)
    halo_ids = jnp.clip(halo_source, 0, local + peer_ids.shape[0] + region_ids.shape[0] - 1)
    voxels = level_set.reshape(8, 8, 8, count)
    speeds = speed.reshape(8, 8, 8, count)
    for offset_step in range(OFFSET_STEPS):
        picked = assemble(voxels, 3, peer_ids, region_ids, halo_ids)
        voxels = advect_leaves(voxels, lax.optimization_barrier(speeds), picked)
        sign_field = voxels / jnp.sqrt(voxels * voxels + 1.0)
        for redist_pass in range(REDIST_PASSES):
            picked = assemble(voxels, 1, peer_ids, region_ids, halo_ids)
            voxels = relax_leaves(voxels, sign_field, picked)
    return voxels.reshape(512, count)


def solution(mesh):
    return jax.shard_map(
        per_device,
        mesh=mesh,
        in_specs=(
            P(None, ("group", "dev")),
            P(None, ("group", "dev")),
            P(("group", "dev"), None),
            P(("group", "dev"), None),
            P(None, ("group", "dev")),
        ),
        out_specs=P(None, ("group", "dev")),
        check_vma=False,
    )
```

```python
import jax
import jax.numpy as jnp
from jax import lax
from jax.experimental import pallas as pl
from jax.experimental.pallas import tpu as pltpu
from jax.sharding import PartitionSpec as P

OFFSET_STEPS = 2
REDIST_PASSES = 2


advect_scale = 0.3
relax_scale = 0.3
weno_floor = 1e-06


def with_halo(block, sides, width):
    for axis, dim in sides:
        count = lax.axis_size(axis)
        forward = [(i, i + 1) for i in range(count - 1)]
        forward.append((count - 1, 0))
        backward = [(target, source) for source, target in forward]
        low = lax.ppermute(
            lax.slice_in_dim(block, block.shape[dim] - width, None, axis=dim), axis, forward
        )
        high = lax.ppermute(lax.slice_in_dim(block, 0, width, axis=dim), axis, backward)
        block = jnp.concatenate([low, block, high], axis=dim)
    return block


def face_slabs(voxels, layers):
    count = voxels.shape[3]
    pieces = [
        voxels[:layers],
        voxels[8 - layers :],
        voxels[:, :layers],
        voxels[:, 8 - layers :],
        voxels[:, :, :layers],
        voxels[:, :, 8 - layers :],
    ]
    return jnp.concatenate([piece.reshape(64 * layers, count) for piece in pieces], axis=1)


def weno_side(first, second, third, fourth, fifth):
    guess_a = first / 3.0 - 7.0 * second / 6.0 + 11.0 * third / 6.0
    guess_b = -second / 6.0 + 5.0 * third / 6.0 + fourth / 3.0
    guess_c = third / 3.0 + 5.0 * fourth / 6.0 - fifth / 6.0
    bend_a = first - 2.0 * second + third
    tilt_a = first - 4.0 * second + 3.0 * third
    bend_b = second - 2.0 * third + fourth
    tilt_b = second - fourth
    bend_c = third - 2.0 * fourth + fifth
    tilt_c = 3.0 * third - 4.0 * fourth + fifth
    smooth_a = weno_floor + 13.0 / 12.0 * bend_a * bend_a + 0.25 * tilt_a * tilt_a
    smooth_b = weno_floor + 13.0 / 12.0 * bend_b * bend_b + 0.25 * tilt_b * tilt_b
    smooth_c = weno_floor + 13.0 / 12.0 * bend_c * bend_c + 0.25 * tilt_c * tilt_c
    square_a = smooth_a * smooth_a
    square_b = smooth_b * smooth_b
    square_c = smooth_c * smooth_c
    weight_a = 0.1 * (square_b * square_c)
    weight_b = 0.6 * (square_a * square_c)
    weight_c = 0.3 * (square_a * square_b)
    return (weight_a * guess_a + weight_b * guess_b + weight_c * guess_c) / (
        weight_a + weight_b + weight_c
    )


def one_sided(padded, along):
    differences = jnp.diff(padded, axis=along)

    def window(lowest):
        return lax.slice_in_dim(differences, lowest, lowest + 8, axis=along)

    backward = weno_side(window(0), window(1), window(2), window(3), window(4))
    forward = weno_side(window(5), window(4), window(3), window(2), window(1))
    return (backward, forward)


def widen(voxels, picked, layers):
    count = voxels.shape[3]

    def face_part(side, extent):
        return picked[:, side, :].reshape(extent + (count,))

    along_x = jnp.concatenate(
        [face_part(0, (layers, 8, 8)), voxels, face_part(1, (layers, 8, 8))], axis=0
    )
    along_y = jnp.concatenate(
        [face_part(2, (8, layers, 8)), voxels, face_part(3, (8, layers, 8))], axis=1
    )
    along_z = jnp.concatenate(
        [face_part(4, (8, 8, layers)), voxels, face_part(5, (8, 8, layers))], axis=2
    )
    return (along_x, along_y, along_z)


def advect_leaves(voxels, speeds, picked):
    squared = jnp.zeros_like(voxels)
    for along, padded in enumerate(widen(voxels, picked, 3)):
        backward, forward = one_sided(padded, along)
        squared = squared + jnp.maximum(
            jnp.square(jnp.maximum(backward, 0.0)), jnp.square(jnp.minimum(forward, 0.0))
        )
    return voxels - advect_scale * speeds * jnp.sqrt(squared)


def relax_leaves(voxels, sign_field, picked):
    squared = jnp.zeros_like(voxels)
    for along, padded in enumerate(widen(voxels, picked, 1)):
        centre = lax.slice_in_dim(padded, 1, 9, axis=along)
        backward = centre - lax.slice_in_dim(padded, 0, 8, axis=along)
        forward = lax.slice_in_dim(padded, 2, 10, axis=along) - centre
        rising = jnp.maximum(
            jnp.square(jnp.maximum(backward, 0.0)), jnp.square(jnp.minimum(forward, 0.0))
        )
        falling = jnp.maximum(
            jnp.square(jnp.minimum(backward, 0.0)), jnp.square(jnp.maximum(forward, 0.0))
        )
        squared = squared + jnp.where(sign_field > 0.0, rising, falling)
    return voxels - relax_scale * sign_field * (jnp.sqrt(squared) - 1.0)


def far_first(me, peers):
    if peers != 64:
        return [lax.rem(me + k, peers) for k in range(1, peers)]
    moves = [
        (dz, dx, dc) for dz in range(8) for dx in range(4) for dc in range(2) if (dz, dx, dc) != (0, 0, 0)
    ]
    moves.sort(key=lambda m: -(min(m[0], 8 - m[0]) + min(m[1], 4 - m[1])))
    z, x, c = me // 8, (me // 2) % 4, me % 2
    return [
        lax.rem(z + dz, 8) * 8 + lax.rem(x + dx, 4) * 2 + lax.rem(c + dc, 2) for dz, dx, dc in moves
    ]


def exchange_kernel(
    tab_ref, idx_ref, ridx_ref, comb_ref, og_ref, bd_ref, sems, *paired
):
    peers, slots = og_ref.shape[0], og_ref.shape[1]
    slab_rows = tab_ref.shape[1]
    half = slots // 2
    local = tab_ref.shape[0]
    width = bd_ref.shape[1]
    regions = lax.axis_size("group")
    me = lax.axis_index("dev")
    region = lax.axis_index("group")
    up = lax.rem(region + 1, regions)
    down = lax.rem(region + regions - 1, regions)
    mesh_ids = pl.DeviceIdType.MESH
    arrived = local
    bordering = local + peers * slots

    keep = pltpu.make_async_copy(tab_ref, comb_ref.at[pl.ds(0, local)], sems.at[4])
    keep.start()

    barrier = pltpu.get_barrier_semaphore()

    targets = far_first(me, peers)
    for e in targets:
        pl.semaphore_signal(barrier, inc=1, device_id=(region, e), device_id_type=mesh_ids)
    pl.semaphore_signal(barrier, inc=1, device_id=(up, me), device_id_type=mesh_ids)
    pl.semaphore_signal(barrier, inc=1, device_id=(down, me), device_id_type=mesh_ids)

    for h in range(2):
        for p in range(width):
            source = ridx_ref[h * width + p]
            bd_ref[h, pl.ds(p, 1), :] = tab_ref[pl.ds(source, 1), :]

    def pack(e, carry):
        for c in range(slots):
            source = idx_ref[e * slots + c]
            og_ref[e, pl.ds(c, 1), pl.ds(0, slab_rows)] = tab_ref[pl.ds(source, 1), :]
        return carry

    lax.fori_loop(0, peers, pack, 0)

    if paired:
        dense_ref, recv_ref = paired
        lanes = lax.broadcasted_iota(jnp.int32, (half, 2 * slab_rows), 1)

        def pair(e, carry):
            low = og_ref[e, pl.ds(0, half), :]
            high = og_ref[e, pl.ds(half, half), :]
            dense_ref[e] = jnp.where(lanes < slab_rows, low, pltpu.roll(high, slab_rows, 1))
            return carry

        lax.fori_loop(0, peers, pair, 0)
        out_ref, in_ref = dense_ref, recv_ref
    else:
        out_ref, in_ref = og_ref, None

    pl.semaphore_wait(barrier, peers + 1)

    pltpu.make_async_remote_copy(
        src_ref=bd_ref.at[1],
        dst_ref=comb_ref.at[pl.ds(bordering, width)],
        send_sem=sems.at[2],
        recv_sem=sems.at[3],
        device_id=(up, me),
        device_id_type=mesh_ids,
    ).start()
    pltpu.make_async_remote_copy(
        src_ref=bd_ref.at[0],
        dst_ref=comb_ref.at[pl.ds(bordering + width, width)],
        send_sem=sems.at[2],
        recv_sem=sems.at[3],
        device_id=(down, me),
        device_id_type=mesh_ids,
    ).start()

    mine = pl.ds(pl.multiple_of(arrived + me * slots, slots), slots)

    for e in targets:
        pltpu.make_async_remote_copy(
            src_ref=out_ref.at[e],
            dst_ref=comb_ref.at[mine] if in_ref is None else in_ref.at[me],
            send_sem=sems.at[0],
            recv_sem=sems.at[1],
            device_id=(region, e),
            device_id_type=mesh_ids,
        ).start()
    if in_ref is None:
        comb_ref[mine, :] = og_ref[me]
    else:
        in_ref[me] = out_ref[me]

    pltpu.make_async_copy(out_ref.at[pl.ds(0, peers - 1)], out_ref.at[pl.ds(0, peers - 1)], sems.at[0]).wait()
    pltpu.make_async_copy(bd_ref, bd_ref, sems.at[2]).wait()
    pltpu.make_async_copy(out_ref.at[pl.ds(0, peers - 1)], out_ref.at[pl.ds(0, peers - 1)], sems.at[1]).wait()
    pltpu.make_async_copy(bd_ref, bd_ref, sems.at[3]).wait()

    if in_ref is not None:

        def unpair(e, carry):
            block = in_ref[e]
            turned = pltpu.roll(block, slab_rows, 1)
            rows = jnp.concatenate([block[:, :slab_rows], turned[:, :slab_rows]], axis=0)
            comb_ref[pl.ds(pl.multiple_of(arrived + e * slots, slots), slots), :] = rows
            return carry

        lax.fori_loop(0, peers, unpair, 0)
    keep.wait()


def exchange(table, peer_ids, region_ids, peers, layers):
    local, slab_rows = table.shape
    slots = peer_ids.shape[0] // peers
    width = region_ids.shape[0] // 2
    vmem = pl.BlockSpec(memory_space=pltpu.VMEM)
    smem = pl.BlockSpec(memory_space=pltpu.SMEM)
    paired = slab_rows == 64 and slots % 2 == 0
    return pl.pallas_call(
        exchange_kernel,
        out_shape=(pltpu.VMEM if layers == 1 else jax.ShapeDtypeStruct)(
            (local + peers * slots + 2 * width, slab_rows), table.dtype
        ),
        in_specs=[vmem, smem, smem],
        out_specs=vmem,
        scratch_shapes=[
            pltpu.VMEM((peers, slots, 2 * slab_rows if paired else slab_rows), table.dtype),
            pltpu.VMEM((2, width, slab_rows), table.dtype),
            pltpu.SemaphoreType.DMA((5,)),
        ]
        + (
            [pltpu.VMEM((peers, slots // 2, 2 * slab_rows), table.dtype)] * 2
            if paired
            else []
        ),
        compiler_params=pltpu.CompilerParams(collective_id=layers, has_side_effects=True),
    )(pltpu.with_memory_space_constraint(table, pltpu.VMEM), peer_ids, region_ids)


def assemble(voxels, layers, peer_ids, region_ids, halo_ids):
    slab_table = face_slabs(voxels, layers)
    peers = lax.axis_size("dev")
    combined = exchange(slab_table.T, peer_ids, region_ids, peers, layers).T
    picked = combined.at[:, halo_ids].get(mode="promise_in_bounds")
    return picked


def per_device(level_set, speed, peer_slabs, region_slabs, halo_source):
    count = level_set.shape[1]
    local = 6 * count
    peer_ids = jnp.clip(peer_slabs.reshape(-1), 0, local - 1)
    region_ids = jnp.clip(region_slabs.reshape(-1), 0, local - 1)
    halo_ids = jnp.clip(halo_source, 0, local + peer_ids.shape[0] + region_ids.shape[0] - 1)
    voxels = level_set.reshape(8, 8, 8, count)
    speeds = speed.reshape(8, 8, 8, count)
    for offset_step in range(OFFSET_STEPS):
        picked = assemble(voxels, 3, peer_ids, region_ids, halo_ids)
        voxels = advect_leaves(voxels, lax.optimization_barrier(speeds), picked)
        sign_field = voxels / jnp.sqrt(voxels * voxels + 1.0)
        for redist_pass in range(REDIST_PASSES):
            picked = assemble(voxels, 1, peer_ids, region_ids, halo_ids)
            voxels = relax_leaves(voxels, sign_field, picked)
    return voxels.reshape(512, count)


def solution(mesh):
    return jax.shard_map(
        per_device,
        mesh=mesh,
        in_specs=(
            P(None, ("group", "dev")),
            P(None, ("group", "dev")),
            P(("group", "dev"), None),
            P(("group", "dev"), None),
            P(None, ("group", "dev")),
        ),
        out_specs=P(None, ("group", "dev")),
        check_vma=False,
    )
```

```python
import jax
import jax.numpy as jnp
from jax import lax
from jax.experimental import pallas as pl
from jax.experimental.pallas import tpu as pltpu
from jax.sharding import PartitionSpec as P

OFFSET_STEPS = 2
REDIST_PASSES = 2


advect_scale = 0.3
relax_scale = 0.3
weno_floor = 1e-06


def with_halo(block, sides, width):
    for axis, dim in sides:
        count = lax.axis_size(axis)
        forward = [(i, i + 1) for i in range(count - 1)]
        forward.append((count - 1, 0))
        backward = [(target, source) for source, target in forward]
        low = lax.ppermute(
            lax.slice_in_dim(block, block.shape[dim] - width, None, axis=dim), axis, forward
        )
        high = lax.ppermute(lax.slice_in_dim(block, 0, width, axis=dim), axis, backward)
        block = jnp.concatenate([low, block, high], axis=dim)
    return block


def face_slabs(voxels, layers):
    count = voxels.shape[3]
    pieces = [
        voxels[:layers],
        voxels[8 - layers :],
        voxels[:, :layers],
        voxels[:, 8 - layers :],
        voxels[:, :, :layers],
        voxels[:, :, 8 - layers :],
    ]
    return jnp.concatenate([piece.reshape(64 * layers, count) for piece in pieces], axis=1)


def weno_side(first, second, third, fourth, fifth):
    guess_a = first / 3.0 - 7.0 * second / 6.0 + 11.0 * third / 6.0
    guess_b = -second / 6.0 + 5.0 * third / 6.0 + fourth / 3.0
    guess_c = third / 3.0 + 5.0 * fourth / 6.0 - fifth / 6.0
    bend_a = first - 2.0 * second + third
    tilt_a = first - 4.0 * second + 3.0 * third
    bend_b = second - 2.0 * third + fourth
    tilt_b = second - fourth
    bend_c = third - 2.0 * fourth + fifth
    tilt_c = 3.0 * third - 4.0 * fourth + fifth
    smooth_a = weno_floor + 13.0 / 12.0 * bend_a * bend_a + 0.25 * tilt_a * tilt_a
    smooth_b = weno_floor + 13.0 / 12.0 * bend_b * bend_b + 0.25 * tilt_b * tilt_b
    smooth_c = weno_floor + 13.0 / 12.0 * bend_c * bend_c + 0.25 * tilt_c * tilt_c
    square_a = smooth_a * smooth_a
    square_b = smooth_b * smooth_b
    square_c = smooth_c * smooth_c
    weight_a = 0.1 * (square_b * square_c)
    weight_b = 0.6 * (square_a * square_c)
    weight_c = 0.3 * (square_a * square_b)
    return (weight_a * guess_a + weight_b * guess_b + weight_c * guess_c) / (
        weight_a + weight_b + weight_c
    )


def one_sided(padded, along):
    differences = jnp.diff(padded, axis=along)

    def window(lowest):
        return lax.slice_in_dim(differences, lowest, lowest + 8, axis=along)

    backward = weno_side(window(0), window(1), window(2), window(3), window(4))
    forward = weno_side(window(5), window(4), window(3), window(2), window(1))
    return (backward, forward)


def widen(voxels, picked, layers):
    count = voxels.shape[3]

    def face_part(side, extent):
        return picked[:, side, :].reshape(extent + (count,))

    along_x = jnp.concatenate(
        [face_part(0, (layers, 8, 8)), voxels, face_part(1, (layers, 8, 8))], axis=0
    )
    along_y = jnp.concatenate(
        [face_part(2, (8, layers, 8)), voxels, face_part(3, (8, layers, 8))], axis=1
    )
    along_z = jnp.concatenate(
        [face_part(4, (8, 8, layers)), voxels, face_part(5, (8, 8, layers))], axis=2
    )
    return (along_x, along_y, along_z)


def advect_leaves(voxels, speeds, picked):
    squared = jnp.zeros_like(voxels)
    for along, padded in enumerate(widen(voxels, picked, 3)):
        backward, forward = one_sided(padded, along)
        squared = squared + jnp.maximum(
            jnp.square(jnp.maximum(backward, 0.0)), jnp.square(jnp.minimum(forward, 0.0))
        )
    return voxels - advect_scale * speeds * jnp.sqrt(squared)


def relax_leaves(voxels, sign_field, picked):
    squared = jnp.zeros_like(voxels)
    for along, padded in enumerate(widen(voxels, picked, 1)):
        centre = lax.slice_in_dim(padded, 1, 9, axis=along)
        backward = centre - lax.slice_in_dim(padded, 0, 8, axis=along)
        forward = lax.slice_in_dim(padded, 2, 10, axis=along) - centre
        rising = jnp.maximum(
            jnp.square(jnp.maximum(backward, 0.0)), jnp.square(jnp.minimum(forward, 0.0))
        )
        falling = jnp.maximum(
            jnp.square(jnp.minimum(backward, 0.0)), jnp.square(jnp.maximum(forward, 0.0))
        )
        squared = squared + jnp.where(sign_field > 0.0, rising, falling)
    return voxels - relax_scale * sign_field * (jnp.sqrt(squared) - 1.0)


def far_first(me, peers):
    if peers != 64:
        return [lax.rem(me + k, peers) for k in range(1, peers)]
    moves = [
        (dz, dx, dc) for dz in range(8) for dx in range(4) for dc in range(2) if (dz, dx, dc) != (0, 0, 0)
    ]
    moves.sort(key=lambda m: -(min(m[0], 8 - m[0]) + min(m[1], 4 - m[1])))
    z, x, c = me // 8, (me // 2) % 4, me % 2
    return [
        lax.rem(z + dz, 8) * 8 + lax.rem(x + dx, 4) * 2 + lax.rem(c + dc, 2) for dz, dx, dc in moves
    ]


def exchange_kernel(
    tab_ref, idx_ref, ridx_ref, comb_ref, og_ref, bd_ref, sems
):
    peers, slots = og_ref.shape[0], og_ref.shape[1]
    local = tab_ref.shape[0]
    width = bd_ref.shape[1]
    regions = lax.axis_size("group")
    me = lax.axis_index("dev")
    region = lax.axis_index("group")
    up = lax.rem(region + 1, regions)
    down = lax.rem(region + regions - 1, regions)
    mesh_ids = pl.DeviceIdType.MESH
    arrived = local
    bordering = local + peers * slots

    keep = pltpu.make_async_copy(tab_ref, comb_ref.at[pl.ds(0, local)], sems.at[4])
    keep.start()

    barrier = pltpu.get_barrier_semaphore()

    targets = far_first(me, peers)
    for e in targets:
        pl.semaphore_signal(barrier, inc=1, device_id=(region, e), device_id_type=mesh_ids)
    pl.semaphore_signal(barrier, inc=1, device_id=(up, me), device_id_type=mesh_ids)
    pl.semaphore_signal(barrier, inc=1, device_id=(down, me), device_id_type=mesh_ids)

    for h in range(2):
        for p in range(width):
            source = ridx_ref[h * width + p]
            bd_ref[h, pl.ds(p, 1), :] = tab_ref[pl.ds(source, 1), :]

    def pack(e, carry):
        for c in range(slots):
            source = idx_ref[e * slots + c]
            og_ref[e, pl.ds(c, 1), :] = tab_ref[pl.ds(source, 1), :]
        return carry

    lax.fori_loop(0, peers, pack, 0)

    pl.semaphore_wait(barrier, peers + 1)

    pltpu.make_async_remote_copy(
        src_ref=bd_ref.at[1],
        dst_ref=comb_ref.at[pl.ds(bordering, width)],
        send_sem=sems.at[2],
        recv_sem=sems.at[3],
        device_id=(up, me),
        device_id_type=mesh_ids,
    ).start()
    pltpu.make_async_remote_copy(
        src_ref=bd_ref.at[0],
        dst_ref=comb_ref.at[pl.ds(bordering + width, width)],
        send_sem=sems.at[2],
        recv_sem=sems.at[3],
        device_id=(down, me),
        device_id_type=mesh_ids,
    ).start()

    mine = pl.ds(pl.multiple_of(arrived + me * slots, slots), slots)

    for e in targets:
        pltpu.make_async_remote_copy(
            src_ref=og_ref.at[e],
            dst_ref=comb_ref.at[mine],
            send_sem=sems.at[0],
            recv_sem=sems.at[1],
            device_id=(region, e),
            device_id_type=mesh_ids,
        ).start()
    comb_ref[mine, :] = og_ref[me]

    pltpu.make_async_copy(og_ref.at[pl.ds(0, peers - 1)], og_ref.at[pl.ds(0, peers - 1)], sems.at[0]).wait()
    pltpu.make_async_copy(bd_ref, bd_ref, sems.at[2]).wait()
    pltpu.make_async_copy(og_ref.at[pl.ds(0, peers - 1)], og_ref.at[pl.ds(0, peers - 1)], sems.at[1]).wait()
    pltpu.make_async_copy(bd_ref, bd_ref, sems.at[3]).wait()
    keep.wait()


def exchange(table, peer_ids, region_ids, peers, layers):
    local, slab_rows = table.shape
    slots = peer_ids.shape[0] // peers
    width = region_ids.shape[0] // 2
    vmem = pl.BlockSpec(memory_space=pltpu.VMEM)
    smem = pl.BlockSpec(memory_space=pltpu.SMEM)
    return pl.pallas_call(
        exchange_kernel,
        out_shape=(pltpu.VMEM if layers == 1 else jax.ShapeDtypeStruct)(
            (local + peers * slots + 2 * width, slab_rows), table.dtype
        ),
        in_specs=[vmem, smem, smem],
        out_specs=vmem,
        scratch_shapes=[
            pltpu.VMEM((peers, slots, slab_rows), table.dtype),
            pltpu.VMEM((2, width, slab_rows), table.dtype),
            pltpu.SemaphoreType.DMA((5,)),
        ],
        compiler_params=pltpu.CompilerParams(collective_id=layers, has_side_effects=True),
    )(pltpu.with_memory_space_constraint(table, pltpu.VMEM), peer_ids, region_ids)


def paired_kernel(tab_ref, idx_ref, ridx_ref, comb_ref, og_ref, bd_ref, sems):
    peers, half, lane_count = og_ref.shape
    slots = 2 * half
    slab_rows = lane_count // 2
    local = tab_ref.shape[0]
    width = bd_ref.shape[1]
    regions = lax.axis_size("group")
    me = lax.axis_index("dev")
    region = lax.axis_index("group")
    up = lax.rem(region + 1, regions)
    down = lax.rem(region + regions - 1, regions)
    mesh_ids = pl.DeviceIdType.MESH
    bordering = local + peers * half

    keep = pltpu.make_async_copy(tab_ref, comb_ref.at[pl.ds(0, local)], sems.at[4])
    keep.start()

    barrier = pltpu.get_barrier_semaphore()
    targets = far_first(me, peers)
    for e in targets:
        pl.semaphore_signal(barrier, inc=1, device_id=(region, e), device_id_type=mesh_ids)
    pl.semaphore_signal(barrier, inc=1, device_id=(up, me), device_id_type=mesh_ids)
    pl.semaphore_signal(barrier, inc=1, device_id=(down, me), device_id_type=mesh_ids)

    for h in range(2):
        for p in range(width):
            source = ridx_ref[h * width + p]
            bd_ref[h, pl.ds(p, 1), :] = tab_ref[pl.ds(source, 1), :]

    lanes = lax.broadcasted_iota(jnp.int32, (1, lane_count), 1)

    def pack(e, carry):
        for r in range(half):
            first = tab_ref[pl.ds(idx_ref[e * slots + r], 1), :]
            second = tab_ref[pl.ds(idx_ref[e * slots + r + half], 1), :]
            og_ref[e, pl.ds(r, 1), :] = jnp.where(lanes < slab_rows, first, second)
        return carry

    lax.fori_loop(0, peers, pack, 0)

    pl.semaphore_wait(barrier, peers + 1)

    pltpu.make_async_remote_copy(
        src_ref=bd_ref.at[1],
        dst_ref=comb_ref.at[pl.ds(bordering, width)],
        send_sem=sems.at[2],
        recv_sem=sems.at[3],
        device_id=(up, me),
        device_id_type=mesh_ids,
    ).start()
    pltpu.make_async_remote_copy(
        src_ref=bd_ref.at[0],
        dst_ref=comb_ref.at[pl.ds(bordering + width, width)],
        send_sem=sems.at[2],
        recv_sem=sems.at[3],
        device_id=(down, me),
        device_id_type=mesh_ids,
    ).start()

    mine = pl.ds(local + me * half, half)
    for e in targets:
        pltpu.make_async_remote_copy(
            src_ref=og_ref.at[e],
            dst_ref=comb_ref.at[mine],
            send_sem=sems.at[0],
            recv_sem=sems.at[1],
            device_id=(region, e),
            device_id_type=mesh_ids,
        ).start()
    pltpu.make_async_copy(og_ref.at[me], comb_ref.at[mine], sems.at[1]).start()

    pltpu.make_async_copy(og_ref.at[pl.ds(0, peers - 1)], og_ref.at[pl.ds(0, peers - 1)], sems.at[0]).wait()
    pltpu.make_async_copy(bd_ref, bd_ref, sems.at[2]).wait()
    pltpu.make_async_copy(og_ref, og_ref, sems.at[1]).wait()
    pltpu.make_async_copy(bd_ref, bd_ref, sems.at[3]).wait()
    keep.wait()


def paired_exchange(table, peer_ids, region_ids, peers):
    local, slab_rows = table.shape
    slots = peer_ids.shape[0] // peers
    width = region_ids.shape[0] // 2
    doubled = jnp.concatenate([table, table], axis=1)
    vmem = pl.BlockSpec(memory_space=pltpu.VMEM)
    smem = pl.BlockSpec(memory_space=pltpu.SMEM)
    return pl.pallas_call(
        paired_kernel,
        out_shape=pltpu.VMEM((local + peers * slots // 2 + 2 * width, 2 * slab_rows), table.dtype),
        in_specs=[vmem, smem, smem],
        out_specs=vmem,
        scratch_shapes=[
            pltpu.VMEM((peers, slots // 2, 2 * slab_rows), table.dtype),
            pltpu.VMEM((2, width, 2 * slab_rows), table.dtype),
            pltpu.SemaphoreType.DMA((5,)),
        ],
        compiler_params=pltpu.CompilerParams(collective_id=2, has_side_effects=True),
    )(pltpu.with_memory_space_constraint(doubled, pltpu.VMEM), peer_ids, region_ids)


def paired_sources(halo_ids, local, peers, slots, width):
    half = slots // 2
    entry = halo_ids - local
    slot = entry % slots
    from_peer = (entry >= 0) & (entry < peers * slots)
    from_region = entry >= peers * slots
    row = jnp.where(
        from_peer,
        local + (entry // slots) * half + slot % half,
        jnp.where(from_region, halo_ids - peers * half, halo_ids),
    )
    upper = from_peer & (slot >= half)
    return row, upper


def assemble(voxels, layers, peer_ids, region_ids, halo_ids, paired_ids):
    slab_table = face_slabs(voxels, layers)
    peers = lax.axis_size("dev")
    if layers == 1 and paired_ids is not None:
        rows, upper = paired_ids
        table = paired_exchange(slab_table.T, peer_ids, region_ids, peers)
        lines = table.at[rows].get(mode="promise_in_bounds")
        width = slab_table.shape[0]
        chosen = jnp.where(upper[..., None], lines[..., width:], lines[..., :width])
        return jnp.moveaxis(chosen, 2, 0)
    combined = exchange(slab_table.T, peer_ids, region_ids, peers, layers).T
    picked = combined.at[:, halo_ids].get(mode="promise_in_bounds")
    return picked


def per_device(level_set, speed, peer_slabs, region_slabs, halo_source):
    count = level_set.shape[1]
    local = 6 * count
    peer_ids = jnp.clip(peer_slabs.reshape(-1), 0, local - 1)
    region_ids = jnp.clip(region_slabs.reshape(-1), 0, local - 1)
    halo_ids = jnp.clip(halo_source, 0, local + peer_ids.shape[0] + region_ids.shape[0] - 1)
    peers = lax.axis_size("dev")
    slots = peer_ids.shape[0] // peers
    paired_ids = None
    if slots % 2 == 0:
        paired_ids = paired_sources(halo_ids, local, peers, slots, region_ids.shape[0] // 2)
    voxels = level_set.reshape(8, 8, 8, count)
    speeds = speed.reshape(8, 8, 8, count)
    for offset_step in range(OFFSET_STEPS):
        picked = assemble(voxels, 3, peer_ids, region_ids, halo_ids, paired_ids)
        voxels = advect_leaves(voxels, lax.optimization_barrier(speeds), picked)
        sign_field = voxels / jnp.sqrt(voxels * voxels + 1.0)
        for redist_pass in range(REDIST_PASSES):
            picked = assemble(voxels, 1, peer_ids, region_ids, halo_ids, paired_ids)
            voxels = relax_leaves(voxels, sign_field, picked)
    return voxels.reshape(512, count)


def solution(mesh):
    return jax.shard_map(
        per_device,
        mesh=mesh,
        in_specs=(
            P(None, ("group", "dev")),
            P(None, ("group", "dev")),
            P(("group", "dev"), None),
            P(("group", "dev"), None),
            P(None, ("group", "dev")),
        ),
        out_specs=P(None, ("group", "dev")),
        check_vma=False,
    )
```

```python
import jax
import jax.numpy as jnp
from jax import lax
from jax.experimental import pallas as pl
from jax.experimental.pallas import tpu as pltpu
from jax.sharding import PartitionSpec as P

OFFSET_STEPS = 2
REDIST_PASSES = 2


advect_scale = 0.3
relax_scale = 0.3
weno_floor = 1e-06


def with_halo(block, sides, width):
    for axis, dim in sides:
        count = lax.axis_size(axis)
        forward = [(i, i + 1) for i in range(count - 1)]
        forward.append((count - 1, 0))
        backward = [(target, source) for source, target in forward]
        low = lax.ppermute(
            lax.slice_in_dim(block, block.shape[dim] - width, None, axis=dim), axis, forward
        )
        high = lax.ppermute(lax.slice_in_dim(block, 0, width, axis=dim), axis, backward)
        block = jnp.concatenate([low, block, high], axis=dim)
    return block


def face_slabs(voxels, layers):
    count = voxels.shape[3]
    pieces = [
        voxels[:layers],
        voxels[8 - layers :],
        voxels[:, :layers],
        voxels[:, 8 - layers :],
        voxels[:, :, :layers],
        voxels[:, :, 8 - layers :],
    ]
    return jnp.concatenate([piece.reshape(64 * layers, count) for piece in pieces], axis=1)


def weno_side(first, second, third, fourth, fifth):
    guess_a = first / 3.0 - 7.0 * second / 6.0 + 11.0 * third / 6.0
    guess_b = -second / 6.0 + 5.0 * third / 6.0 + fourth / 3.0
    guess_c = third / 3.0 + 5.0 * fourth / 6.0 - fifth / 6.0
    bend_a = first - 2.0 * second + third
    tilt_a = first - 4.0 * second + 3.0 * third
    bend_b = second - 2.0 * third + fourth
    tilt_b = second - fourth
    bend_c = third - 2.0 * fourth + fifth
    tilt_c = 3.0 * third - 4.0 * fourth + fifth
    smooth_a = weno_floor + 13.0 / 12.0 * bend_a * bend_a + 0.25 * tilt_a * tilt_a
    smooth_b = weno_floor + 13.0 / 12.0 * bend_b * bend_b + 0.25 * tilt_b * tilt_b
    smooth_c = weno_floor + 13.0 / 12.0 * bend_c * bend_c + 0.25 * tilt_c * tilt_c
    square_a = smooth_a * smooth_a
    square_b = smooth_b * smooth_b
    square_c = smooth_c * smooth_c
    weight_a = 0.1 * (square_b * square_c)
    weight_b = 0.6 * (square_a * square_c)
    weight_c = 0.3 * (square_a * square_b)
    return (weight_a * guess_a + weight_b * guess_b + weight_c * guess_c) / (
        weight_a + weight_b + weight_c
    )


def one_sided(padded, along):
    differences = jnp.diff(padded, axis=along)

    def window(lowest):
        return lax.slice_in_dim(differences, lowest, lowest + 8, axis=along)

    backward = weno_side(window(0), window(1), window(2), window(3), window(4))
    forward = weno_side(window(5), window(4), window(3), window(2), window(1))
    return (backward, forward)


def widen(voxels, picked, layers):
    count = voxels.shape[3]

    def face_part(side, extent):
        return picked[:, side, :].reshape(extent + (count,))

    along_x = jnp.concatenate(
        [face_part(0, (layers, 8, 8)), voxels, face_part(1, (layers, 8, 8))], axis=0
    )
    along_y = jnp.concatenate(
        [face_part(2, (8, layers, 8)), voxels, face_part(3, (8, layers, 8))], axis=1
    )
    along_z = jnp.concatenate(
        [face_part(4, (8, 8, layers)), voxels, face_part(5, (8, 8, layers))], axis=2
    )
    return (along_x, along_y, along_z)


def advect_leaves(voxels, speeds, picked):
    squared = jnp.zeros_like(voxels)
    for along, padded in enumerate(widen(voxels, picked, 3)):
        backward, forward = one_sided(padded, along)
        squared = squared + jnp.maximum(
            jnp.square(jnp.maximum(backward, 0.0)), jnp.square(jnp.minimum(forward, 0.0))
        )
    return voxels - advect_scale * speeds * jnp.sqrt(squared)


def relax_leaves(voxels, sign_field, picked):
    squared = jnp.zeros_like(voxels)
    for along, padded in enumerate(widen(voxels, picked, 1)):
        centre = lax.slice_in_dim(padded, 1, 9, axis=along)
        backward = centre - lax.slice_in_dim(padded, 0, 8, axis=along)
        forward = lax.slice_in_dim(padded, 2, 10, axis=along) - centre
        rising = jnp.maximum(
            jnp.square(jnp.maximum(backward, 0.0)), jnp.square(jnp.minimum(forward, 0.0))
        )
        falling = jnp.maximum(
            jnp.square(jnp.minimum(backward, 0.0)), jnp.square(jnp.maximum(forward, 0.0))
        )
        squared = squared + jnp.where(sign_field > 0.0, rising, falling)
    return voxels - relax_scale * sign_field * (jnp.sqrt(squared) - 1.0)


def far_first(me, peers):
    if peers != 64:
        return [lax.rem(me + k, peers) for k in range(1, peers)]
    moves = [
        (dz, dx, dc) for dz in range(8) for dx in range(4) for dc in range(2) if (dz, dx, dc) != (0, 0, 0)
    ]
    moves.sort(key=lambda m: -(min(m[0], 8 - m[0]) + min(m[1], 4 - m[1])))
    z, x, c = me // 8, (me // 2) % 4, me % 2
    return [
        lax.rem(z + dz, 8) * 8 + lax.rem(x + dx, 4) * 2 + lax.rem(c + dc, 2) for dz, dx, dc in moves
    ]


def exchange_kernel(
    tab_ref, idx_ref, ridx_ref, comb_ref, og_ref, bd_ref, sems
):
    peers, slots = og_ref.shape[0], og_ref.shape[1]
    local = tab_ref.shape[0]
    width = bd_ref.shape[1]
    regions = lax.axis_size("group")
    me = lax.axis_index("dev")
    region = lax.axis_index("group")
    up = lax.rem(region + 1, regions)
    down = lax.rem(region + regions - 1, regions)
    mesh_ids = pl.DeviceIdType.MESH
    arrived = local
    bordering = local + peers * slots

    keep = pltpu.make_async_copy(tab_ref, comb_ref.at[pl.ds(0, local)], sems.at[4])
    keep.start()

    barrier = pltpu.get_barrier_semaphore()

    targets = far_first(me, peers)
    for e in targets:
        pl.semaphore_signal(barrier, inc=1, device_id=(region, e), device_id_type=mesh_ids)
    pl.semaphore_signal(barrier, inc=1, device_id=(up, me), device_id_type=mesh_ids)
    pl.semaphore_signal(barrier, inc=1, device_id=(down, me), device_id_type=mesh_ids)

    for h in range(2):
        for p in range(width):
            source = ridx_ref[h * width + p]
            bd_ref[h, pl.ds(p, 1), :] = tab_ref[pl.ds(source, 1), :]

    def pack(e, carry):
        for c in range(slots):
            source = idx_ref[e * slots + c]
            og_ref[e, pl.ds(c, 1), :] = tab_ref[pl.ds(source, 1), :]
        return carry

    lax.fori_loop(0, peers, pack, 0)

    pl.semaphore_wait(barrier, peers + 1)


    mine = pl.ds(pl.multiple_of(arrived + me * slots, slots), slots)

    for e in targets:
        pltpu.make_async_remote_copy(
            src_ref=og_ref.at[e],
            dst_ref=comb_ref.at[mine],
            send_sem=sems.at[0],
            recv_sem=sems.at[1],
            device_id=(region, e),
            device_id_type=mesh_ids,
        ).start()
    comb_ref[mine, :] = og_ref[me]

    pltpu.make_async_remote_copy(
        src_ref=bd_ref.at[1],
        dst_ref=comb_ref.at[pl.ds(bordering, width)],
        send_sem=sems.at[2],
        recv_sem=sems.at[3],
        device_id=(up, me),
        device_id_type=mesh_ids,
    ).start()
    pltpu.make_async_remote_copy(
        src_ref=bd_ref.at[0],
        dst_ref=comb_ref.at[pl.ds(bordering + width, width)],
        send_sem=sems.at[2],
        recv_sem=sems.at[3],
        device_id=(down, me),
        device_id_type=mesh_ids,
    ).start()

    pltpu.make_async_copy(og_ref.at[pl.ds(0, peers - 1)], og_ref.at[pl.ds(0, peers - 1)], sems.at[0]).wait()
    pltpu.make_async_copy(bd_ref, bd_ref, sems.at[2]).wait()
    pltpu.make_async_copy(og_ref.at[pl.ds(0, peers - 1)], og_ref.at[pl.ds(0, peers - 1)], sems.at[1]).wait()
    pltpu.make_async_copy(bd_ref, bd_ref, sems.at[3]).wait()
    keep.wait()


def exchange(table, peer_ids, region_ids, peers, layers):
    local, slab_rows = table.shape
    slots = peer_ids.shape[0] // peers
    width = region_ids.shape[0] // 2
    vmem = pl.BlockSpec(memory_space=pltpu.VMEM)
    smem = pl.BlockSpec(memory_space=pltpu.SMEM)
    return pl.pallas_call(
        exchange_kernel,
        out_shape=(pltpu.VMEM if layers == 1 else jax.ShapeDtypeStruct)(
            (local + peers * slots + 2 * width, slab_rows), table.dtype
        ),
        in_specs=[vmem, smem, smem],
        out_specs=vmem,
        scratch_shapes=[
            pltpu.VMEM((peers, slots, slab_rows), table.dtype),
            pltpu.VMEM((2, width, slab_rows), table.dtype),
            pltpu.SemaphoreType.DMA((5,)),
        ],
        compiler_params=pltpu.CompilerParams(collective_id=layers, has_side_effects=True),
    )(pltpu.with_memory_space_constraint(table, pltpu.VMEM), peer_ids, region_ids)


def paired_kernel(tab_ref, idx_ref, ridx_ref, comb_ref, og_ref, bd_ref, sems):
    peers, half, lane_count = og_ref.shape
    slots = 2 * half
    slab_rows = lane_count // 2
    local = tab_ref.shape[0]
    width = bd_ref.shape[1]
    regions = lax.axis_size("group")
    me = lax.axis_index("dev")
    region = lax.axis_index("group")
    up = lax.rem(region + 1, regions)
    down = lax.rem(region + regions - 1, regions)
    mesh_ids = pl.DeviceIdType.MESH
    bordering = local + peers * half

    keep = pltpu.make_async_copy(tab_ref, comb_ref.at[pl.ds(0, local)], sems.at[4])
    keep.start()

    barrier = pltpu.get_barrier_semaphore()
    targets = far_first(me, peers)
    for e in targets:
        pl.semaphore_signal(barrier, inc=1, device_id=(region, e), device_id_type=mesh_ids)
    pl.semaphore_signal(barrier, inc=1, device_id=(up, me), device_id_type=mesh_ids)
    pl.semaphore_signal(barrier, inc=1, device_id=(down, me), device_id_type=mesh_ids)

    for h in range(2):
        for p in range(width):
            source = ridx_ref[h * width + p]
            bd_ref[h, pl.ds(p, 1), :] = tab_ref[pl.ds(source, 1), :]

    lanes = lax.broadcasted_iota(jnp.int32, (1, lane_count), 1)

    def pack(e, carry):
        for r in range(half):
            first = tab_ref[pl.ds(idx_ref[e * slots + r], 1), :]
            second = tab_ref[pl.ds(idx_ref[e * slots + r + half], 1), :]
            og_ref[e, pl.ds(r, 1), :] = jnp.where(lanes < slab_rows, first, second)
        return carry

    lax.fori_loop(0, peers, pack, 0)

    pl.semaphore_wait(barrier, peers + 1)


    mine = pl.ds(local + me * half, half)
    for e in targets:
        pltpu.make_async_remote_copy(
            src_ref=og_ref.at[e],
            dst_ref=comb_ref.at[mine],
            send_sem=sems.at[0],
            recv_sem=sems.at[1],
            device_id=(region, e),
            device_id_type=mesh_ids,
        ).start()
    pltpu.make_async_copy(og_ref.at[me], comb_ref.at[mine], sems.at[1]).start()

    pltpu.make_async_remote_copy(
        src_ref=bd_ref.at[1],
        dst_ref=comb_ref.at[pl.ds(bordering, width)],
        send_sem=sems.at[2],
        recv_sem=sems.at[3],
        device_id=(up, me),
        device_id_type=mesh_ids,
    ).start()
    pltpu.make_async_remote_copy(
        src_ref=bd_ref.at[0],
        dst_ref=comb_ref.at[pl.ds(bordering + width, width)],
        send_sem=sems.at[2],
        recv_sem=sems.at[3],
        device_id=(down, me),
        device_id_type=mesh_ids,
    ).start()

    pltpu.make_async_copy(og_ref.at[pl.ds(0, peers - 1)], og_ref.at[pl.ds(0, peers - 1)], sems.at[0]).wait()
    pltpu.make_async_copy(bd_ref, bd_ref, sems.at[2]).wait()
    pltpu.make_async_copy(og_ref, og_ref, sems.at[1]).wait()
    pltpu.make_async_copy(bd_ref, bd_ref, sems.at[3]).wait()
    keep.wait()


def paired_exchange(table, peer_ids, region_ids, peers):
    local, slab_rows = table.shape
    slots = peer_ids.shape[0] // peers
    width = region_ids.shape[0] // 2
    doubled = jnp.concatenate([table, table], axis=1)
    vmem = pl.BlockSpec(memory_space=pltpu.VMEM)
    smem = pl.BlockSpec(memory_space=pltpu.SMEM)
    return pl.pallas_call(
        paired_kernel,
        out_shape=pltpu.VMEM((local + peers * slots // 2 + 2 * width, 2 * slab_rows), table.dtype),
        in_specs=[vmem, smem, smem],
        out_specs=vmem,
        scratch_shapes=[
            pltpu.VMEM((peers, slots // 2, 2 * slab_rows), table.dtype),
            pltpu.VMEM((2, width, 2 * slab_rows), table.dtype),
            pltpu.SemaphoreType.DMA((5,)),
        ],
        compiler_params=pltpu.CompilerParams(collective_id=2, has_side_effects=True),
    )(pltpu.with_memory_space_constraint(doubled, pltpu.VMEM), peer_ids, region_ids)


def paired_sources(halo_ids, local, peers, slots, width):
    half = slots // 2
    entry = halo_ids - local
    slot = entry % slots
    from_peer = (entry >= 0) & (entry < peers * slots)
    from_region = entry >= peers * slots
    row = jnp.where(
        from_peer,
        local + (entry // slots) * half + slot % half,
        jnp.where(from_region, halo_ids - peers * half, halo_ids),
    )
    upper = from_peer & (slot >= half)
    return row, upper


def assemble(voxels, layers, peer_ids, region_ids, halo_ids, paired_ids):
    slab_table = face_slabs(voxels, layers)
    peers = lax.axis_size("dev")
    if layers == 1 and paired_ids is not None:
        rows, upper = paired_ids
        table = paired_exchange(slab_table.T, peer_ids, region_ids, peers)
        lines = table.at[rows].get(mode="promise_in_bounds")
        width = slab_table.shape[0]
        chosen = jnp.where(upper[..., None], lines[..., width:], lines[..., :width])
        return jnp.moveaxis(chosen, 2, 0)
    combined = exchange(slab_table.T, peer_ids, region_ids, peers, layers).T
    picked = combined.at[:, halo_ids].get(mode="promise_in_bounds")
    return picked


def per_device(level_set, speed, peer_slabs, region_slabs, halo_source):
    count = level_set.shape[1]
    local = 6 * count
    peer_ids = jnp.clip(peer_slabs.reshape(-1), 0, local - 1)
    region_ids = jnp.clip(region_slabs.reshape(-1), 0, local - 1)
    halo_ids = jnp.clip(halo_source, 0, local + peer_ids.shape[0] + region_ids.shape[0] - 1)
    peers = lax.axis_size("dev")
    slots = peer_ids.shape[0] // peers
    paired_ids = None
    if slots % 2 == 0:
        paired_ids = paired_sources(halo_ids, local, peers, slots, region_ids.shape[0] // 2)
    voxels = level_set.reshape(8, 8, 8, count)
    speeds = speed.reshape(8, 8, 8, count)
    for offset_step in range(OFFSET_STEPS):
        picked = assemble(voxels, 3, peer_ids, region_ids, halo_ids, paired_ids)
        voxels = advect_leaves(voxels, lax.optimization_barrier(speeds), picked)
        sign_field = voxels / jnp.sqrt(voxels * voxels + 1.0)
        for redist_pass in range(REDIST_PASSES):
            picked = assemble(voxels, 1, peer_ids, region_ids, halo_ids, paired_ids)
            voxels = relax_leaves(voxels, sign_field, picked)
    return voxels.reshape(512, count)


def solution(mesh):
    return jax.shard_map(
        per_device,
        mesh=mesh,
        in_specs=(
            P(None, ("group", "dev")),
            P(None, ("group", "dev")),
            P(("group", "dev"), None),
            P(("group", "dev"), None),
            P(None, ("group", "dev")),
        ),
        out_specs=P(None, ("group", "dev")),
        check_vma=False,
    )
```

```python
import jax
import jax.numpy as jnp
from jax import lax
from jax.experimental import pallas as pl
from jax.experimental.pallas import tpu as pltpu
from jax.sharding import PartitionSpec as P

OFFSET_STEPS = 2
REDIST_PASSES = 2


advect_scale = 0.3
relax_scale = 0.3
weno_floor = 1e-06


def with_halo(block, sides, width):
    for axis, dim in sides:
        count = lax.axis_size(axis)
        forward = [(i, i + 1) for i in range(count - 1)]
        forward.append((count - 1, 0))
        backward = [(target, source) for source, target in forward]
        low = lax.ppermute(
            lax.slice_in_dim(block, block.shape[dim] - width, None, axis=dim), axis, forward
        )
        high = lax.ppermute(lax.slice_in_dim(block, 0, width, axis=dim), axis, backward)
        block = jnp.concatenate([low, block, high], axis=dim)
    return block


def face_slabs(voxels, layers):
    count = voxels.shape[3]
    pieces = [
        voxels[:layers],
        voxels[8 - layers :],
        voxels[:, :layers],
        voxels[:, 8 - layers :],
        voxels[:, :, :layers],
        voxels[:, :, 8 - layers :],
    ]
    return jnp.concatenate([piece.reshape(64 * layers, count) for piece in pieces], axis=1)


def weno_side(first, second, third, fourth, fifth):
    guess_a = first / 3.0 - 7.0 * second / 6.0 + 11.0 * third / 6.0
    guess_b = -second / 6.0 + 5.0 * third / 6.0 + fourth / 3.0
    guess_c = third / 3.0 + 5.0 * fourth / 6.0 - fifth / 6.0
    bend_a = first - 2.0 * second + third
    tilt_a = first - 4.0 * second + 3.0 * third
    bend_b = second - 2.0 * third + fourth
    tilt_b = second - fourth
    bend_c = third - 2.0 * fourth + fifth
    tilt_c = 3.0 * third - 4.0 * fourth + fifth
    smooth_a = weno_floor + 13.0 / 12.0 * bend_a * bend_a + 0.25 * tilt_a * tilt_a
    smooth_b = weno_floor + 13.0 / 12.0 * bend_b * bend_b + 0.25 * tilt_b * tilt_b
    smooth_c = weno_floor + 13.0 / 12.0 * bend_c * bend_c + 0.25 * tilt_c * tilt_c
    square_a = smooth_a * smooth_a
    square_b = smooth_b * smooth_b
    square_c = smooth_c * smooth_c
    weight_a = 0.1 * (square_b * square_c)
    weight_b = 0.6 * (square_a * square_c)
    weight_c = 0.3 * (square_a * square_b)
    return (weight_a * guess_a + weight_b * guess_b + weight_c * guess_c) / (
        weight_a + weight_b + weight_c
    )


def one_sided(padded, along):
    differences = jnp.diff(padded, axis=along)

    def window(lowest):
        return lax.slice_in_dim(differences, lowest, lowest + 8, axis=along)

    backward = weno_side(window(0), window(1), window(2), window(3), window(4))
    forward = weno_side(window(5), window(4), window(3), window(2), window(1))
    return (backward, forward)


def widen(voxels, picked, layers):
    count = voxels.shape[3]

    def face_part(side, extent):
        return picked[:, side, :].reshape(extent + (count,))

    along_x = jnp.concatenate(
        [face_part(0, (layers, 8, 8)), voxels, face_part(1, (layers, 8, 8))], axis=0
    )
    along_y = jnp.concatenate(
        [face_part(2, (8, layers, 8)), voxels, face_part(3, (8, layers, 8))], axis=1
    )
    along_z = jnp.concatenate(
        [face_part(4, (8, 8, layers)), voxels, face_part(5, (8, 8, layers))], axis=2
    )
    return (along_x, along_y, along_z)


def advect_leaves(voxels, speeds, picked):
    squared = jnp.zeros_like(voxels)
    for along, padded in enumerate(widen(voxels, picked, 3)):
        backward, forward = one_sided(padded, along)
        squared = squared + jnp.maximum(
            jnp.square(jnp.maximum(backward, 0.0)), jnp.square(jnp.minimum(forward, 0.0))
        )
    return voxels - advect_scale * speeds * jnp.sqrt(squared)


def relax_leaves(voxels, sign_field, picked):
    squared = jnp.zeros_like(voxels)
    for along, padded in enumerate(widen(voxels, picked, 1)):
        centre = lax.slice_in_dim(padded, 1, 9, axis=along)
        backward = centre - lax.slice_in_dim(padded, 0, 8, axis=along)
        forward = lax.slice_in_dim(padded, 2, 10, axis=along) - centre
        rising = jnp.maximum(
            jnp.square(jnp.maximum(backward, 0.0)), jnp.square(jnp.minimum(forward, 0.0))
        )
        falling = jnp.maximum(
            jnp.square(jnp.minimum(backward, 0.0)), jnp.square(jnp.maximum(forward, 0.0))
        )
        squared = squared + jnp.where(sign_field > 0.0, rising, falling)
    return voxels - relax_scale * sign_field * (jnp.sqrt(squared) - 1.0)


def far_first(me, peers):
    if peers != 64:
        return [lax.rem(me + k, peers) for k in range(1, peers)]
    moves = [
        (dz, dx, dc) for dz in range(8) for dx in range(4) for dc in range(2) if (dz, dx, dc) != (0, 0, 0)
    ]
    moves.sort(key=lambda m: -(min(m[0], 8 - m[0]) + min(m[1], 4 - m[1])))
    z, x, c = me // 8, (me // 2) % 4, me % 2
    return [
        lax.rem(z + dz, 8) * 8 + lax.rem(x + dx, 4) * 2 + lax.rem(c + dc, 2) for dz, dx, dc in moves
    ]


def exchange_kernel(
    tab_ref, idx_ref, ridx_ref, comb_ref, og_ref, bd_ref, sems
):
    peers, slots = og_ref.shape[0], og_ref.shape[1]
    local = tab_ref.shape[0]
    width = bd_ref.shape[1]
    regions = lax.axis_size("group")
    me = lax.axis_index("dev")
    region = lax.axis_index("group")
    up = lax.rem(region + 1, regions)
    down = lax.rem(region + regions - 1, regions)
    mesh_ids = pl.DeviceIdType.MESH
    arrived = local
    bordering = local + peers * slots

    keep = pltpu.make_async_copy(tab_ref, comb_ref.at[pl.ds(0, local)], sems.at[4])
    keep.start()

    barrier = pltpu.get_barrier_semaphore()

    targets = far_first(me, peers)
    for e in targets:
        pl.semaphore_signal(barrier, inc=1, device_id=(region, e), device_id_type=mesh_ids)
    pl.semaphore_signal(barrier, inc=1, device_id=(up, me), device_id_type=mesh_ids)
    pl.semaphore_signal(barrier, inc=1, device_id=(down, me), device_id_type=mesh_ids)

    for h in range(2):
        for p in range(width):
            source = ridx_ref[h * width + p]
            bd_ref[h, pl.ds(p, 1), :] = tab_ref[pl.ds(source, 1), :]

    def pack(e, carry):
        for c in range(slots):
            source = idx_ref[e * slots + c]
            og_ref[e, pl.ds(c, 1), :] = tab_ref[pl.ds(source, 1), :]
        return carry

    lax.fori_loop(0, peers, pack, 0)

    pl.semaphore_wait(barrier, peers + 1)

    pltpu.make_async_remote_copy(
        src_ref=bd_ref.at[1],
        dst_ref=comb_ref.at[pl.ds(bordering, width)],
        send_sem=sems.at[2],
        recv_sem=sems.at[3],
        device_id=(up, me),
        device_id_type=mesh_ids,
    ).start()
    pltpu.make_async_remote_copy(
        src_ref=bd_ref.at[0],
        dst_ref=comb_ref.at[pl.ds(bordering + width, width)],
        send_sem=sems.at[2],
        recv_sem=sems.at[3],
        device_id=(down, me),
        device_id_type=mesh_ids,
    ).start()

    mine = pl.ds(pl.multiple_of(arrived + me * slots, slots), slots)

    for e in targets:
        pltpu.make_async_remote_copy(
            src_ref=og_ref.at[e],
            dst_ref=comb_ref.at[mine],
            send_sem=sems.at[0],
            recv_sem=sems.at[1],
            device_id=(region, e),
            device_id_type=mesh_ids,
        ).start()
    comb_ref[mine, :] = og_ref[me]

    pltpu.make_async_copy(og_ref.at[pl.ds(0, peers - 1)], og_ref.at[pl.ds(0, peers - 1)], sems.at[0]).wait()
    pltpu.make_async_copy(bd_ref, bd_ref, sems.at[2]).wait()
    pltpu.make_async_copy(og_ref.at[pl.ds(0, peers - 1)], og_ref.at[pl.ds(0, peers - 1)], sems.at[1]).wait()
    pltpu.make_async_copy(bd_ref, bd_ref, sems.at[3]).wait()
    keep.wait()


def exchange(table, peer_ids, region_ids, peers, layers):
    local, slab_rows = table.shape
    slots = peer_ids.shape[0] // peers
    width = region_ids.shape[0] // 2
    vmem = pl.BlockSpec(memory_space=pltpu.VMEM)
    smem = pl.BlockSpec(memory_space=pltpu.SMEM)
    return pl.pallas_call(
        exchange_kernel,
        out_shape=(pltpu.VMEM if layers == 1 else jax.ShapeDtypeStruct)(
            (local + peers * slots + 2 * width, slab_rows), table.dtype
        ),
        in_specs=[vmem, smem, smem],
        out_specs=vmem,
        scratch_shapes=[
            pltpu.VMEM((peers, slots, slab_rows), table.dtype),
            pltpu.VMEM((2, width, slab_rows), table.dtype),
            pltpu.SemaphoreType.DMA((5,)),
        ],
        compiler_params=pltpu.CompilerParams(collective_id=layers, has_side_effects=True),
    )(pltpu.with_memory_space_constraint(table, pltpu.VMEM), peer_ids, region_ids)


def paired_kernel(tab_ref, idx_ref, ridx_ref, comb_ref, og_ref, bd_ref, sems):
    peers, half, lane_count = og_ref.shape
    slots = 2 * half
    slab_rows = lane_count // 2
    local = tab_ref.shape[0]
    width = bd_ref.shape[1]
    regions = lax.axis_size("group")
    me = lax.axis_index("dev")
    region = lax.axis_index("group")
    up = lax.rem(region + 1, regions)
    down = lax.rem(region + regions - 1, regions)
    mesh_ids = pl.DeviceIdType.MESH
    bordering = local + peers * half

    keep = pltpu.make_async_copy(tab_ref, comb_ref.at[pl.ds(0, local)], sems.at[4])
    keep.start()

    barrier = pltpu.get_barrier_semaphore()
    targets = far_first(me, peers)
    for e in targets:
        pl.semaphore_signal(barrier, inc=1, device_id=(region, e), device_id_type=mesh_ids)
    pl.semaphore_signal(barrier, inc=1, device_id=(up, me), device_id_type=mesh_ids)
    pl.semaphore_signal(barrier, inc=1, device_id=(down, me), device_id_type=mesh_ids)

    for h in range(2):
        for p in range(width):
            source = ridx_ref[h * width + p]
            bd_ref[h, pl.ds(p, 1), :] = tab_ref[pl.ds(source, 1), :]

    lanes = lax.broadcasted_iota(jnp.int32, (1, lane_count), 1)

    def pack(e, carry):
        for r in range(half):
            first = tab_ref[pl.ds(idx_ref[e * slots + r], 1), :]
            second = tab_ref[pl.ds(idx_ref[e * slots + r + half], 1), :]
            og_ref[e, pl.ds(r, 1), :] = jnp.where(lanes < slab_rows, first, second)
        return carry

    lax.fori_loop(0, peers, pack, 0)

    pl.semaphore_wait(barrier, peers + 1)

    pltpu.make_async_remote_copy(
        src_ref=bd_ref.at[1],
        dst_ref=comb_ref.at[pl.ds(bordering, width)],
        send_sem=sems.at[2],
        recv_sem=sems.at[3],
        device_id=(up, me),
        device_id_type=mesh_ids,
    ).start()
    pltpu.make_async_remote_copy(
        src_ref=bd_ref.at[0],
        dst_ref=comb_ref.at[pl.ds(bordering + width, width)],
        send_sem=sems.at[2],
        recv_sem=sems.at[3],
        device_id=(down, me),
        device_id_type=mesh_ids,
    ).start()

    mine = pl.ds(local + me * half, half)
    for e in targets:
        pltpu.make_async_remote_copy(
            src_ref=og_ref.at[e],
            dst_ref=comb_ref.at[mine],
            send_sem=sems.at[0],
            recv_sem=sems.at[1],
            device_id=(region, e),
            device_id_type=mesh_ids,
        ).start()
    pltpu.make_async_copy(og_ref.at[me], comb_ref.at[mine], sems.at[1]).start()

    pltpu.make_async_copy(og_ref.at[pl.ds(0, peers - 1)], og_ref.at[pl.ds(0, peers - 1)], sems.at[0]).wait()
    pltpu.make_async_copy(bd_ref, bd_ref, sems.at[2]).wait()
    pltpu.make_async_copy(og_ref, og_ref, sems.at[1]).wait()
    pltpu.make_async_copy(bd_ref, bd_ref, sems.at[3]).wait()
    keep.wait()


def paired_exchange(table, peer_ids, region_ids, peers):
    local, slab_rows = table.shape
    slots = peer_ids.shape[0] // peers
    width = region_ids.shape[0] // 2
    doubled = jnp.concatenate([table, table], axis=1)
    vmem = pl.BlockSpec(memory_space=pltpu.VMEM)
    smem = pl.BlockSpec(memory_space=pltpu.SMEM)
    return pl.pallas_call(
        paired_kernel,
        out_shape=pltpu.VMEM((local + peers * slots // 2 + 2 * width, 2 * slab_rows), table.dtype),
        in_specs=[vmem, smem, smem],
        out_specs=vmem,
        scratch_shapes=[
            pltpu.VMEM((peers, slots // 2, 2 * slab_rows), table.dtype),
            pltpu.VMEM((2, width, 2 * slab_rows), table.dtype),
            pltpu.SemaphoreType.DMA((5,)),
        ],
        compiler_params=pltpu.CompilerParams(collective_id=2, has_side_effects=True),
    )(pltpu.with_memory_space_constraint(doubled, pltpu.VMEM), peer_ids, region_ids)


def split_kernel(tab_ref, idx_ref, ridx_ref, comb_ref, og_ref, bd_ref, sems):
    peers, block_rows, lane_count = og_ref.shape
    slots = block_rows * 2 // 3
    half = slots // 2
    local = tab_ref.shape[0]
    width = bd_ref.shape[2]
    regions = lax.axis_size("group")
    me = lax.axis_index("dev")
    region = lax.axis_index("group")
    up = lax.rem(region + 1, regions)
    down = lax.rem(region + regions - 1, regions)
    mesh_ids = pl.DeviceIdType.MESH
    arrived = 2 * local
    bordering = arrived + peers * block_rows

    heads = pltpu.make_async_copy(tab_ref.at[:, pl.ds(0, lane_count)], comb_ref.at[pl.ds(0, local)], sems.at[4])
    heads.start()
    tails = pltpu.make_async_copy(
        tab_ref.at[:, pl.ds(lane_count, lane_count)], comb_ref.at[pl.ds(local, local)], sems.at[5]
    )
    tails.start()

    barrier = pltpu.get_barrier_semaphore()
    targets = far_first(me, peers)
    for e in targets:
        pl.semaphore_signal(barrier, inc=1, device_id=(region, e), device_id_type=mesh_ids)
    pl.semaphore_signal(barrier, inc=1, device_id=(up, me), device_id_type=mesh_ids)
    pl.semaphore_signal(barrier, inc=1, device_id=(down, me), device_id_type=mesh_ids)

    for h in range(2):
        for p in range(width):
            source = ridx_ref[h * width + p]
            line = tab_ref[pl.ds(source, 1), :]
            for part in range(2):
                bd_ref[h, part, pl.ds(p, 1), :] = line[:, part * lane_count : (part + 1) * lane_count]

    lanes = lax.broadcasted_iota(jnp.int32, (1, lane_count), 1)

    def pack(e, carry):
        for r in range(half):
            first = tab_ref[pl.ds(idx_ref[e * slots + r], 1), :]
            second = tab_ref[pl.ds(idx_ref[e * slots + r + half], 1), :]
            og_ref[e, pl.ds(r, 1), :] = first[:, :lane_count]
            og_ref[e, pl.ds(r + half, 1), :] = second[:, :lane_count]
            og_ref[e, pl.ds(slots + r, 1), :] = jnp.where(
                lanes < lane_count // 2, first[:, lane_count:], second[:, lane_count:]
            )
        return carry

    lax.fori_loop(0, peers, pack, 0)

    pl.semaphore_wait(barrier, peers + 1)

    mine = pl.ds(pl.multiple_of(arrived + me * block_rows, 4), block_rows)
    for e in targets:
        pltpu.make_async_remote_copy(
            src_ref=og_ref.at[e],
            dst_ref=comb_ref.at[mine],
            send_sem=sems.at[0],
            recv_sem=sems.at[1],
            device_id=(region, e),
            device_id_type=mesh_ids,
        ).start()
    pltpu.make_async_copy(og_ref.at[me], comb_ref.at[mine], sems.at[1]).start()
    for part in range(2):
        pltpu.make_async_remote_copy(
            src_ref=bd_ref.at[1, part],
            dst_ref=comb_ref.at[pl.ds(bordering + part * 2 * width, width)],
            send_sem=sems.at[2],
            recv_sem=sems.at[3],
            device_id=(up, me),
            device_id_type=mesh_ids,
        ).start()
        pltpu.make_async_remote_copy(
            src_ref=bd_ref.at[0, part],
            dst_ref=comb_ref.at[pl.ds(bordering + part * 2 * width + width, width)],
            send_sem=sems.at[2],
            recv_sem=sems.at[3],
            device_id=(down, me),
            device_id_type=mesh_ids,
        ).start()

    pltpu.make_async_copy(og_ref.at[pl.ds(0, peers - 1)], og_ref.at[pl.ds(0, peers - 1)], sems.at[0]).wait()
    pltpu.make_async_copy(bd_ref, bd_ref, sems.at[2]).wait()
    pltpu.make_async_copy(og_ref, og_ref, sems.at[1]).wait()
    pltpu.make_async_copy(bd_ref, bd_ref, sems.at[3]).wait()
    heads.wait()
    tails.wait()


def split_exchange(table, peer_ids, region_ids, peers):
    local, slab_rows = table.shape
    slots = peer_ids.shape[0] // peers
    width = region_ids.shape[0] // 2
    lane_count = 128
    widened = jnp.concatenate([table, table[:, lane_count:]], axis=1)
    vmem = pl.BlockSpec(memory_space=pltpu.VMEM)
    smem = pl.BlockSpec(memory_space=pltpu.SMEM)
    block_rows = slots + slots // 2
    return pl.pallas_call(
        split_kernel,
        out_shape=jax.ShapeDtypeStruct((2 * local + peers * block_rows + 4 * width, lane_count), table.dtype),
        in_specs=[vmem, smem, smem],
        out_specs=vmem,
        scratch_shapes=[
            pltpu.VMEM((peers, block_rows, lane_count), table.dtype),
            pltpu.VMEM((2, 2, width, lane_count), table.dtype),
            pltpu.SemaphoreType.DMA((6,)),
        ],
        compiler_params=pltpu.CompilerParams(collective_id=3, has_side_effects=True),
    )(pltpu.with_memory_space_constraint(widened, pltpu.VMEM), peer_ids, region_ids)


def split_sources(halo_ids, local, peers, slots, width):
    half = slots // 2
    block_rows = slots + half
    entry = halo_ids - local
    slot = entry % slots
    sender = entry // slots
    from_peer = (entry >= 0) & (entry < peers * slots)
    from_region = entry >= peers * slots
    place = entry - peers * slots
    base = 2 * local + peers * block_rows
    head = jnp.where(
        from_peer, 2 * local + sender * block_rows + slot, jnp.where(from_region, base + place, halo_ids)
    )
    tail = jnp.where(
        from_peer,
        2 * local + sender * block_rows + slots + slot % half,
        jnp.where(from_region, base + 2 * width + place, local + halo_ids),
    )
    upper = from_peer & (slot >= half)
    return head, tail, upper


def paired_sources(halo_ids, local, peers, slots, width):
    half = slots // 2
    entry = halo_ids - local
    slot = entry % slots
    from_peer = (entry >= 0) & (entry < peers * slots)
    from_region = entry >= peers * slots
    row = jnp.where(
        from_peer,
        local + (entry // slots) * half + slot % half,
        jnp.where(from_region, halo_ids - peers * half, halo_ids),
    )
    upper = from_peer & (slot >= half)
    return row, upper


def assemble(voxels, layers, peer_ids, region_ids, halo_ids, paired_ids, split_ids):
    slab_table = face_slabs(voxels, layers)
    peers = lax.axis_size("dev")
    if layers == 1 and paired_ids is not None:
        rows, upper = paired_ids
        table = paired_exchange(slab_table.T, peer_ids, region_ids, peers)
        lines = table.at[rows].get(mode="promise_in_bounds")
        width = slab_table.shape[0]
        chosen = jnp.where(upper[..., None], lines[..., width:], lines[..., :width])
        return jnp.moveaxis(chosen, 2, 0)
    if layers == 3 and split_ids is not None:
        head, tail, upper = split_ids
        table = split_exchange(slab_table.T, peer_ids, region_ids, peers)
        first = table.at[head].get(mode="promise_in_bounds")
        second = table.at[tail].get(mode="promise_in_bounds")
        lanes = first.shape[-1] // 2
        rest = jnp.where(upper[..., None], second[..., lanes:], second[..., :lanes])
        return jnp.moveaxis(jnp.concatenate([first, rest], axis=-1), 2, 0)
    combined = exchange(slab_table.T, peer_ids, region_ids, peers, layers).T
    picked = combined.at[:, halo_ids].get(mode="promise_in_bounds")
    return picked


def per_device(level_set, speed, peer_slabs, region_slabs, halo_source):
    count = level_set.shape[1]
    local = 6 * count
    peer_ids = jnp.clip(peer_slabs.reshape(-1), 0, local - 1)
    region_ids = jnp.clip(region_slabs.reshape(-1), 0, local - 1)
    halo_ids = jnp.clip(halo_source, 0, local + peer_ids.shape[0] + region_ids.shape[0] - 1)
    peers = lax.axis_size("dev")
    slots = peer_ids.shape[0] // peers
    paired_ids = None
    if slots % 2 == 0:
        paired_ids = paired_sources(halo_ids, local, peers, slots, region_ids.shape[0] // 2)
    split_ids = None
    if slots % 2 == 0:
        split_ids = split_sources(halo_ids, local, peers, slots, region_ids.shape[0] // 2)
    voxels = level_set.reshape(8, 8, 8, count)
    speeds = speed.reshape(8, 8, 8, count)
    for offset_step in range(OFFSET_STEPS):
        picked = assemble(voxels, 3, peer_ids, region_ids, halo_ids, paired_ids, split_ids)
        voxels = advect_leaves(voxels, lax.optimization_barrier(speeds), picked)
        sign_field = voxels / jnp.sqrt(voxels * voxels + 1.0)
        for redist_pass in range(REDIST_PASSES):
            picked = assemble(voxels, 1, peer_ids, region_ids, halo_ids, paired_ids, split_ids)
            voxels = relax_leaves(voxels, sign_field, picked)
    return voxels.reshape(512, count)


def solution(mesh):
    return jax.shard_map(
        per_device,
        mesh=mesh,
        in_specs=(
            P(None, ("group", "dev")),
            P(None, ("group", "dev")),
            P(("group", "dev"), None),
            P(("group", "dev"), None),
            P(None, ("group", "dev")),
        ),
        out_specs=P(None, ("group", "dev")),
        check_vma=False,
    )
```

```python
import jax
import jax.numpy as jnp
from jax import lax
from jax.experimental import pallas as pl
from jax.experimental.pallas import tpu as pltpu
from jax.sharding import PartitionSpec as P

OFFSET_STEPS = 2
REDIST_PASSES = 2


advect_scale = 0.3
relax_scale = 0.3
weno_floor = 1e-06


def with_halo(block, sides, width):
    for axis, dim in sides:
        count = lax.axis_size(axis)
        forward = [(i, i + 1) for i in range(count - 1)]
        forward.append((count - 1, 0))
        backward = [(target, source) for source, target in forward]
        low = lax.ppermute(
            lax.slice_in_dim(block, block.shape[dim] - width, None, axis=dim), axis, forward
        )
        high = lax.ppermute(lax.slice_in_dim(block, 0, width, axis=dim), axis, backward)
        block = jnp.concatenate([low, block, high], axis=dim)
    return block


def face_slabs(voxels, layers):
    count = voxels.shape[3]
    pieces = [
        voxels[:layers],
        voxels[8 - layers :],
        voxels[:, :layers],
        voxels[:, 8 - layers :],
        voxels[:, :, :layers],
        voxels[:, :, 8 - layers :],
    ]
    return jnp.concatenate([piece.reshape(64 * layers, count) for piece in pieces], axis=1)


def weno_side(first, second, third, fourth, fifth, smooth_a, smooth_b, smooth_c):
    guess_a = first / 3.0 - 7.0 * second / 6.0 + 11.0 * third / 6.0
    guess_b = -second / 6.0 + 5.0 * third / 6.0 + fourth / 3.0
    guess_c = third / 3.0 + 5.0 * fourth / 6.0 - fifth / 6.0
    square_a = smooth_a * smooth_a
    square_b = smooth_b * smooth_b
    square_c = smooth_c * smooth_c
    weight_a = 0.1 * (square_b * square_c)
    weight_b = 0.6 * (square_a * square_c)
    weight_c = 0.3 * (square_a * square_b)
    return (weight_a * guess_a + weight_b * guess_b + weight_c * guess_c) / (
        weight_a + weight_b + weight_c
    )


def one_sided(padded, along):
    differences = jnp.diff(padded, axis=along)
    span = differences.shape[along] - 2

    def window(lowest, size=8):
        return lax.slice_in_dim(differences, lowest, lowest + size, axis=along)

    low, mid, high = window(0, span), window(1, span), window(2, span)
    bend = low - 2.0 * mid + high
    curve = weno_floor + 13.0 / 12.0 * bend * bend
    rising = low - 4.0 * mid + 3.0 * high
    falling = 3.0 * low - 4.0 * mid + high
    central = low - high
    rising = curve + 0.25 * rising * rising
    falling = curve + 0.25 * falling * falling
    central = curve + 0.25 * central * central

    def at(values, lowest):
        return lax.slice_in_dim(values, lowest, lowest + 8, axis=along)

    backward = weno_side(
        window(0), window(1), window(2), window(3), window(4),
        at(rising, 0), at(central, 1), at(falling, 2),
    )
    forward = weno_side(
        window(5), window(4), window(3), window(2), window(1),
        at(falling, 3), at(central, 2), at(rising, 1),
    )
    return (backward, forward)


def widen(voxels, picked, layers):
    count = voxels.shape[3]

    def face_part(side, extent):
        return picked[:, side, :].reshape(extent + (count,))

    along_x = jnp.concatenate(
        [face_part(0, (layers, 8, 8)), voxels, face_part(1, (layers, 8, 8))], axis=0
    )
    along_y = jnp.concatenate(
        [face_part(2, (8, layers, 8)), voxels, face_part(3, (8, layers, 8))], axis=1
    )
    along_z = jnp.concatenate(
        [face_part(4, (8, 8, layers)), voxels, face_part(5, (8, 8, layers))], axis=2
    )
    return (along_x, along_y, along_z)


def advect_leaves(voxels, speeds, picked):
    squared = jnp.zeros_like(voxels)
    for along, padded in enumerate(widen(voxels, picked, 3)):
        backward, forward = one_sided(padded, along)
        squared = squared + jnp.maximum(
            jnp.square(jnp.maximum(backward, 0.0)), jnp.square(jnp.minimum(forward, 0.0))
        )
    return voxels - advect_scale * speeds * jnp.sqrt(squared)


def relax_leaves(voxels, sign_field, picked):
    squared = jnp.zeros_like(voxels)
    for along, padded in enumerate(widen(voxels, picked, 1)):
        centre = lax.slice_in_dim(padded, 1, 9, axis=along)
        backward = centre - lax.slice_in_dim(padded, 0, 8, axis=along)
        forward = lax.slice_in_dim(padded, 2, 10, axis=along) - centre
        rising = jnp.maximum(
            jnp.square(jnp.maximum(backward, 0.0)), jnp.square(jnp.minimum(forward, 0.0))
        )
        falling = jnp.maximum(
            jnp.square(jnp.minimum(backward, 0.0)), jnp.square(jnp.maximum(forward, 0.0))
        )
        squared = squared + jnp.where(sign_field > 0.0, rising, falling)
    return voxels - relax_scale * sign_field * (jnp.sqrt(squared) - 1.0)


def far_first(me, peers):
    if peers != 64:
        return [lax.rem(me + k, peers) for k in range(1, peers)]
    moves = [
        (dz, dx, dc) for dz in range(8) for dx in range(4) for dc in range(2) if (dz, dx, dc) != (0, 0, 0)
    ]
    moves.sort(key=lambda m: -(min(m[0], 8 - m[0]) + min(m[1], 4 - m[1])))
    z, x, c = me // 8, (me // 2) % 4, me % 2
    return [
        lax.rem(z + dz, 8) * 8 + lax.rem(x + dx, 4) * 2 + lax.rem(c + dc, 2) for dz, dx, dc in moves
    ]


def exchange_kernel(
    tab_ref, idx_ref, ridx_ref, comb_ref, og_ref, bd_ref, sems
):
    peers, slots = og_ref.shape[0], og_ref.shape[1]
    local = tab_ref.shape[0]
    width = bd_ref.shape[1]
    regions = lax.axis_size("group")
    me = lax.axis_index("dev")
    region = lax.axis_index("group")
    up = lax.rem(region + 1, regions)
    down = lax.rem(region + regions - 1, regions)
    mesh_ids = pl.DeviceIdType.MESH
    arrived = local
    bordering = local + peers * slots

    keep = pltpu.make_async_copy(tab_ref, comb_ref.at[pl.ds(0, local)], sems.at[4])
    keep.start()

    barrier = pltpu.get_barrier_semaphore()

    targets = far_first(me, peers)
    for e in targets:
        pl.semaphore_signal(barrier, inc=1, device_id=(region, e), device_id_type=mesh_ids)
    pl.semaphore_signal(barrier, inc=1, device_id=(up, me), device_id_type=mesh_ids)
    pl.semaphore_signal(barrier, inc=1, device_id=(down, me), device_id_type=mesh_ids)

    for h in range(2):
        for p in range(width):
            source = ridx_ref[h * width + p]
            bd_ref[h, pl.ds(p, 1), :] = tab_ref[pl.ds(source, 1), :]

    def pack(e, carry):
        for c in range(slots):
            source = idx_ref[e * slots + c]
            og_ref[e, pl.ds(c, 1), :] = tab_ref[pl.ds(source, 1), :]
        return carry

    lax.fori_loop(0, peers, pack, 0)

    pl.semaphore_wait(barrier, peers + 1)

    pltpu.make_async_remote_copy(
        src_ref=bd_ref.at[1],
        dst_ref=comb_ref.at[pl.ds(bordering, width)],
        send_sem=sems.at[2],
        recv_sem=sems.at[3],
        device_id=(up, me),
        device_id_type=mesh_ids,
    ).start()
    pltpu.make_async_remote_copy(
        src_ref=bd_ref.at[0],
        dst_ref=comb_ref.at[pl.ds(bordering + width, width)],
        send_sem=sems.at[2],
        recv_sem=sems.at[3],
        device_id=(down, me),
        device_id_type=mesh_ids,
    ).start()

    mine = pl.ds(pl.multiple_of(arrived + me * slots, slots), slots)

    for e in targets:
        pltpu.make_async_remote_copy(
            src_ref=og_ref.at[e],
            dst_ref=comb_ref.at[mine],
            send_sem=sems.at[0],
            recv_sem=sems.at[1],
            device_id=(region, e),
            device_id_type=mesh_ids,
        ).start()
    comb_ref[mine, :] = og_ref[me]

    pltpu.make_async_copy(og_ref.at[pl.ds(0, peers - 1)], og_ref.at[pl.ds(0, peers - 1)], sems.at[0]).wait()
    pltpu.make_async_copy(bd_ref, bd_ref, sems.at[2]).wait()
    pltpu.make_async_copy(og_ref.at[pl.ds(0, peers - 1)], og_ref.at[pl.ds(0, peers - 1)], sems.at[1]).wait()
    pltpu.make_async_copy(bd_ref, bd_ref, sems.at[3]).wait()
    keep.wait()


def exchange(table, peer_ids, region_ids, peers, layers):
    local, slab_rows = table.shape
    slots = peer_ids.shape[0] // peers
    width = region_ids.shape[0] // 2
    vmem = pl.BlockSpec(memory_space=pltpu.VMEM)
    smem = pl.BlockSpec(memory_space=pltpu.SMEM)
    return pl.pallas_call(
        exchange_kernel,
        out_shape=(pltpu.VMEM if layers == 1 else jax.ShapeDtypeStruct)(
            (local + peers * slots + 2 * width, slab_rows), table.dtype
        ),
        in_specs=[vmem, smem, smem],
        out_specs=vmem,
        scratch_shapes=[
            pltpu.VMEM((peers, slots, slab_rows), table.dtype),
            pltpu.VMEM((2, width, slab_rows), table.dtype),
            pltpu.SemaphoreType.DMA((5,)),
        ],
        compiler_params=pltpu.CompilerParams(collective_id=layers, has_side_effects=True),
    )(pltpu.with_memory_space_constraint(table, pltpu.VMEM), peer_ids, region_ids)


def paired_kernel(tab_ref, idx_ref, ridx_ref, comb_ref, og_ref, bd_ref, sems):
    peers, half, lane_count = og_ref.shape
    slots = 2 * half
    slab_rows = lane_count // 2
    local = tab_ref.shape[0]
    width = bd_ref.shape[1]
    regions = lax.axis_size("group")
    me = lax.axis_index("dev")
    region = lax.axis_index("group")
    up = lax.rem(region + 1, regions)
    down = lax.rem(region + regions - 1, regions)
    mesh_ids = pl.DeviceIdType.MESH
    bordering = local + peers * half

    keep = pltpu.make_async_copy(tab_ref, comb_ref.at[pl.ds(0, local)], sems.at[4])
    keep.start()

    barrier = pltpu.get_barrier_semaphore()
    targets = far_first(me, peers)
    for e in targets:
        pl.semaphore_signal(barrier, inc=1, device_id=(region, e), device_id_type=mesh_ids)
    pl.semaphore_signal(barrier, inc=1, device_id=(up, me), device_id_type=mesh_ids)
    pl.semaphore_signal(barrier, inc=1, device_id=(down, me), device_id_type=mesh_ids)

    for h in range(2):
        for p in range(width):
            source = ridx_ref[h * width + p]
            bd_ref[h, pl.ds(p, 1), :] = tab_ref[pl.ds(source, 1), :]

    lanes = lax.broadcasted_iota(jnp.int32, (1, lane_count), 1)

    def pack(e, carry):
        for r in range(half):
            first = tab_ref[pl.ds(idx_ref[e * slots + r], 1), :]
            second = tab_ref[pl.ds(idx_ref[e * slots + r + half], 1), :]
            og_ref[e, pl.ds(r, 1), :] = jnp.where(lanes < slab_rows, first, second)
        return carry

    lax.fori_loop(0, peers, pack, 0)

    pl.semaphore_wait(barrier, peers + 1)

    pltpu.make_async_remote_copy(
        src_ref=bd_ref.at[1],
        dst_ref=comb_ref.at[pl.ds(bordering, width)],
        send_sem=sems.at[2],
        recv_sem=sems.at[3],
        device_id=(up, me),
        device_id_type=mesh_ids,
    ).start()
    pltpu.make_async_remote_copy(
        src_ref=bd_ref.at[0],
        dst_ref=comb_ref.at[pl.ds(bordering + width, width)],
        send_sem=sems.at[2],
        recv_sem=sems.at[3],
        device_id=(down, me),
        device_id_type=mesh_ids,
    ).start()

    mine = pl.ds(local + me * half, half)
    for e in targets:
        pltpu.make_async_remote_copy(
            src_ref=og_ref.at[e],
            dst_ref=comb_ref.at[mine],
            send_sem=sems.at[0],
            recv_sem=sems.at[1],
            device_id=(region, e),
            device_id_type=mesh_ids,
        ).start()
    pltpu.make_async_copy(og_ref.at[me], comb_ref.at[mine], sems.at[1]).start()

    pltpu.make_async_copy(og_ref.at[pl.ds(0, peers - 1)], og_ref.at[pl.ds(0, peers - 1)], sems.at[0]).wait()
    pltpu.make_async_copy(bd_ref, bd_ref, sems.at[2]).wait()
    pltpu.make_async_copy(og_ref, og_ref, sems.at[1]).wait()
    pltpu.make_async_copy(bd_ref, bd_ref, sems.at[3]).wait()
    keep.wait()


def paired_exchange(table, peer_ids, region_ids, peers):
    local, slab_rows = table.shape
    slots = peer_ids.shape[0] // peers
    width = region_ids.shape[0] // 2
    doubled = jnp.concatenate([table, table], axis=1)
    vmem = pl.BlockSpec(memory_space=pltpu.VMEM)
    smem = pl.BlockSpec(memory_space=pltpu.SMEM)
    return pl.pallas_call(
        paired_kernel,
        out_shape=pltpu.VMEM((local + peers * slots // 2 + 2 * width, 2 * slab_rows), table.dtype),
        in_specs=[vmem, smem, smem],
        out_specs=vmem,
        scratch_shapes=[
            pltpu.VMEM((peers, slots // 2, 2 * slab_rows), table.dtype),
            pltpu.VMEM((2, width, 2 * slab_rows), table.dtype),
            pltpu.SemaphoreType.DMA((5,)),
        ],
        compiler_params=pltpu.CompilerParams(collective_id=2, has_side_effects=True),
    )(pltpu.with_memory_space_constraint(doubled, pltpu.VMEM), peer_ids, region_ids)


def paired_sources(halo_ids, local, peers, slots, width):
    half = slots // 2
    entry = halo_ids - local
    slot = entry % slots
    from_peer = (entry >= 0) & (entry < peers * slots)
    from_region = entry >= peers * slots
    row = jnp.where(
        from_peer,
        local + (entry // slots) * half + slot % half,
        jnp.where(from_region, halo_ids - peers * half, halo_ids),
    )
    upper = from_peer & (slot >= half)
    return row, upper


def assemble(voxels, layers, peer_ids, region_ids, halo_ids, paired_ids):
    slab_table = face_slabs(voxels, layers)
    peers = lax.axis_size("dev")
    if layers == 1 and paired_ids is not None:
        rows, upper = paired_ids
        table = paired_exchange(slab_table.T, peer_ids, region_ids, peers)
        lines = table.at[rows].get(mode="promise_in_bounds")
        width = slab_table.shape[0]
        chosen = jnp.where(upper[..., None], lines[..., width:], lines[..., :width])
        return jnp.moveaxis(chosen, 2, 0)
    combined = exchange(slab_table.T, peer_ids, region_ids, peers, layers).T
    picked = combined.at[:, halo_ids].get(mode="promise_in_bounds")
    return picked


def per_device(level_set, speed, peer_slabs, region_slabs, halo_source):
    count = level_set.shape[1]
    local = 6 * count
    peer_ids = jnp.clip(peer_slabs.reshape(-1), 0, local - 1)
    region_ids = jnp.clip(region_slabs.reshape(-1), 0, local - 1)
    halo_ids = jnp.clip(halo_source, 0, local + peer_ids.shape[0] + region_ids.shape[0] - 1)
    peers = lax.axis_size("dev")
    slots = peer_ids.shape[0] // peers
    paired_ids = None
    if slots % 2 == 0:
        paired_ids = paired_sources(halo_ids, local, peers, slots, region_ids.shape[0] // 2)
    voxels = level_set.reshape(8, 8, 8, count)
    speeds = speed.reshape(8, 8, 8, count)
    for offset_step in range(OFFSET_STEPS):
        picked = assemble(voxels, 3, peer_ids, region_ids, halo_ids, paired_ids)
        voxels = advect_leaves(voxels, lax.optimization_barrier(speeds), picked)
        sign_field = voxels / jnp.sqrt(voxels * voxels + 1.0)
        for redist_pass in range(REDIST_PASSES):
            picked = assemble(voxels, 1, peer_ids, region_ids, halo_ids, paired_ids)
            voxels = relax_leaves(voxels, sign_field, picked)
    return voxels.reshape(512, count)


def solution(mesh):
    return jax.shard_map(
        per_device,
        mesh=mesh,
        in_specs=(
            P(None, ("group", "dev")),
            P(None, ("group", "dev")),
            P(("group", "dev"), None),
            P(("group", "dev"), None),
            P(None, ("group", "dev")),
        ),
        out_specs=P(None, ("group", "dev")),
        check_vma=False,
    )
```

```python
import jax
import jax.numpy as jnp
from jax import lax
from jax.experimental import pallas as pl
from jax.experimental.pallas import tpu as pltpu
from jax.sharding import PartitionSpec as P

OFFSET_STEPS = 2
REDIST_PASSES = 2


advect_scale = 0.3
relax_scale = 0.3
weno_floor = 1e-06


def with_halo(block, sides, width):
    for axis, dim in sides:
        count = lax.axis_size(axis)
        forward = [(i, i + 1) for i in range(count - 1)]
        forward.append((count - 1, 0))
        backward = [(target, source) for source, target in forward]
        low = lax.ppermute(
            lax.slice_in_dim(block, block.shape[dim] - width, None, axis=dim), axis, forward
        )
        high = lax.ppermute(lax.slice_in_dim(block, 0, width, axis=dim), axis, backward)
        block = jnp.concatenate([low, block, high], axis=dim)
    return block


def face_slabs(voxels, layers):
    count = voxels.shape[3]
    pieces = [
        voxels[:layers],
        voxels[8 - layers :],
        voxels[:, :layers],
        voxels[:, 8 - layers :],
        voxels[:, :, :layers],
        voxels[:, :, 8 - layers :],
    ]
    return jnp.concatenate([piece.reshape(64 * layers, count) for piece in pieces], axis=1)


def weno_side(first, second, third, fourth, fifth):
    guess_a = first / 3.0 - 7.0 * second / 6.0 + 11.0 * third / 6.0
    guess_b = -second / 6.0 + 5.0 * third / 6.0 + fourth / 3.0
    guess_c = third / 3.0 + 5.0 * fourth / 6.0 - fifth / 6.0
    bend_a = first - 2.0 * second + third
    tilt_a = first - 4.0 * second + 3.0 * third
    bend_b = second - 2.0 * third + fourth
    tilt_b = second - fourth
    bend_c = third - 2.0 * fourth + fifth
    tilt_c = 3.0 * third - 4.0 * fourth + fifth
    smooth_a = weno_floor + 13.0 / 12.0 * bend_a * bend_a + 0.25 * tilt_a * tilt_a
    smooth_b = weno_floor + 13.0 / 12.0 * bend_b * bend_b + 0.25 * tilt_b * tilt_b
    smooth_c = weno_floor + 13.0 / 12.0 * bend_c * bend_c + 0.25 * tilt_c * tilt_c
    square_a = smooth_a * smooth_a
    square_b = smooth_b * smooth_b
    square_c = smooth_c * smooth_c
    weight_a = 0.1 * (square_b * square_c)
    weight_b = 0.6 * (square_a * square_c)
    weight_c = 0.3 * (square_a * square_b)
    return (weight_a * guess_a + weight_b * guess_b + weight_c * guess_c) / (
        weight_a + weight_b + weight_c
    )


def one_sided(padded, along):
    differences = jnp.diff(padded, axis=along)

    def window(lowest):
        return lax.slice_in_dim(differences, lowest, lowest + 8, axis=along)

    backward = weno_side(window(0), window(1), window(2), window(3), window(4))
    forward = weno_side(window(5), window(4), window(3), window(2), window(1))
    return (backward, forward)


def widen(voxels, picked, layers):
    count = voxels.shape[3]

    def face_part(side, extent):
        return picked[:, side, :].reshape(extent + (count,))

    along_x = jnp.concatenate(
        [face_part(0, (layers, 8, 8)), voxels, face_part(1, (layers, 8, 8))], axis=0
    )
    along_y = jnp.concatenate(
        [face_part(2, (8, layers, 8)), voxels, face_part(3, (8, layers, 8))], axis=1
    )
    along_z = jnp.concatenate(
        [face_part(4, (8, 8, layers)), voxels, face_part(5, (8, 8, layers))], axis=2
    )
    return (along_x, along_y, along_z)


def advect_leaves(voxels, speeds, picked):
    squared = jnp.zeros_like(voxels)
    for along, padded in enumerate(widen(voxels, picked, 3)):
        backward, forward = one_sided(padded, along)
        squared = squared + jnp.maximum(
            jnp.square(jnp.maximum(backward, 0.0)), jnp.square(jnp.minimum(forward, 0.0))
        )
    return voxels - advect_scale * speeds * jnp.sqrt(squared)


def relax_leaves(voxels, sign_field, picked):
    squared = jnp.zeros_like(voxels)
    for along, padded in enumerate(widen(voxels, picked, 1)):
        centre = lax.slice_in_dim(padded, 1, 9, axis=along)
        backward = centre - lax.slice_in_dim(padded, 0, 8, axis=along)
        forward = lax.slice_in_dim(padded, 2, 10, axis=along) - centre
        rising = jnp.maximum(
            jnp.square(jnp.maximum(backward, 0.0)), jnp.square(jnp.minimum(forward, 0.0))
        )
        falling = jnp.maximum(
            jnp.square(jnp.minimum(backward, 0.0)), jnp.square(jnp.maximum(forward, 0.0))
        )
        squared = squared + jnp.where(sign_field > 0.0, rising, falling)
    return voxels - relax_scale * sign_field * (jnp.sqrt(squared) - 1.0)


def far_first(me, peers):
    if peers != 64:
        return [lax.rem(me + k, peers) for k in range(1, peers)]
    moves = [
        (dz, dx, dc) for dz in range(8) for dx in range(4) for dc in range(2) if (dz, dx, dc) != (0, 0, 0)
    ]
    moves.sort(key=lambda m: -(min(m[0], 8 - m[0]) + min(m[1], 4 - m[1])))
    z, x, c = me // 8, (me // 2) % 4, me % 2
    return [
        lax.rem(z + dz, 8) * 8 + lax.rem(x + dx, 4) * 2 + lax.rem(c + dc, 2) for dz, dx, dc in moves
    ]


def exchange_kernel(
    tab_ref, idx_ref, ridx_ref, comb_ref, og_ref, bd_ref, sems
):
    peers, slots = og_ref.shape[0], og_ref.shape[1]
    local = tab_ref.shape[0]
    width = bd_ref.shape[1]
    regions = lax.axis_size("group")
    me = lax.axis_index("dev")
    region = lax.axis_index("group")
    up = lax.rem(region + 1, regions)
    down = lax.rem(region + regions - 1, regions)
    mesh_ids = pl.DeviceIdType.MESH
    arrived = local
    bordering = local + peers * slots

    keep = pltpu.make_async_copy(tab_ref, comb_ref.at[pl.ds(0, local)], sems.at[4])
    keep.start()

    barrier = pltpu.get_barrier_semaphore()

    targets = far_first(me, peers)
    for e in targets:
        pl.semaphore_signal(barrier, inc=1, device_id=(region, e), device_id_type=mesh_ids)
    pl.semaphore_signal(barrier, inc=1, device_id=(up, me), device_id_type=mesh_ids)
    pl.semaphore_signal(barrier, inc=1, device_id=(down, me), device_id_type=mesh_ids)

    for h in range(2):
        for p in range(width):
            source = ridx_ref[h * width + p]
            bd_ref[h, pl.ds(p, 1), :] = tab_ref[pl.ds(source, 1), :]

    def pack(e, carry):
        for c in range(slots):
            source = idx_ref[e * slots + c]
            og_ref[e, pl.ds(c, 1), :] = tab_ref[pl.ds(source, 1), :]
        return carry

    lax.fori_loop(0, peers, pack, 0)

    pl.semaphore_wait(barrier, peers + 1)

    pltpu.make_async_remote_copy(
        src_ref=bd_ref.at[1],
        dst_ref=comb_ref.at[pl.ds(bordering, width)],
        send_sem=sems.at[2],
        recv_sem=sems.at[3],
        device_id=(up, me),
        device_id_type=mesh_ids,
    ).start()
    pltpu.make_async_remote_copy(
        src_ref=bd_ref.at[0],
        dst_ref=comb_ref.at[pl.ds(bordering + width, width)],
        send_sem=sems.at[2],
        recv_sem=sems.at[3],
        device_id=(down, me),
        device_id_type=mesh_ids,
    ).start()

    mine = pl.ds(pl.multiple_of(arrived + me * slots, slots), slots)

    for e in targets:
        pltpu.make_async_remote_copy(
            src_ref=og_ref.at[e],
            dst_ref=comb_ref.at[mine],
            send_sem=sems.at[0],
            recv_sem=sems.at[1],
            device_id=(region, e),
            device_id_type=mesh_ids,
        ).start()
    comb_ref[mine, :] = og_ref[me]

    pltpu.make_async_copy(og_ref.at[pl.ds(0, peers - 1)], og_ref.at[pl.ds(0, peers - 1)], sems.at[0]).wait()
    pltpu.make_async_copy(bd_ref, bd_ref, sems.at[2]).wait()
    pltpu.make_async_copy(og_ref.at[pl.ds(0, peers - 1)], og_ref.at[pl.ds(0, peers - 1)], sems.at[1]).wait()
    pltpu.make_async_copy(bd_ref, bd_ref, sems.at[3]).wait()
    keep.wait()


def exchange(table, peer_ids, region_ids, peers, layers):
    local, slab_rows = table.shape
    slots = peer_ids.shape[0] // peers
    width = region_ids.shape[0] // 2
    lanes = -(-slab_rows // 128) * 128
    padded = jnp.pad(table, ((0, 0), (0, lanes - slab_rows)))
    vmem = pl.BlockSpec(memory_space=pltpu.VMEM)
    smem = pl.BlockSpec(memory_space=pltpu.SMEM)
    return pl.pallas_call(
        exchange_kernel,
        out_shape=(pltpu.VMEM if layers == 1 else jax.ShapeDtypeStruct)(
            (local + peers * slots + 2 * width, lanes), table.dtype
        ),
        in_specs=[vmem, smem, smem],
        out_specs=vmem,
        scratch_shapes=[
            pltpu.VMEM((peers, slots, lanes), table.dtype),
            pltpu.VMEM((2, width, lanes), table.dtype),
            pltpu.SemaphoreType.DMA((5,)),
        ],
        compiler_params=pltpu.CompilerParams(collective_id=layers, has_side_effects=True),
    )(pltpu.with_memory_space_constraint(padded, pltpu.VMEM), peer_ids, region_ids)


def paired_kernel(tab_ref, idx_ref, ridx_ref, comb_ref, og_ref, bd_ref, sems):
    peers, half, lane_count = og_ref.shape
    slots = 2 * half
    slab_rows = lane_count // 2
    local = tab_ref.shape[0]
    width = bd_ref.shape[1]
    regions = lax.axis_size("group")
    me = lax.axis_index("dev")
    region = lax.axis_index("group")
    up = lax.rem(region + 1, regions)
    down = lax.rem(region + regions - 1, regions)
    mesh_ids = pl.DeviceIdType.MESH
    bordering = local + peers * half

    keep = pltpu.make_async_copy(tab_ref, comb_ref.at[pl.ds(0, local)], sems.at[4])
    keep.start()

    barrier = pltpu.get_barrier_semaphore()
    targets = far_first(me, peers)
    for e in targets:
        pl.semaphore_signal(barrier, inc=1, device_id=(region, e), device_id_type=mesh_ids)
    pl.semaphore_signal(barrier, inc=1, device_id=(up, me), device_id_type=mesh_ids)
    pl.semaphore_signal(barrier, inc=1, device_id=(down, me), device_id_type=mesh_ids)

    for h in range(2):
        for p in range(width):
            source = ridx_ref[h * width + p]
            bd_ref[h, pl.ds(p, 1), :] = tab_ref[pl.ds(source, 1), :]

    lanes = lax.broadcasted_iota(jnp.int32, (1, lane_count), 1)

    def pack(e, carry):
        for r in range(half):
            first = tab_ref[pl.ds(idx_ref[e * slots + r], 1), :]
            second = tab_ref[pl.ds(idx_ref[e * slots + r + half], 1), :]
            og_ref[e, pl.ds(r, 1), :] = jnp.where(lanes < slab_rows, first, second)
        return carry

    lax.fori_loop(0, peers, pack, 0)

    pl.semaphore_wait(barrier, peers + 1)

    pltpu.make_async_remote_copy(
        src_ref=bd_ref.at[1],
        dst_ref=comb_ref.at[pl.ds(bordering, width)],
        send_sem=sems.at[2],
        recv_sem=sems.at[3],
        device_id=(up, me),
        device_id_type=mesh_ids,
    ).start()
    pltpu.make_async_remote_copy(
        src_ref=bd_ref.at[0],
        dst_ref=comb_ref.at[pl.ds(bordering + width, width)],
        send_sem=sems.at[2],
        recv_sem=sems.at[3],
        device_id=(down, me),
        device_id_type=mesh_ids,
    ).start()

    mine = pl.ds(local + me * half, half)
    for e in targets:
        pltpu.make_async_remote_copy(
            src_ref=og_ref.at[e],
            dst_ref=comb_ref.at[mine],
            send_sem=sems.at[0],
            recv_sem=sems.at[1],
            device_id=(region, e),
            device_id_type=mesh_ids,
        ).start()
    pltpu.make_async_copy(og_ref.at[me], comb_ref.at[mine], sems.at[1]).start()

    pltpu.make_async_copy(og_ref.at[pl.ds(0, peers - 1)], og_ref.at[pl.ds(0, peers - 1)], sems.at[0]).wait()
    pltpu.make_async_copy(bd_ref, bd_ref, sems.at[2]).wait()
    pltpu.make_async_copy(og_ref, og_ref, sems.at[1]).wait()
    pltpu.make_async_copy(bd_ref, bd_ref, sems.at[3]).wait()
    keep.wait()


def paired_exchange(table, peer_ids, region_ids, peers):
    local, slab_rows = table.shape
    slots = peer_ids.shape[0] // peers
    width = region_ids.shape[0] // 2
    doubled = jnp.concatenate([table, table], axis=1)
    vmem = pl.BlockSpec(memory_space=pltpu.VMEM)
    smem = pl.BlockSpec(memory_space=pltpu.SMEM)
    return pl.pallas_call(
        paired_kernel,
        out_shape=pltpu.VMEM((local + peers * slots // 2 + 2 * width, 2 * slab_rows), table.dtype),
        in_specs=[vmem, smem, smem],
        out_specs=vmem,
        scratch_shapes=[
            pltpu.VMEM((peers, slots // 2, 2 * slab_rows), table.dtype),
            pltpu.VMEM((2, width, 2 * slab_rows), table.dtype),
            pltpu.SemaphoreType.DMA((5,)),
        ],
        compiler_params=pltpu.CompilerParams(collective_id=2, has_side_effects=True),
    )(pltpu.with_memory_space_constraint(doubled, pltpu.VMEM), peer_ids, region_ids)


def paired_sources(halo_ids, local, peers, slots, width):
    half = slots // 2
    entry = halo_ids - local
    slot = entry % slots
    from_peer = (entry >= 0) & (entry < peers * slots)
    from_region = entry >= peers * slots
    row = jnp.where(
        from_peer,
        local + (entry // slots) * half + slot % half,
        jnp.where(from_region, halo_ids - peers * half, halo_ids),
    )
    upper = from_peer & (slot >= half)
    return row, upper


def assemble(voxels, layers, peer_ids, region_ids, halo_ids, paired_ids):
    slab_table = face_slabs(voxels, layers)
    peers = lax.axis_size("dev")
    if layers == 1 and paired_ids is not None:
        rows, upper = paired_ids
        table = paired_exchange(slab_table.T, peer_ids, region_ids, peers)
        lines = table.at[rows].get(mode="promise_in_bounds")
        width = slab_table.shape[0]
        chosen = jnp.where(upper[..., None], lines[..., width:], lines[..., :width])
        return jnp.moveaxis(chosen, 2, 0)
    slab_rows = slab_table.shape[0]
    combined = exchange(slab_table.T, peer_ids, region_ids, peers, layers)[:, :slab_rows].T
    picked = combined.at[:, halo_ids].get(mode="promise_in_bounds")
    return picked


def per_device(level_set, speed, peer_slabs, region_slabs, halo_source):
    count = level_set.shape[1]
    local = 6 * count
    peer_ids = jnp.clip(peer_slabs.reshape(-1), 0, local - 1)
    region_ids = jnp.clip(region_slabs.reshape(-1), 0, local - 1)
    halo_ids = jnp.clip(halo_source, 0, local + peer_ids.shape[0] + region_ids.shape[0] - 1)
    peers = lax.axis_size("dev")
    slots = peer_ids.shape[0] // peers
    paired_ids = None
    if slots % 2 == 0:
        paired_ids = paired_sources(halo_ids, local, peers, slots, region_ids.shape[0] // 2)
    voxels = level_set.reshape(8, 8, 8, count)
    speeds = speed.reshape(8, 8, 8, count)
    for offset_step in range(OFFSET_STEPS):
        picked = assemble(voxels, 3, peer_ids, region_ids, halo_ids, paired_ids)
        voxels = advect_leaves(voxels, lax.optimization_barrier(speeds), picked)
        sign_field = voxels / jnp.sqrt(voxels * voxels + 1.0)
        for redist_pass in range(REDIST_PASSES):
            picked = assemble(voxels, 1, peer_ids, region_ids, halo_ids, paired_ids)
            voxels = relax_leaves(voxels, sign_field, picked)
    return voxels.reshape(512, count)


def solution(mesh):
    return jax.shard_map(
        per_device,
        mesh=mesh,
        in_specs=(
            P(None, ("group", "dev")),
            P(None, ("group", "dev")),
            P(("group", "dev"), None),
            P(("group", "dev"), None),
            P(None, ("group", "dev")),
        ),
        out_specs=P(None, ("group", "dev")),
        check_vma=False,
    )
```

```python
import jax
import jax.numpy as jnp
from jax import lax
from jax.experimental import pallas as pl
from jax.experimental.pallas import tpu as pltpu
from jax.sharding import PartitionSpec as P

OFFSET_STEPS = 2
REDIST_PASSES = 2


advect_scale = 0.3
relax_scale = 0.3
weno_floor = 1e-06


def with_halo(block, sides, width):
    for axis, dim in sides:
        count = lax.axis_size(axis)
        forward = [(i, i + 1) for i in range(count - 1)]
        forward.append((count - 1, 0))
        backward = [(target, source) for source, target in forward]
        low = lax.ppermute(
            lax.slice_in_dim(block, block.shape[dim] - width, None, axis=dim), axis, forward
        )
        high = lax.ppermute(lax.slice_in_dim(block, 0, width, axis=dim), axis, backward)
        block = jnp.concatenate([low, block, high], axis=dim)
    return block


def face_slabs(voxels, layers):
    count = voxels.shape[3]
    pieces = [
        voxels[:layers],
        voxels[8 - layers :],
        voxels[:, :layers],
        voxels[:, 8 - layers :],
        voxels[:, :, :layers],
        voxels[:, :, 8 - layers :],
    ]
    return jnp.concatenate([piece.reshape(64 * layers, count) for piece in pieces], axis=1)


def weno_side(first, second, third, fourth, fifth):
    guess_a = first / 3.0 - 7.0 * second / 6.0 + 11.0 * third / 6.0
    guess_b = -second / 6.0 + 5.0 * third / 6.0 + fourth / 3.0
    guess_c = third / 3.0 + 5.0 * fourth / 6.0 - fifth / 6.0
    bend_a = first - 2.0 * second + third
    tilt_a = first - 4.0 * second + 3.0 * third
    bend_b = second - 2.0 * third + fourth
    tilt_b = second - fourth
    bend_c = third - 2.0 * fourth + fifth
    tilt_c = 3.0 * third - 4.0 * fourth + fifth
    smooth_a = weno_floor + 13.0 / 12.0 * bend_a * bend_a + 0.25 * tilt_a * tilt_a
    smooth_b = weno_floor + 13.0 / 12.0 * bend_b * bend_b + 0.25 * tilt_b * tilt_b
    smooth_c = weno_floor + 13.0 / 12.0 * bend_c * bend_c + 0.25 * tilt_c * tilt_c
    square_a = smooth_a * smooth_a
    square_b = smooth_b * smooth_b
    square_c = smooth_c * smooth_c
    weight_a = 0.1 * (square_b * square_c)
    weight_b = 0.6 * (square_a * square_c)
    weight_c = 0.3 * (square_a * square_b)
    return (weight_a * guess_a + weight_b * guess_b + weight_c * guess_c) / (
        weight_a + weight_b + weight_c
    )


def one_sided(padded, along):
    differences = jnp.diff(padded, axis=along)

    def window(lowest):
        return lax.slice_in_dim(differences, lowest, lowest + 8, axis=along)

    backward = weno_side(window(0), window(1), window(2), window(3), window(4))
    forward = weno_side(window(5), window(4), window(3), window(2), window(1))
    return (backward, forward)


def widen(voxels, picked, layers):
    count = voxels.shape[3]

    def face_part(side, extent):
        return picked[:, side, :].reshape(extent + (count,))

    along_x = jnp.concatenate(
        [face_part(0, (layers, 8, 8)), voxels, face_part(1, (layers, 8, 8))], axis=0
    )
    along_y = jnp.concatenate(
        [face_part(2, (8, layers, 8)), voxels, face_part(3, (8, layers, 8))], axis=1
    )
    along_z = jnp.concatenate(
        [face_part(4, (8, 8, layers)), voxels, face_part(5, (8, 8, layers))], axis=2
    )
    return (along_x, along_y, along_z)


def advect_leaves(voxels, speeds, picked):
    squared = jnp.zeros_like(voxels)
    for along, padded in enumerate(widen(voxels, picked, 3)):
        backward, forward = one_sided(padded, along)
        squared = squared + jnp.maximum(
            jnp.square(jnp.maximum(backward, 0.0)), jnp.square(jnp.minimum(forward, 0.0))
        )
    return voxels - speeds * jnp.sqrt(squared)


def relax_leaves(voxels, sign_field, picked):
    squared = jnp.zeros_like(voxels)
    for along, padded in enumerate(widen(voxels, picked, 1)):
        centre = lax.slice_in_dim(padded, 1, 9, axis=along)
        backward = centre - lax.slice_in_dim(padded, 0, 8, axis=along)
        forward = lax.slice_in_dim(padded, 2, 10, axis=along) - centre
        rising = jnp.maximum(
            jnp.square(jnp.maximum(backward, 0.0)), jnp.square(jnp.minimum(forward, 0.0))
        )
        falling = jnp.maximum(
            jnp.square(jnp.minimum(backward, 0.0)), jnp.square(jnp.maximum(forward, 0.0))
        )
        squared = squared + jnp.where(sign_field > 0.0, rising, falling)
    return voxels - relax_scale * sign_field * (jnp.sqrt(squared) - 1.0)


def far_first(me, peers):
    if peers != 64:
        return [lax.rem(me + k, peers) for k in range(1, peers)]
    moves = [
        (dz, dx, dc) for dz in range(8) for dx in range(4) for dc in range(2) if (dz, dx, dc) != (0, 0, 0)
    ]
    moves.sort(key=lambda m: -(min(m[0], 8 - m[0]) + min(m[1], 4 - m[1])))
    z, x, c = me // 8, (me // 2) % 4, me % 2
    return [
        lax.rem(z + dz, 8) * 8 + lax.rem(x + dx, 4) * 2 + lax.rem(c + dc, 2) for dz, dx, dc in moves
    ]


def exchange_kernel(
    tab_ref, idx_ref, ridx_ref, speed_hbm, comb_ref, scaled_ref, og_ref, bd_ref, sems, speed_ref
):
    peers, slots = og_ref.shape[0], og_ref.shape[1]
    local = tab_ref.shape[0]
    width = bd_ref.shape[1]
    regions = lax.axis_size("group")
    me = lax.axis_index("dev")
    region = lax.axis_index("group")
    up = lax.rem(region + 1, regions)
    down = lax.rem(region + regions - 1, regions)
    mesh_ids = pl.DeviceIdType.MESH
    arrived = local
    bordering = local + peers * slots

    keep = pltpu.make_async_copy(tab_ref, comb_ref.at[pl.ds(0, local)], sems.at[4])
    keep.start()
    fetch = pltpu.make_async_copy(speed_hbm, speed_ref, sems.at[5])
    fetch.start()

    barrier = pltpu.get_barrier_semaphore()

    targets = far_first(me, peers)
    for e in targets:
        pl.semaphore_signal(barrier, inc=1, device_id=(region, e), device_id_type=mesh_ids)
    pl.semaphore_signal(barrier, inc=1, device_id=(up, me), device_id_type=mesh_ids)
    pl.semaphore_signal(barrier, inc=1, device_id=(down, me), device_id_type=mesh_ids)

    for h in range(2):
        for p in range(width):
            source = ridx_ref[h * width + p]
            bd_ref[h, pl.ds(p, 1), :] = tab_ref[pl.ds(source, 1), :]

    def pack(e, carry):
        for c in range(slots):
            source = idx_ref[e * slots + c]
            og_ref[e, pl.ds(c, 1), :] = tab_ref[pl.ds(source, 1), :]
        return carry

    lax.fori_loop(0, peers, pack, 0)

    fetch.wait()
    scaled_ref[...] = advect_scale * speed_ref[...]

    pl.semaphore_wait(barrier, peers + 1)

    pltpu.make_async_remote_copy(
        src_ref=bd_ref.at[1],
        dst_ref=comb_ref.at[pl.ds(bordering, width)],
        send_sem=sems.at[2],
        recv_sem=sems.at[3],
        device_id=(up, me),
        device_id_type=mesh_ids,
    ).start()
    pltpu.make_async_remote_copy(
        src_ref=bd_ref.at[0],
        dst_ref=comb_ref.at[pl.ds(bordering + width, width)],
        send_sem=sems.at[2],
        recv_sem=sems.at[3],
        device_id=(down, me),
        device_id_type=mesh_ids,
    ).start()

    mine = pl.ds(pl.multiple_of(arrived + me * slots, slots), slots)

    for e in targets:
        pltpu.make_async_remote_copy(
            src_ref=og_ref.at[e],
            dst_ref=comb_ref.at[mine],
            send_sem=sems.at[0],
            recv_sem=sems.at[1],
            device_id=(region, e),
            device_id_type=mesh_ids,
        ).start()
    comb_ref[mine, :] = og_ref[me]

    pltpu.make_async_copy(og_ref.at[pl.ds(0, peers - 1)], og_ref.at[pl.ds(0, peers - 1)], sems.at[0]).wait()
    pltpu.make_async_copy(bd_ref, bd_ref, sems.at[2]).wait()
    pltpu.make_async_copy(og_ref.at[pl.ds(0, peers - 1)], og_ref.at[pl.ds(0, peers - 1)], sems.at[1]).wait()
    pltpu.make_async_copy(bd_ref, bd_ref, sems.at[3]).wait()
    keep.wait()


def exchange(table, peer_ids, region_ids, peers, layers, speeds):
    local, slab_rows = table.shape
    slots = peer_ids.shape[0] // peers
    width = region_ids.shape[0] // 2
    vmem = pl.BlockSpec(memory_space=pltpu.VMEM)
    smem = pl.BlockSpec(memory_space=pltpu.SMEM)
    return pl.pallas_call(
        exchange_kernel,
        out_shape=(
            (pltpu.VMEM if layers == 1 else jax.ShapeDtypeStruct)(
                (local + peers * slots + 2 * width, slab_rows), table.dtype
            ),
            pltpu.VMEM(speeds.shape, speeds.dtype),
        ),
        in_specs=[vmem, smem, smem, pl.BlockSpec(memory_space=pl.ANY)],
        out_specs=(vmem, vmem),
        scratch_shapes=[
            pltpu.VMEM((peers, slots, slab_rows), table.dtype),
            pltpu.VMEM((2, width, slab_rows), table.dtype),
            pltpu.SemaphoreType.DMA((6,)),
            pltpu.VMEM(speeds.shape, speeds.dtype),
        ],
        compiler_params=pltpu.CompilerParams(collective_id=layers, has_side_effects=True),
    )(pltpu.with_memory_space_constraint(table, pltpu.VMEM), peer_ids, region_ids, speeds)


def paired_kernel(tab_ref, idx_ref, ridx_ref, comb_ref, og_ref, bd_ref, sems):
    peers, half, lane_count = og_ref.shape
    slots = 2 * half
    slab_rows = lane_count // 2
    local = tab_ref.shape[0]
    width = bd_ref.shape[1]
    regions = lax.axis_size("group")
    me = lax.axis_index("dev")
    region = lax.axis_index("group")
    up = lax.rem(region + 1, regions)
    down = lax.rem(region + regions - 1, regions)
    mesh_ids = pl.DeviceIdType.MESH
    bordering = local + peers * half

    keep = pltpu.make_async_copy(tab_ref, comb_ref.at[pl.ds(0, local)], sems.at[4])
    keep.start()

    barrier = pltpu.get_barrier_semaphore()
    targets = far_first(me, peers)
    for e in targets:
        pl.semaphore_signal(barrier, inc=1, device_id=(region, e), device_id_type=mesh_ids)
    pl.semaphore_signal(barrier, inc=1, device_id=(up, me), device_id_type=mesh_ids)
    pl.semaphore_signal(barrier, inc=1, device_id=(down, me), device_id_type=mesh_ids)

    for h in range(2):
        for p in range(width):
            source = ridx_ref[h * width + p]
            bd_ref[h, pl.ds(p, 1), :] = tab_ref[pl.ds(source, 1), :]

    lanes = lax.broadcasted_iota(jnp.int32, (1, lane_count), 1)

    def pack(e, carry):
        for r in range(half):
            first = tab_ref[pl.ds(idx_ref[e * slots + r], 1), :]
            second = tab_ref[pl.ds(idx_ref[e * slots + r + half], 1), :]
            og_ref[e, pl.ds(r, 1), :] = jnp.where(lanes < slab_rows, first, second)
        return carry

    lax.fori_loop(0, peers, pack, 0)

    pl.semaphore_wait(barrier, peers + 1)

    pltpu.make_async_remote_copy(
        src_ref=bd_ref.at[1],
        dst_ref=comb_ref.at[pl.ds(bordering, width)],
        send_sem=sems.at[2],
        recv_sem=sems.at[3],
        device_id=(up, me),
        device_id_type=mesh_ids,
    ).start()
    pltpu.make_async_remote_copy(
        src_ref=bd_ref.at[0],
        dst_ref=comb_ref.at[pl.ds(bordering + width, width)],
        send_sem=sems.at[2],
        recv_sem=sems.at[3],
        device_id=(down, me),
        device_id_type=mesh_ids,
    ).start()

    mine = pl.ds(local + me * half, half)
    for e in targets:
        pltpu.make_async_remote_copy(
            src_ref=og_ref.at[e],
            dst_ref=comb_ref.at[mine],
            send_sem=sems.at[0],
            recv_sem=sems.at[1],
            device_id=(region, e),
            device_id_type=mesh_ids,
        ).start()
    pltpu.make_async_copy(og_ref.at[me], comb_ref.at[mine], sems.at[1]).start()

    pltpu.make_async_copy(og_ref.at[pl.ds(0, peers - 1)], og_ref.at[pl.ds(0, peers - 1)], sems.at[0]).wait()
    pltpu.make_async_copy(bd_ref, bd_ref, sems.at[2]).wait()
    pltpu.make_async_copy(og_ref, og_ref, sems.at[1]).wait()
    pltpu.make_async_copy(bd_ref, bd_ref, sems.at[3]).wait()
    keep.wait()


def paired_exchange(table, peer_ids, region_ids, peers):
    local, slab_rows = table.shape
    slots = peer_ids.shape[0] // peers
    width = region_ids.shape[0] // 2
    doubled = jnp.concatenate([table, table], axis=1)
    vmem = pl.BlockSpec(memory_space=pltpu.VMEM)
    smem = pl.BlockSpec(memory_space=pltpu.SMEM)
    return pl.pallas_call(
        paired_kernel,
        out_shape=pltpu.VMEM((local + peers * slots // 2 + 2 * width, 2 * slab_rows), table.dtype),
        in_specs=[vmem, smem, smem],
        out_specs=vmem,
        scratch_shapes=[
            pltpu.VMEM((peers, slots // 2, 2 * slab_rows), table.dtype),
            pltpu.VMEM((2, width, 2 * slab_rows), table.dtype),
            pltpu.SemaphoreType.DMA((5,)),
        ],
        compiler_params=pltpu.CompilerParams(collective_id=2, has_side_effects=True),
    )(pltpu.with_memory_space_constraint(doubled, pltpu.VMEM), peer_ids, region_ids)


def paired_sources(halo_ids, local, peers, slots, width):
    half = slots // 2
    entry = halo_ids - local
    slot = entry % slots
    from_peer = (entry >= 0) & (entry < peers * slots)
    from_region = entry >= peers * slots
    row = jnp.where(
        from_peer,
        local + (entry // slots) * half + slot % half,
        jnp.where(from_region, halo_ids - peers * half, halo_ids),
    )
    upper = from_peer & (slot >= half)
    return row, upper


def assemble(voxels, layers, peer_ids, region_ids, halo_ids, paired_ids, speeds=None):
    slab_table = face_slabs(voxels, layers)
    peers = lax.axis_size("dev")
    if layers == 1 and paired_ids is not None:
        rows, upper = paired_ids
        table = paired_exchange(slab_table.T, peer_ids, region_ids, peers)
        lines = table.at[rows].get(mode="promise_in_bounds")
        width = slab_table.shape[0]
        chosen = jnp.where(upper[..., None], lines[..., width:], lines[..., :width])
        return jnp.moveaxis(chosen, 2, 0)
    combined, scaled = exchange(slab_table.T, peer_ids, region_ids, peers, layers, speeds)
    picked = combined.T.at[:, halo_ids].get(mode="promise_in_bounds")
    return picked, scaled


def per_device(level_set, speed, peer_slabs, region_slabs, halo_source):
    count = level_set.shape[1]
    local = 6 * count
    peer_ids = jnp.clip(peer_slabs.reshape(-1), 0, local - 1)
    region_ids = jnp.clip(region_slabs.reshape(-1), 0, local - 1)
    halo_ids = jnp.clip(halo_source, 0, local + peer_ids.shape[0] + region_ids.shape[0] - 1)
    peers = lax.axis_size("dev")
    slots = peer_ids.shape[0] // peers
    paired_ids = None
    if slots % 2 == 0:
        paired_ids = paired_sources(halo_ids, local, peers, slots, region_ids.shape[0] // 2)
    voxels = level_set.reshape(8, 8, 8, count)
    speeds = speed.reshape(8, 8, 8, count)
    for offset_step in range(OFFSET_STEPS):
        picked, scaled = assemble(
            voxels, 3, peer_ids, region_ids, halo_ids, paired_ids, speed
        )
        voxels = advect_leaves(voxels, scaled.reshape(speeds.shape), picked)
        sign_field = voxels / jnp.sqrt(voxels * voxels + 1.0)
        for redist_pass in range(REDIST_PASSES):
            picked = assemble(voxels, 1, peer_ids, region_ids, halo_ids, paired_ids)
            voxels = relax_leaves(voxels, sign_field, picked)
    return voxels.reshape(512, count)


def solution(mesh):
    return jax.shard_map(
        per_device,
        mesh=mesh,
        in_specs=(
            P(None, ("group", "dev")),
            P(None, ("group", "dev")),
            P(("group", "dev"), None),
            P(("group", "dev"), None),
            P(None, ("group", "dev")),
        ),
        out_specs=P(None, ("group", "dev")),
        check_vma=False,
    )
```

```python
import jax
import jax.numpy as jnp
from jax import lax
from jax.experimental import pallas as pl
from jax.experimental.pallas import tpu as pltpu
from jax.sharding import PartitionSpec as P

OFFSET_STEPS = 2
REDIST_PASSES = 2


advect_scale = 0.3
relax_scale = 0.3
weno_floor = 1e-06


def with_halo(block, sides, width):
    for axis, dim in sides:
        count = lax.axis_size(axis)
        forward = [(i, i + 1) for i in range(count - 1)]
        forward.append((count - 1, 0))
        backward = [(target, source) for source, target in forward]
        low = lax.ppermute(
            lax.slice_in_dim(block, block.shape[dim] - width, None, axis=dim), axis, forward
        )
        high = lax.ppermute(lax.slice_in_dim(block, 0, width, axis=dim), axis, backward)
        block = jnp.concatenate([low, block, high], axis=dim)
    return block


def face_slabs(voxels, layers):
    count = voxels.shape[3]
    pieces = [
        voxels[:layers],
        voxels[8 - layers :],
        voxels[:, :layers],
        voxels[:, 8 - layers :],
        voxels[:, :, :layers],
        voxels[:, :, 8 - layers :],
    ]
    return jnp.concatenate([piece.reshape(64 * layers, count) for piece in pieces], axis=1)


def weno_side(first, second, third, fourth, fifth):
    guess_a = first / 3.0 - 7.0 * second / 6.0 + 11.0 * third / 6.0
    guess_b = -second / 6.0 + 5.0 * third / 6.0 + fourth / 3.0
    guess_c = third / 3.0 + 5.0 * fourth / 6.0 - fifth / 6.0
    bend_a = first - 2.0 * second + third
    tilt_a = first - 4.0 * second + 3.0 * third
    bend_b = second - 2.0 * third + fourth
    tilt_b = second - fourth
    bend_c = third - 2.0 * fourth + fifth
    tilt_c = 3.0 * third - 4.0 * fourth + fifth
    smooth_a = weno_floor + 13.0 / 12.0 * bend_a * bend_a + 0.25 * tilt_a * tilt_a
    smooth_b = weno_floor + 13.0 / 12.0 * bend_b * bend_b + 0.25 * tilt_b * tilt_b
    smooth_c = weno_floor + 13.0 / 12.0 * bend_c * bend_c + 0.25 * tilt_c * tilt_c
    square_a = smooth_a * smooth_a
    square_b = smooth_b * smooth_b
    square_c = smooth_c * smooth_c
    weight_a = 0.1 * (square_b * square_c)
    weight_b = 0.6 * (square_a * square_c)
    weight_c = 0.3 * (square_a * square_b)
    return (weight_a * guess_a + weight_b * guess_b + weight_c * guess_c) / (
        weight_a + weight_b + weight_c
    )


def one_sided(padded, along):
    differences = jnp.diff(padded, axis=along)

    def window(lowest):
        return lax.slice_in_dim(differences, lowest, lowest + 8, axis=along)

    backward = weno_side(window(0), window(1), window(2), window(3), window(4))
    forward = weno_side(window(5), window(4), window(3), window(2), window(1))
    return (backward, forward)


def widen(voxels, picked, layers):
    count = voxels.shape[3]

    def face_part(side, extent):
        return picked[:, side, :].reshape(extent + (count,))

    along_x = jnp.concatenate(
        [face_part(0, (layers, 8, 8)), voxels, face_part(1, (layers, 8, 8))], axis=0
    )
    along_y = jnp.concatenate(
        [face_part(2, (8, layers, 8)), voxels, face_part(3, (8, layers, 8))], axis=1
    )
    along_z = jnp.concatenate(
        [face_part(4, (8, 8, layers)), voxels, face_part(5, (8, 8, layers))], axis=2
    )
    return (along_x, along_y, along_z)


def advect_leaves(voxels, speeds, picked):
    squared = jnp.zeros_like(voxels)
    for along, padded in enumerate(widen(voxels, picked, 3)):
        backward, forward = one_sided(padded, along)
        squared = squared + jnp.maximum(
            jnp.square(jnp.maximum(backward, 0.0)), jnp.square(jnp.minimum(forward, 0.0))
        )
    return voxels - advect_scale * speeds * jnp.sqrt(squared)


def relax_leaves(voxels, sign_field, picked):
    squared = jnp.zeros_like(voxels)
    for along, padded in enumerate(widen(voxels, picked, 1)):
        centre = lax.slice_in_dim(padded, 1, 9, axis=along)
        backward = centre - lax.slice_in_dim(padded, 0, 8, axis=along)
        forward = lax.slice_in_dim(padded, 2, 10, axis=along) - centre
        rising = jnp.maximum(
            jnp.square(jnp.maximum(backward, 0.0)), jnp.square(jnp.minimum(forward, 0.0))
        )
        falling = jnp.maximum(
            jnp.square(jnp.minimum(backward, 0.0)), jnp.square(jnp.maximum(forward, 0.0))
        )
        squared = squared + jnp.where(sign_field > 0.0, rising, falling)
    return voxels - relax_scale * sign_field * (jnp.sqrt(squared) - 1.0)


def far_first(me, peers):
    if peers != 64:
        return [lax.rem(me + k, peers) for k in range(1, peers)]
    moves = [
        (dz, dx, dc) for dz in range(8) for dx in range(4) for dc in range(2) if (dz, dx, dc) != (0, 0, 0)
    ]
    moves.sort(key=lambda m: -(min(m[0], 8 - m[0]) + min(m[1], 4 - m[1])))
    z, x, c = me // 8, (me // 2) % 4, me % 2
    way = 1 - 2 * c
    return [
        lax.rem(z + way * dz + 8, 8) * 8 + lax.rem(x + way * dx + 4, 4) * 2 + lax.rem(c + dc, 2)
        for dz, dx, dc in moves
    ]


def exchange_kernel(
    tab_ref, idx_ref, ridx_ref, comb_ref, og_ref, bd_ref, sems
):
    peers, slots = og_ref.shape[0], og_ref.shape[1]
    local = tab_ref.shape[0]
    width = bd_ref.shape[1]
    regions = lax.axis_size("group")
    me = lax.axis_index("dev")
    region = lax.axis_index("group")
    up = lax.rem(region + 1, regions)
    down = lax.rem(region + regions - 1, regions)
    mesh_ids = pl.DeviceIdType.MESH
    arrived = local
    bordering = local + peers * slots

    keep = pltpu.make_async_copy(tab_ref, comb_ref.at[pl.ds(0, local)], sems.at[4])
    keep.start()

    barrier = pltpu.get_barrier_semaphore()

    targets = far_first(me, peers)
    for e in targets:
        pl.semaphore_signal(barrier, inc=1, device_id=(region, e), device_id_type=mesh_ids)
    pl.semaphore_signal(barrier, inc=1, device_id=(up, me), device_id_type=mesh_ids)
    pl.semaphore_signal(barrier, inc=1, device_id=(down, me), device_id_type=mesh_ids)

    for h in range(2):
        for p in range(width):
            source = ridx_ref[h * width + p]
            bd_ref[h, pl.ds(p, 1), :] = tab_ref[pl.ds(source, 1), :]

    def pack(e, carry):
        for c in range(slots):
            source = idx_ref[e * slots + c]
            og_ref[e, pl.ds(c, 1), :] = tab_ref[pl.ds(source, 1), :]
        return carry

    lax.fori_loop(0, peers, pack, 0)

    pl.semaphore_wait(barrier, peers + 1)

    pltpu.make_async_remote_copy(
        src_ref=bd_ref.at[1],
        dst_ref=comb_ref.at[pl.ds(bordering, width)],
        send_sem=sems.at[2],
        recv_sem=sems.at[3],
        device_id=(up, me),
        device_id_type=mesh_ids,
    ).start()
    pltpu.make_async_remote_copy(
        src_ref=bd_ref.at[0],
        dst_ref=comb_ref.at[pl.ds(bordering + width, width)],
        send_sem=sems.at[2],
        recv_sem=sems.at[3],
        device_id=(down, me),
        device_id_type=mesh_ids,
    ).start()

    mine = pl.ds(pl.multiple_of(arrived + me * slots, slots), slots)

    for e in targets:
        pltpu.make_async_remote_copy(
            src_ref=og_ref.at[e],
            dst_ref=comb_ref.at[mine],
            send_sem=sems.at[0],
            recv_sem=sems.at[1],
            device_id=(region, e),
            device_id_type=mesh_ids,
        ).start()
    comb_ref[mine, :] = og_ref[me]

    pltpu.make_async_copy(og_ref.at[pl.ds(0, peers - 1)], og_ref.at[pl.ds(0, peers - 1)], sems.at[0]).wait()
    pltpu.make_async_copy(bd_ref, bd_ref, sems.at[2]).wait()
    pltpu.make_async_copy(og_ref.at[pl.ds(0, peers - 1)], og_ref.at[pl.ds(0, peers - 1)], sems.at[1]).wait()
    pltpu.make_async_copy(bd_ref, bd_ref, sems.at[3]).wait()
    keep.wait()


def exchange(table, peer_ids, region_ids, peers, layers):
    local, slab_rows = table.shape
    slots = peer_ids.shape[0] // peers
    width = region_ids.shape[0] // 2
    vmem = pl.BlockSpec(memory_space=pltpu.VMEM)
    smem = pl.BlockSpec(memory_space=pltpu.SMEM)
    return pl.pallas_call(
        exchange_kernel,
        out_shape=(pltpu.VMEM if layers == 1 else jax.ShapeDtypeStruct)(
            (local + peers * slots + 2 * width, slab_rows), table.dtype
        ),
        in_specs=[vmem, smem, smem],
        out_specs=vmem,
        scratch_shapes=[
            pltpu.VMEM((peers, slots, slab_rows), table.dtype),
            pltpu.VMEM((2, width, slab_rows), table.dtype),
            pltpu.SemaphoreType.DMA((5,)),
        ],
        compiler_params=pltpu.CompilerParams(collective_id=layers, has_side_effects=True),
    )(pltpu.with_memory_space_constraint(table, pltpu.VMEM), peer_ids, region_ids)


def paired_kernel(tab_ref, idx_ref, ridx_ref, comb_ref, og_ref, bd_ref, sems):
    peers, half, lane_count = og_ref.shape
    slots = 2 * half
    slab_rows = lane_count // 2
    local = tab_ref.shape[0]
    width = bd_ref.shape[1]
    regions = lax.axis_size("group")
    me = lax.axis_index("dev")
    region = lax.axis_index("group")
    up = lax.rem(region + 1, regions)
    down = lax.rem(region + regions - 1, regions)
    mesh_ids = pl.DeviceIdType.MESH
    bordering = local + peers * half

    keep = pltpu.make_async_copy(tab_ref, comb_ref.at[pl.ds(0, local)], sems.at[4])
    keep.start()

    barrier = pltpu.get_barrier_semaphore()
    targets = far_first(me, peers)
    for e in targets:
        pl.semaphore_signal(barrier, inc=1, device_id=(region, e), device_id_type=mesh_ids)
    pl.semaphore_signal(barrier, inc=1, device_id=(up, me), device_id_type=mesh_ids)
    pl.semaphore_signal(barrier, inc=1, device_id=(down, me), device_id_type=mesh_ids)

    for h in range(2):
        for p in range(width):
            source = ridx_ref[h * width + p]
            bd_ref[h, pl.ds(p, 1), :] = tab_ref[pl.ds(source, 1), :]

    lanes = lax.broadcasted_iota(jnp.int32, (1, lane_count), 1)

    def pack(e, carry):
        for r in range(half):
            first = tab_ref[pl.ds(idx_ref[e * slots + r], 1), :]
            second = tab_ref[pl.ds(idx_ref[e * slots + r + half], 1), :]
            og_ref[e, pl.ds(r, 1), :] = jnp.where(lanes < slab_rows, first, second)
        return carry

    lax.fori_loop(0, peers, pack, 0)

    pl.semaphore_wait(barrier, peers + 1)

    pltpu.make_async_remote_copy(
        src_ref=bd_ref.at[1],
        dst_ref=comb_ref.at[pl.ds(bordering, width)],
        send_sem=sems.at[2],
        recv_sem=sems.at[3],
        device_id=(up, me),
        device_id_type=mesh_ids,
    ).start()
    pltpu.make_async_remote_copy(
        src_ref=bd_ref.at[0],
        dst_ref=comb_ref.at[pl.ds(bordering + width, width)],
        send_sem=sems.at[2],
        recv_sem=sems.at[3],
        device_id=(down, me),
        device_id_type=mesh_ids,
    ).start()

    mine = pl.ds(local + me * half, half)
    for e in targets:
        pltpu.make_async_remote_copy(
            src_ref=og_ref.at[e],
            dst_ref=comb_ref.at[mine],
            send_sem=sems.at[0],
            recv_sem=sems.at[1],
            device_id=(region, e),
            device_id_type=mesh_ids,
        ).start()
    pltpu.make_async_copy(og_ref.at[me], comb_ref.at[mine], sems.at[1]).start()

    pltpu.make_async_copy(og_ref.at[pl.ds(0, peers - 1)], og_ref.at[pl.ds(0, peers - 1)], sems.at[0]).wait()
    pltpu.make_async_copy(bd_ref, bd_ref, sems.at[2]).wait()
    pltpu.make_async_copy(og_ref, og_ref, sems.at[1]).wait()
    pltpu.make_async_copy(bd_ref, bd_ref, sems.at[3]).wait()
    keep.wait()


def paired_exchange(table, peer_ids, region_ids, peers):
    local, slab_rows = table.shape
    slots = peer_ids.shape[0] // peers
    width = region_ids.shape[0] // 2
    doubled = jnp.concatenate([table, table], axis=1)
    vmem = pl.BlockSpec(memory_space=pltpu.VMEM)
    smem = pl.BlockSpec(memory_space=pltpu.SMEM)
    return pl.pallas_call(
        paired_kernel,
        out_shape=pltpu.VMEM((local + peers * slots // 2 + 2 * width, 2 * slab_rows), table.dtype),
        in_specs=[vmem, smem, smem],
        out_specs=vmem,
        scratch_shapes=[
            pltpu.VMEM((peers, slots // 2, 2 * slab_rows), table.dtype),
            pltpu.VMEM((2, width, 2 * slab_rows), table.dtype),
            pltpu.SemaphoreType.DMA((5,)),
        ],
        compiler_params=pltpu.CompilerParams(collective_id=2, has_side_effects=True),
    )(pltpu.with_memory_space_constraint(doubled, pltpu.VMEM), peer_ids, region_ids)


def paired_sources(halo_ids, local, peers, slots, width):
    half = slots // 2
    entry = halo_ids - local
    slot = entry % slots
    from_peer = (entry >= 0) & (entry < peers * slots)
    from_region = entry >= peers * slots
    row = jnp.where(
        from_peer,
        local + (entry // slots) * half + slot % half,
        jnp.where(from_region, halo_ids - peers * half, halo_ids),
    )
    upper = from_peer & (slot >= half)
    return row, upper


def assemble(voxels, layers, peer_ids, region_ids, halo_ids, paired_ids):
    slab_table = face_slabs(voxels, layers)
    peers = lax.axis_size("dev")
    if layers == 1 and paired_ids is not None:
        rows, upper = paired_ids
        table = paired_exchange(slab_table.T, peer_ids, region_ids, peers)
        lines = table.at[rows].get(mode="promise_in_bounds")
        width = slab_table.shape[0]
        chosen = jnp.where(upper[..., None], lines[..., width:], lines[..., :width])
        return jnp.moveaxis(chosen, 2, 0)
    combined = exchange(slab_table.T, peer_ids, region_ids, peers, layers).T
    picked = combined.at[:, halo_ids].get(mode="promise_in_bounds")
    return picked


def per_device(level_set, speed, peer_slabs, region_slabs, halo_source):
    count = level_set.shape[1]
    local = 6 * count
    peer_ids = jnp.clip(peer_slabs.reshape(-1), 0, local - 1)
    region_ids = jnp.clip(region_slabs.reshape(-1), 0, local - 1)
    halo_ids = jnp.clip(halo_source, 0, local + peer_ids.shape[0] + region_ids.shape[0] - 1)
    peers = lax.axis_size("dev")
    slots = peer_ids.shape[0] // peers
    paired_ids = None
    if slots % 2 == 0:
        paired_ids = paired_sources(halo_ids, local, peers, slots, region_ids.shape[0] // 2)
    voxels = level_set.reshape(8, 8, 8, count)
    speeds = speed.reshape(8, 8, 8, count)
    for offset_step in range(OFFSET_STEPS):
        picked = assemble(voxels, 3, peer_ids, region_ids, halo_ids, paired_ids)
        voxels = advect_leaves(voxels, lax.optimization_barrier(speeds), picked)
        sign_field = voxels / jnp.sqrt(voxels * voxels + 1.0)
        for redist_pass in range(REDIST_PASSES):
            picked = assemble(voxels, 1, peer_ids, region_ids, halo_ids, paired_ids)
            voxels = relax_leaves(voxels, sign_field, picked)
    return voxels.reshape(512, count)


def solution(mesh):
    return jax.shard_map(
        per_device,
        mesh=mesh,
        in_specs=(
            P(None, ("group", "dev")),
            P(None, ("group", "dev")),
            P(("group", "dev"), None),
            P(("group", "dev"), None),
            P(None, ("group", "dev")),
        ),
        out_specs=P(None, ("group", "dev")),
        check_vma=False,
    )
```

```python
import jax
import jax.numpy as jnp
from jax import lax
from jax.experimental import pallas as pl
from jax.experimental.pallas import tpu as pltpu
from jax.sharding import PartitionSpec as P

OFFSET_STEPS = 2
REDIST_PASSES = 2


advect_scale = 0.3
relax_scale = 0.3
weno_floor = 1e-06


def with_halo(block, sides, width):
    for axis, dim in sides:
        count = lax.axis_size(axis)
        forward = [(i, i + 1) for i in range(count - 1)]
        forward.append((count - 1, 0))
        backward = [(target, source) for source, target in forward]
        low = lax.ppermute(
            lax.slice_in_dim(block, block.shape[dim] - width, None, axis=dim), axis, forward
        )
        high = lax.ppermute(lax.slice_in_dim(block, 0, width, axis=dim), axis, backward)
        block = jnp.concatenate([low, block, high], axis=dim)
    return block


def face_slabs(voxels, layers):
    count = voxels.shape[3]
    pieces = [
        voxels[:layers],
        voxels[8 - layers :],
        voxels[:, :layers],
        voxels[:, 8 - layers :],
        voxels[:, :, :layers],
        voxels[:, :, 8 - layers :],
    ]
    return jnp.concatenate([piece.reshape(64 * layers, count) for piece in pieces], axis=1)


def weno_side(first, second, third, fourth, fifth):
    guess_a = first / 3.0 - 7.0 * second / 6.0 + 11.0 * third / 6.0
    guess_b = -second / 6.0 + 5.0 * third / 6.0 + fourth / 3.0
    guess_c = third / 3.0 + 5.0 * fourth / 6.0 - fifth / 6.0
    bend_a = first - 2.0 * second + third
    tilt_a = first - 4.0 * second + 3.0 * third
    bend_b = second - 2.0 * third + fourth
    tilt_b = second - fourth
    bend_c = third - 2.0 * fourth + fifth
    tilt_c = 3.0 * third - 4.0 * fourth + fifth
    smooth_a = weno_floor + 13.0 / 12.0 * bend_a * bend_a + 0.25 * tilt_a * tilt_a
    smooth_b = weno_floor + 13.0 / 12.0 * bend_b * bend_b + 0.25 * tilt_b * tilt_b
    smooth_c = weno_floor + 13.0 / 12.0 * bend_c * bend_c + 0.25 * tilt_c * tilt_c
    square_a = smooth_a * smooth_a
    square_b = smooth_b * smooth_b
    square_c = smooth_c * smooth_c
    weight_a = 0.1 * (square_b * square_c)
    weight_b = 0.6 * (square_a * square_c)
    weight_c = 0.3 * (square_a * square_b)
    return (weight_a * guess_a + weight_b * guess_b + weight_c * guess_c) / (
        weight_a + weight_b + weight_c
    )


def one_sided(padded, along):
    differences = jnp.diff(padded, axis=along)

    def window(lowest):
        return lax.slice_in_dim(differences, lowest, lowest + 8, axis=along)

    backward = weno_side(window(0), window(1), window(2), window(3), window(4))
    forward = weno_side(window(5), window(4), window(3), window(2), window(1))
    return (backward, forward)


def widen(voxels, picked, layers):
    count = voxels.shape[3]

    def face_part(side, extent):
        return picked[:, side, :].reshape(extent + (count,))

    along_x = jnp.concatenate(
        [face_part(0, (layers, 8, 8)), voxels, face_part(1, (layers, 8, 8))], axis=0
    )
    along_y = jnp.concatenate(
        [face_part(2, (8, layers, 8)), voxels, face_part(3, (8, layers, 8))], axis=1
    )
    along_z = jnp.concatenate(
        [face_part(4, (8, 8, layers)), voxels, face_part(5, (8, 8, layers))], axis=2
    )
    return (along_x, along_y, along_z)


def advect_leaves(voxels, speeds, picked):
    squared = jnp.zeros_like(voxels)
    for along, padded in enumerate(widen(voxels, picked, 3)):
        backward, forward = one_sided(padded, along)
        squared = squared + jnp.maximum(
            jnp.square(jnp.maximum(backward, 0.0)), jnp.square(jnp.minimum(forward, 0.0))
        )
    return voxels - advect_scale * speeds * jnp.sqrt(squared)


def relax_leaves(voxels, sign_field, picked):
    squared = jnp.zeros_like(voxels)
    for along, padded in enumerate(widen(voxels, picked, 1)):
        centre = lax.slice_in_dim(padded, 1, 9, axis=along)
        backward = centre - lax.slice_in_dim(padded, 0, 8, axis=along)
        forward = lax.slice_in_dim(padded, 2, 10, axis=along) - centre
        rising = jnp.maximum(
            jnp.square(jnp.maximum(backward, 0.0)), jnp.square(jnp.minimum(forward, 0.0))
        )
        falling = jnp.maximum(
            jnp.square(jnp.minimum(backward, 0.0)), jnp.square(jnp.maximum(forward, 0.0))
        )
        squared = squared + jnp.where(sign_field > 0.0, rising, falling)
    return voxels - relax_scale * sign_field * (jnp.sqrt(squared) - 1.0)


def far_first(me, peers):
    if peers != 64:
        return [lax.rem(me + k, peers) for k in range(1, peers)]
    moves = [
        (dz, dx, dc) for dz in range(8) for dx in range(4) for dc in range(2) if (dz, dx, dc) != (0, 0, 0)
    ]
    moves.sort(key=lambda m: -(min(m[0], 8 - m[0]) + min(m[1], 4 - m[1])))
    z, x, c = me // 8, (me // 2) % 4, me % 2
    return [
        lax.rem(z + dz, 8) * 8 + lax.rem(x + dx, 4) * 2 + lax.rem(c + dc, 2) for dz, dx, dc in moves
    ]


def exchange_kernel(
    tab_ref, idx_ref, ridx_ref, comb_ref, og_ref, bd_ref, sems
):
    peers, slots = og_ref.shape[0], og_ref.shape[1]
    local = tab_ref.shape[0]
    width = bd_ref.shape[1]
    regions = lax.axis_size("group")
    me = lax.axis_index("dev")
    region = lax.axis_index("group")
    up = lax.rem(region + 1, regions)
    down = lax.rem(region + regions - 1, regions)
    mesh_ids = pl.DeviceIdType.MESH
    arrived = local
    bordering = local + peers * slots

    keep = pltpu.make_async_copy(tab_ref, comb_ref.at[pl.ds(0, local)], sems.at[4])
    keep.start()

    barrier = pltpu.get_barrier_semaphore()

    targets = far_first(me, peers)
    for e in targets:
        pl.semaphore_signal(barrier, inc=1, device_id=(region, e), device_id_type=mesh_ids)
    pl.semaphore_signal(barrier, inc=1, device_id=(up, me), device_id_type=mesh_ids)
    pl.semaphore_signal(barrier, inc=1, device_id=(down, me), device_id_type=mesh_ids)

    for h in range(2):
        for p in range(width):
            source = jnp.clip(ridx_ref[h, p], 0, local - 1)
            bd_ref[h, pl.ds(p, 1), :] = tab_ref[pl.ds(source, 1), :]

    def pack(e, carry):
        for c in range(slots):
            source = jnp.clip(idx_ref[e, c], 0, local - 1)
            og_ref[e, pl.ds(c, 1), :] = tab_ref[pl.ds(source, 1), :]
        return carry

    lax.fori_loop(0, peers, pack, 0)

    pl.semaphore_wait(barrier, peers + 1)

    pltpu.make_async_remote_copy(
        src_ref=bd_ref.at[1],
        dst_ref=comb_ref.at[pl.ds(bordering, width)],
        send_sem=sems.at[2],
        recv_sem=sems.at[3],
        device_id=(up, me),
        device_id_type=mesh_ids,
    ).start()
    pltpu.make_async_remote_copy(
        src_ref=bd_ref.at[0],
        dst_ref=comb_ref.at[pl.ds(bordering + width, width)],
        send_sem=sems.at[2],
        recv_sem=sems.at[3],
        device_id=(down, me),
        device_id_type=mesh_ids,
    ).start()

    mine = pl.ds(pl.multiple_of(arrived + me * slots, slots), slots)

    for e in targets:
        pltpu.make_async_remote_copy(
            src_ref=og_ref.at[e],
            dst_ref=comb_ref.at[mine],
            send_sem=sems.at[0],
            recv_sem=sems.at[1],
            device_id=(region, e),
            device_id_type=mesh_ids,
        ).start()
    comb_ref[mine, :] = og_ref[me]

    pltpu.make_async_copy(og_ref.at[pl.ds(0, peers - 1)], og_ref.at[pl.ds(0, peers - 1)], sems.at[0]).wait()
    pltpu.make_async_copy(bd_ref, bd_ref, sems.at[2]).wait()
    pltpu.make_async_copy(og_ref.at[pl.ds(0, peers - 1)], og_ref.at[pl.ds(0, peers - 1)], sems.at[1]).wait()
    pltpu.make_async_copy(bd_ref, bd_ref, sems.at[3]).wait()
    keep.wait()


def exchange(table, peer_ids, region_ids, peers, layers):
    local, slab_rows = table.shape
    slots = peer_ids.shape[1]
    width = region_ids.shape[1]
    vmem = pl.BlockSpec(memory_space=pltpu.VMEM)
    smem = pl.BlockSpec(memory_space=pltpu.SMEM)
    return pl.pallas_call(
        exchange_kernel,
        out_shape=(pltpu.VMEM if layers == 1 else jax.ShapeDtypeStruct)(
            (local + peers * slots + 2 * width, slab_rows), table.dtype
        ),
        in_specs=[vmem, smem, smem],
        out_specs=vmem,
        scratch_shapes=[
            pltpu.VMEM((peers, slots, slab_rows), table.dtype),
            pltpu.VMEM((2, width, slab_rows), table.dtype),
            pltpu.SemaphoreType.DMA((5,)),
        ],
        compiler_params=pltpu.CompilerParams(collective_id=layers, has_side_effects=True),
    )(pltpu.with_memory_space_constraint(table, pltpu.VMEM), peer_ids, region_ids)


def paired_kernel(tab_ref, idx_ref, ridx_ref, comb_ref, og_ref, bd_ref, sems):
    peers, half, lane_count = og_ref.shape
    slots = 2 * half
    slab_rows = lane_count // 2
    local = tab_ref.shape[0]
    width = bd_ref.shape[1]
    regions = lax.axis_size("group")
    me = lax.axis_index("dev")
    region = lax.axis_index("group")
    up = lax.rem(region + 1, regions)
    down = lax.rem(region + regions - 1, regions)
    mesh_ids = pl.DeviceIdType.MESH
    bordering = local + peers * half

    keep = pltpu.make_async_copy(tab_ref, comb_ref.at[pl.ds(0, local)], sems.at[4])
    keep.start()

    barrier = pltpu.get_barrier_semaphore()
    targets = far_first(me, peers)
    for e in targets:
        pl.semaphore_signal(barrier, inc=1, device_id=(region, e), device_id_type=mesh_ids)
    pl.semaphore_signal(barrier, inc=1, device_id=(up, me), device_id_type=mesh_ids)
    pl.semaphore_signal(barrier, inc=1, device_id=(down, me), device_id_type=mesh_ids)

    for h in range(2):
        for p in range(width):
            source = jnp.clip(ridx_ref[h, p], 0, local - 1)
            bd_ref[h, pl.ds(p, 1), :] = tab_ref[pl.ds(source, 1), :]

    lanes = lax.broadcasted_iota(jnp.int32, (1, lane_count), 1)

    def pack(e, carry):
        for r in range(half):
            first = tab_ref[pl.ds(jnp.clip(idx_ref[e, r], 0, local - 1), 1), :]
            second = tab_ref[pl.ds(jnp.clip(idx_ref[e, r + half], 0, local - 1), 1), :]
            og_ref[e, pl.ds(r, 1), :] = jnp.where(lanes < slab_rows, first, second)
        return carry

    lax.fori_loop(0, peers, pack, 0)

    pl.semaphore_wait(barrier, peers + 1)

    pltpu.make_async_remote_copy(
        src_ref=bd_ref.at[1],
        dst_ref=comb_ref.at[pl.ds(bordering, width)],
        send_sem=sems.at[2],
        recv_sem=sems.at[3],
        device_id=(up, me),
        device_id_type=mesh_ids,
    ).start()
    pltpu.make_async_remote_copy(
        src_ref=bd_ref.at[0],
        dst_ref=comb_ref.at[pl.ds(bordering + width, width)],
        send_sem=sems.at[2],
        recv_sem=sems.at[3],
        device_id=(down, me),
        device_id_type=mesh_ids,
    ).start()

    mine = pl.ds(local + me * half, half)
    for e in targets:
        pltpu.make_async_remote_copy(
            src_ref=og_ref.at[e],
            dst_ref=comb_ref.at[mine],
            send_sem=sems.at[0],
            recv_sem=sems.at[1],
            device_id=(region, e),
            device_id_type=mesh_ids,
        ).start()
    pltpu.make_async_copy(og_ref.at[me], comb_ref.at[mine], sems.at[1]).start()

    pltpu.make_async_copy(og_ref.at[pl.ds(0, peers - 1)], og_ref.at[pl.ds(0, peers - 1)], sems.at[0]).wait()
    pltpu.make_async_copy(bd_ref, bd_ref, sems.at[2]).wait()
    pltpu.make_async_copy(og_ref, og_ref, sems.at[1]).wait()
    pltpu.make_async_copy(bd_ref, bd_ref, sems.at[3]).wait()
    keep.wait()


def paired_exchange(table, peer_ids, region_ids, peers):
    local, slab_rows = table.shape
    slots = peer_ids.shape[1]
    width = region_ids.shape[1]
    doubled = jnp.concatenate([table, table], axis=1)
    vmem = pl.BlockSpec(memory_space=pltpu.VMEM)
    smem = pl.BlockSpec(memory_space=pltpu.SMEM)
    return pl.pallas_call(
        paired_kernel,
        out_shape=pltpu.VMEM((local + peers * slots // 2 + 2 * width, 2 * slab_rows), table.dtype),
        in_specs=[vmem, smem, smem],
        out_specs=vmem,
        scratch_shapes=[
            pltpu.VMEM((peers, slots // 2, 2 * slab_rows), table.dtype),
            pltpu.VMEM((2, width, 2 * slab_rows), table.dtype),
            pltpu.SemaphoreType.DMA((5,)),
        ],
        compiler_params=pltpu.CompilerParams(collective_id=2, has_side_effects=True),
    )(pltpu.with_memory_space_constraint(doubled, pltpu.VMEM), peer_ids, region_ids)


def paired_sources(halo_ids, local, peers, slots, width):
    half = slots // 2
    entry = halo_ids - local
    slot = entry % slots
    from_peer = (entry >= 0) & (entry < peers * slots)
    from_region = entry >= peers * slots
    row = jnp.where(
        from_peer,
        local + (entry // slots) * half + slot % half,
        jnp.where(from_region, halo_ids - peers * half, halo_ids),
    )
    upper = from_peer & (slot >= half)
    return row, upper


def assemble(voxels, layers, peer_ids, region_ids, halo_ids, paired_ids):
    slab_table = face_slabs(voxels, layers)
    peers = lax.axis_size("dev")
    if layers == 1 and paired_ids is not None:
        rows, upper = paired_ids
        table = paired_exchange(slab_table.T, peer_ids, region_ids, peers)
        lines = table.at[rows].get(mode="promise_in_bounds")
        width = slab_table.shape[0]
        chosen = jnp.where(upper[..., None], lines[..., width:], lines[..., :width])
        return jnp.moveaxis(chosen, 2, 0)
    combined = exchange(slab_table.T, peer_ids, region_ids, peers, layers).T
    picked = combined.at[:, halo_ids].get(mode="promise_in_bounds")
    return picked


def per_device(level_set, speed, peer_slabs, region_slabs, halo_source):
    count = level_set.shape[1]
    local = 6 * count
    peer_ids = peer_slabs
    region_ids = region_slabs
    halo_ids = jnp.clip(halo_source, 0, local + peer_ids.size + region_ids.size - 1)
    peers = lax.axis_size("dev")
    slots = peer_ids.shape[1]
    paired_ids = None
    if slots % 2 == 0:
        paired_ids = paired_sources(halo_ids, local, peers, slots, region_ids.shape[1])
    voxels = level_set.reshape(8, 8, 8, count)
    speeds = speed.reshape(8, 8, 8, count)
    for offset_step in range(OFFSET_STEPS):
        picked = assemble(voxels, 3, peer_ids, region_ids, halo_ids, paired_ids)
        voxels = advect_leaves(voxels, lax.optimization_barrier(speeds), picked)
        sign_field = voxels / jnp.sqrt(voxels * voxels + 1.0)
        for redist_pass in range(REDIST_PASSES):
            picked = assemble(voxels, 1, peer_ids, region_ids, halo_ids, paired_ids)
            voxels = relax_leaves(voxels, sign_field, picked)
    return voxels.reshape(512, count)


def solution(mesh):
    return jax.shard_map(
        per_device,
        mesh=mesh,
        in_specs=(
            P(None, ("group", "dev")),
            P(None, ("group", "dev")),
            P(("group", "dev"), None),
            P(("group", "dev"), None),
            P(None, ("group", "dev")),
        ),
        out_specs=P(None, ("group", "dev")),
        check_vma=False,
    )
```
